256 devices in a mesh: strike: 64 (over z, y_hi, x), dip: 4 (over y_lo, core).
Axes of the slice: x: 4, y: 4 (y_hi: 2, y_lo: 2; y = y_hi * 2 + y_lo), z: 8, core: 2. Of those that a mesh axis runs over, the one named last changes fastest.
Arguments:
- coarse_field: bfloat16 [256, 16, 128], P('strike', 'dip'), may hold values from -6 to 6
- up_weight: bfloat16 [8, 8, 8, 32, 32], replicated, may hold values from -0.375 to 0.375
- first_weight: bfloat16 [3, 3, 3, 32, 32], replicated, may hold values from -0.21875 to 0.21875
- second_weight: bfloat16 [3, 3, 3, 32, 32], replicated, may hold values from -0.21875 to 0.21875
Outputs:
- refined: bfloat16 [1024, 64, 512], P('strike', 'dip')
The draws below stay inside these ranges and needn't reach their ends.
All inputs are finite; a program needn't handle non-finite values.
Results may differ from the reference program's by a relative error of at most 0.012.
Values may be sent and summed in bfloat16 or wider, within the bound.
A program may use at most 192 MiB of HBM per device.

```python
import jax
import jax.numpy as jnp
from jax import lax

C = 32
ZC = 4
NXC = 256
NYC = 16


def block_scale(rng, dims, shards, least, top_value):
    def one(position, shards_of):
        draws = jax.random.uniform(jax.random.fold_in(jax.random.fold_in(rng, 6), position), (shards_of,), jnp.float32, least / len(shards), top_value / len(shards))
        return jnp.repeat(jnp.exp(draws), dims[position] // shards_of).reshape((-1,) + (1,) * (len(dims) - position - 1))

    gain = one(*shards[0])
    for cut in shards[1:]:
        gain = gain * one(*cut)
    return gain


def bell_draw(own_key, dims, deviation, most, shards=(), kind=jnp.bfloat16):
    factor_of = block_scale(own_key, dims, shards, -0.22, 0.18) if shards else 1.0
    result = jax.random.normal(own_key, dims, jnp.float32) * deviation * factor_of
    return jnp.minimum(jnp.maximum(result, -most), most).astype(kind)


def setup_inputs(seed: int = 0) -> dict:
    key_of = jax.random.split(jax.random.key(seed), 5)
    coarse_field = bell_draw(key_of[0], (NXC, NYC, ZC * C), 1.0, 6.0, ((0, 64), (1, 4)))
    up_weight = bell_draw(key_of[1], (8, 8, 8, C, C), (8 * C) ** -0.5, 0.375)
    first_weight = bell_draw(key_of[2], (3, 3, 3, C, C), (27 * C) ** -0.5, 0.21875)
    second_weight = bell_draw(key_of[3], (3, 3, 3, C, C), (27 * C) ** -0.5, 0.21875)
    return {"coarse_field": coarse_field, "up_weight": up_weight, "first_weight": first_weight, "second_weight": second_weight}


HIGHEST = lax.Precision.HIGHEST


def upsample(coarse_field, up_weight):
    size_one, size_two, depth_lanes = coarse_field.shape
    channels = up_weight.shape[3]
    coarse_depth = depth_lanes // channels
    coarse_grid = coarse_field.astype(jnp.float32).reshape(size_one, size_two, coarse_depth, channels)
    padded = jnp.pad(coarse_grid, ((1, 1), (1, 1), (1, 1), (0, 0)))
    weights = up_weight.astype(jnp.float32).reshape(2, 4, 2, 4, 2, 4, channels, channels)

    def one_block(block_index):
        start = (block_index * 8).astype(jnp.int32)
        row_slab = lax.dynamic_slice_in_dim(padded, start, 10, 0)
        summed = jnp.zeros((9, size_two + 1, coarse_depth + 1, 4, 4, 4, channels), jnp.float32)
        for high_one in (0, 1):
            for high_two in (0, 1):
                for high_three in (0, 1):
                    shifted = row_slab[1 - high_one:10 - high_one, 1 - high_two:size_two + 2 - high_two,
                                       1 - high_three:coarse_depth + 2 - high_three]
                    summed = summed + jnp.einsum("abcx,pqrxy->abcpqry", shifted,
                                                 weights[high_one, :, high_two, :, high_three],
                                                 precision=HIGHEST)
        summed = summed.transpose(0, 3, 1, 4, 2, 5, 6)
        summed = summed.reshape(36, 4 * size_two + 4, 4 * coarse_depth + 4, channels)
        return summed[2:34, 2:4 * size_two + 2, 2:4 * coarse_depth + 2]

    blocks = lax.map(one_block, jnp.arange(size_one // 8, dtype=jnp.int32))
    return blocks.reshape(4 * size_one, 4 * size_two, 4 * coarse_depth, channels)


def refine(field_in, weight):
    output = lax.conv_general_dilated(field_in.astype(jnp.float32)[None], weight.astype(jnp.float32),
                                      (1, 1, 1), "SAME", dimension_numbers=("NDHWC", "DHWIO", "NDHWC"),
                                      precision=HIGHEST)
    return output[0]


def reference(coarse_field, up_weight, first_weight, second_weight):
    upsampled = upsample(coarse_field, up_weight)
    base = jax.nn.silu(upsampled).astype(jnp.bfloat16)
    hidden = jax.nn.silu(refine(base, first_weight)).astype(jnp.bfloat16)
    refined = (base.astype(jnp.float32) + refine(hidden, second_weight)).astype(jnp.bfloat16)
    return refined.reshape(refined.shape[0], refined.shape[1], refined.shape[2] * refined.shape[3])
```

```python
import jax
import jax.numpy as jnp
import numpy as np
from jax import lax
from jax.sharding import PartitionSpec as P

HIGHEST = lax.Precision.HIGHEST


def passed_along(block, axis, distance):
    devices = range(lax.axis_size(axis))
    route = [(i - distance, i) for i in devices if i - distance in devices]
    return lax.ppermute(block, axis, route)


def extended_2(cells, sides, width):
    for axis, dim in sides:
        count = lax.axis_size(axis)
        ends = count - 1
        head = lax.slice_in_dim(cells, 0, width, axis=dim)
        tail = lax.slice_in_dim(cells, cells.shape[dim] - width, cells.shape[dim], axis=dim)
        cells = jnp.concatenate(
            [
                lax.ppermute(tail, axis, [(i, (i + 1) % count) for i in range(ends)]),
                cells,
                lax.ppermute(head, axis, [((i + 1) % count, i) for i in range(ends)]),
            ],
            axis=dim,
        )
    return cells


def up_tables(up_weight, coarse_depth):
    channels = up_weight.shape[3]
    fine_depth = 4 * coarse_depth
    zero = jnp.zeros((), up_weight.dtype)
    taps = up_weight.reshape(2, 4, 2, 4, 8, channels, channels).transpose(0, 2, 5, 1, 3, 4, 6)
    keep = [(0, 0, 0)] * 5
    placed = jnp.stack(
        [
            lax.pad(taps, zero, keep + [(4 * c - 2, fine_depth - 4 * c - 6, 0), (0, 0, 0)])
            for c in range(coarse_depth)
        ],
        axis=2,
    )
    return placed.reshape(2, 2, coarse_depth * channels, 16 * fine_depth * channels)


def band_tables(weight):
    channels = weight.shape[3]
    zero = jnp.zeros((), weight.dtype)
    keep = [(0, 0, 0)] * 2
    natural = jnp.stack(
        [lax.pad(weight, zero, keep + [(o, 3 - o, 0), (0, 0, 0), (0, 0, 0)]) for o in range(4)],
        axis=4,
    )
    band_mats = jnp.concatenate([natural[:, :, 1:5], natural[:, :, 0:1], natural[:, :, 5:6]], axis=2)
    return band_mats.reshape(3, 3, 6 * channels, 4 * channels)


def spread(coarse_block, up_mats):
    size_one, size_two, depth_lanes = coarse_block.shape
    lane_width = up_mats.shape[3] // 16
    flat_rows = coarse_block.reshape(size_one * size_two, depth_lanes)
    summed = jnp.zeros((size_one + 1, size_two + 1, 4, 4, lane_width), jnp.float32)
    for high_one in (0, 1):
        for high_two in (0, 1):
            product = jnp.dot(
                flat_rows, up_mats[high_one, high_two], preferred_element_type=jnp.float32
            )
            product = product.reshape(size_one, size_two, 4, 4, lane_width)
            summed = summed + jnp.pad(
                product,
                ((high_one, 1 - high_one), (high_two, 1 - high_two), (0, 0), (0, 0), (0, 0)),
            )
    summed = summed.transpose(0, 2, 1, 3, 4)
    return summed.reshape(4 * size_one + 4, 4 * size_two + 4, lane_width)


def refine(padded, band_mats, rows_out, cols_out):
    size_one, size_two, depth_lanes = padded.shape
    quad_lanes = band_mats.shape[3]
    channels = quad_lanes // 4
    groups = depth_lanes // quad_lanes
    blocks = padded.reshape(size_one, size_two, groups, quad_lanes)
    before_cell = jnp.pad(blocks[:, :, :-1, 3 * channels :], ((0, 0), (0, 0), (1, 0), (0, 0)))
    after_cell = jnp.pad(blocks[:, :, 1:, :channels], ((0, 0), (0, 0), (0, 1), (0, 0)))
    widened = jnp.concatenate([blocks, before_cell, after_cell], axis=3)
    summed = jnp.zeros((rows_out * cols_out * groups, quad_lanes), jnp.float32)
    for shift_one in range(3):
        for shift_two in range(3):
            window = widened[shift_one : shift_one + rows_out, shift_two : shift_two + cols_out]
            summed = summed + jnp.dot(
                window.reshape(-1, 6 * channels),
                band_mats[shift_one, shift_two],
                preferred_element_type=jnp.float32,
            )
    return summed.reshape(rows_out, cols_out, depth_lanes)


def strike_move(edge_rows, step):
    return passed_along(edge_rows, "strike", step)


def dip_move(edge_cols, step):
    return passed_along(edge_cols.astype(jnp.bfloat16), "dip", step).astype(edge_cols.dtype)


def conv_step(field_in, band_mats):
    padded = extended_2(field_in, (("strike", 0), ("dip", 1)), 1)
    return refine(padded, band_mats, field_in.shape[0], field_in.shape[1])


def body(coarse_field, up_weight, first_weight, second_weight):
    channels = up_weight.shape[3]
    coarse_depth = coarse_field.shape[2] // channels
    up_mats = up_tables(up_weight, coarse_depth)
    own_rows = 4 * coarse_field.shape[0]
    own_cols = 4 * coarse_field.shape[1]
    first_mats = band_tables(first_weight)
    second_mats = band_tables(second_weight)
    extended = spread(coarse_field, up_mats)
    from_below = strike_move(extended[own_rows + 2 :], 1)
    from_above = strike_move(extended[:2], -1)
    strip = extended[2 : own_rows + 2].at[:2].add(from_below).at[own_rows - 2 :].add(from_above)
    from_left = dip_move(strip[:, own_cols + 2 :], 1)
    from_right = dip_move(strip[:, :2], -1)
    summed = (
        strip[:, 2 : own_cols + 2].at[:, :2].add(from_left).at[:, own_cols - 2 :].add(from_right)
    )
    base = jax.nn.silu(summed).astype(jnp.bfloat16)
    hidden = jax.nn.silu(conv_step(base, first_mats)).astype(jnp.bfloat16)
    second_out = conv_step(hidden, second_mats)
    return (base.astype(jnp.float32) + second_out).astype(jnp.bfloat16)


def solution(mesh):
    return jax.shard_map(
        body,
        mesh=mesh,
        in_specs=(P("strike", "dip", None), P(), P(), P()),
        out_specs=P("strike", "dip", None),
        check_vma=False,
    )
```

```python
import jax
import jax.numpy as jnp
import numpy as np
from jax import lax
from jax.sharding import PartitionSpec as P

HIGHEST = lax.Precision.HIGHEST


def passed_along(block, axis, distance):
    devices = range(lax.axis_size(axis))
    route = [(i - distance, i) for i in devices if i - distance in devices]
    return lax.ppermute(block, axis, route)


def extended_2(cells, sides, width):
    for axis, dim in sides:
        count = lax.axis_size(axis)
        ends = count - 1
        head = lax.slice_in_dim(cells, 0, width, axis=dim)
        tail = lax.slice_in_dim(cells, cells.shape[dim] - width, cells.shape[dim], axis=dim)
        cells = jnp.concatenate(
            [
                lax.ppermute(tail, axis, [(i, (i + 1) % count) for i in range(ends)]),
                cells,
                lax.ppermute(head, axis, [((i + 1) % count, i) for i in range(ends)]),
            ],
            axis=dim,
        )
    return cells


def up_tables(up_weight, coarse_depth):
    channels = up_weight.shape[3]
    fine_depth = 4 * coarse_depth
    zero = jnp.zeros((), up_weight.dtype)
    taps = up_weight.reshape(2, 4, 2, 4, 8, channels, channels).transpose(0, 2, 1, 3, 5, 4, 6)
    taps = taps.reshape(2, 2, 4, 4, channels, 8 * channels)
    keep = [(0, 0, 0)] * 5
    return jnp.concatenate(
        [
            lax.pad(
                taps,
                zero,
                keep + [(channels * (4 * c - 2), channels * (fine_depth - 4 * c - 6), 0)],
            )
            for c in range(coarse_depth)
        ],
        axis=4,
    )


def band_tables(weight):
    channels = weight.shape[3]
    zero = jnp.zeros((), weight.dtype)
    keep = [(0, 0, 0)] * 2
    natural = jnp.stack(
        [lax.pad(weight, zero, keep + [(o, 3 - o, 0), (0, 0, 0), (0, 0, 0)]) for o in range(4)],
        axis=4,
    )
    band_mats = jnp.concatenate([natural[:, :, 1:5], natural[:, :, 0:1], natural[:, :, 5:6]], axis=2)
    return band_mats.reshape(3, 3, 6 * channels, 4 * channels)


def spread(coarse_block, up_mats):
    size_one, size_two, depth_lanes = coarse_block.shape
    lane_width = up_mats.shape[5]
    flat_rows = coarse_block.reshape(size_one * size_two, depth_lanes)
    stacked = up_mats.reshape(64, depth_lanes, lane_width)
    product = jnp.einsum(
        "bpk,bkn->bpn",
        jnp.broadcast_to(flat_rows, (64,) + flat_rows.shape),
        stacked,
        preferred_element_type=jnp.float32,
    )
    product = product.reshape(2, 2, 4, 4, size_one, size_two, lane_width)
    summed = jnp.zeros((4, 4, size_one + 1, size_two + 1, lane_width), jnp.float32)
    for high_one in (0, 1):
        for high_two in (0, 1):
            summed = summed + jnp.pad(
                product[high_one, high_two],
                ((0, 0), (0, 0), (high_one, 1 - high_one), (high_two, 1 - high_two), (0, 0)),
            )
    summed = summed.transpose(2, 0, 3, 1, 4)
    return summed.reshape(4 * size_one + 4, 4 * size_two + 4, lane_width)


def refine(padded, band_mats, rows_out, cols_out):
    size_one, size_two, depth_lanes = padded.shape
    quad_lanes = band_mats.shape[3]
    channels = quad_lanes // 4
    groups = depth_lanes // quad_lanes
    blocks = padded.reshape(size_one, size_two, groups, quad_lanes)
    before_cell = jnp.pad(blocks[:, :, :-1, 3 * channels :], ((0, 0), (0, 0), (1, 0), (0, 0)))
    after_cell = jnp.pad(blocks[:, :, 1:, :channels], ((0, 0), (0, 0), (0, 1), (0, 0)))
    widened = jnp.concatenate([blocks, before_cell, after_cell], axis=3)
    summed = jnp.zeros((rows_out * cols_out * groups, quad_lanes), jnp.float32)
    for shift_one in range(3):
        for shift_two in range(3):
            window = widened[shift_one : shift_one + rows_out, shift_two : shift_two + cols_out]
            summed = summed + jnp.dot(
                window.reshape(-1, 6 * channels),
                band_mats[shift_one, shift_two],
                preferred_element_type=jnp.float32,
            )
    return summed.reshape(rows_out, cols_out, depth_lanes)


def strike_move(edge_rows, step):
    return passed_along(edge_rows, "strike", step)


def dip_move(edge_cols, step):
    return passed_along(edge_cols.astype(jnp.bfloat16), "dip", step).astype(edge_cols.dtype)


def conv_step(field_in, band_mats):
    padded = extended_2(field_in, (("strike", 0), ("dip", 1)), 1)
    return refine(padded, band_mats, field_in.shape[0], field_in.shape[1])


def body(coarse_field, up_weight, first_weight, second_weight):
    channels = up_weight.shape[3]
    coarse_depth = coarse_field.shape[2] // channels
    up_mats = up_tables(up_weight, coarse_depth)
    own_rows = 4 * coarse_field.shape[0]
    own_cols = 4 * coarse_field.shape[1]
    first_mats = band_tables(first_weight)
    second_mats = band_tables(second_weight)
    extended = spread(coarse_field, up_mats)
    from_below = strike_move(extended[own_rows + 2 :], 1)
    from_above = strike_move(extended[:2], -1)
    strip = extended[2 : own_rows + 2].at[:2].add(from_below).at[own_rows - 2 :].add(from_above)
    from_left = dip_move(strip[:, own_cols + 2 :], 1)
    from_right = dip_move(strip[:, :2], -1)
    summed = (
        strip[:, 2 : own_cols + 2].at[:, :2].add(from_left).at[:, own_cols - 2 :].add(from_right)
    )
    base = jax.nn.silu(summed).astype(jnp.bfloat16)
    hidden = jax.nn.silu(conv_step(base, first_mats)).astype(jnp.bfloat16)
    second_out = conv_step(hidden, second_mats)
    return (base.astype(jnp.float32) + second_out).astype(jnp.bfloat16)


def solution(mesh):
    return jax.shard_map(
        body,
        mesh=mesh,
        in_specs=(P("strike", "dip", None), P(), P(), P()),
        out_specs=P("strike", "dip", None),
        check_vma=False,
    )
```

```python
import jax
import jax.numpy as jnp
import numpy as np
from jax import lax
from jax.sharding import PartitionSpec as P

HIGHEST = lax.Precision.HIGHEST


def extended_2(cells, sides, width):
    for axis, dim in sides:
        count = lax.axis_size(axis)
        ends = count - 1
        head = lax.slice_in_dim(cells, 0, width, axis=dim)
        tail = lax.slice_in_dim(cells, cells.shape[dim] - width, cells.shape[dim], axis=dim)
        cells = jnp.concatenate(
            [
                lax.ppermute(tail, axis, [(i, (i + 1) % count) for i in range(ends)]),
                cells,
                lax.ppermute(head, axis, [((i + 1) % count, i) for i in range(ends)]),
            ],
            axis=dim,
        )
    return cells


def up_tables(up_weight, coarse_depth):
    channels = up_weight.shape[3]
    fine_depth = 4 * coarse_depth
    zero = jnp.zeros((), up_weight.dtype)
    taps = up_weight.reshape(2, 4, 2, 4, 8, channels, channels).transpose(0, 2, 1, 3, 5, 4, 6)
    taps = taps.reshape(2, 2, 4, 4, channels, 8 * channels)
    keep = [(0, 0, 0)] * 5
    return jnp.concatenate(
        [
            lax.pad(
                taps,
                zero,
                keep + [(channels * (4 * c - 2), channels * (fine_depth - 4 * c - 6), 0)],
            )
            for c in range(coarse_depth)
        ],
        axis=4,
    )


def band_tables(weight):
    channels = weight.shape[3]
    zero = jnp.zeros((), weight.dtype)
    keep = [(0, 0, 0)] * 2
    natural = jnp.stack(
        [lax.pad(weight, zero, keep + [(o, 3 - o, 0), (0, 0, 0), (0, 0, 0)]) for o in range(4)],
        axis=4,
    )
    band_mats = jnp.concatenate([natural[:, :, 1:5], natural[:, :, 0:1], natural[:, :, 5:6]], axis=2)
    return band_mats.reshape(3, 3, 6 * channels, 4 * channels)


def spread(coarse_block, up_mats):
    size_one, size_two, depth_lanes = coarse_block.shape
    lane_width = up_mats.shape[5]
    flat_rows = coarse_block.reshape(size_one * size_two, depth_lanes)
    stacked = up_mats.reshape(64, depth_lanes, lane_width)
    product = jnp.einsum(
        "bpk,bkn->bpn",
        jnp.broadcast_to(flat_rows, (64,) + flat_rows.shape),
        stacked,
        preferred_element_type=jnp.float32,
    )
    product = product.reshape(2, 2, 4, 4, size_one, size_two, lane_width)
    summed = jnp.zeros((4, 4, size_one + 1, size_two + 1, lane_width), jnp.float32)
    for high_one in (0, 1):
        for high_two in (0, 1):
            summed = summed + jnp.pad(
                product[high_one, high_two],
                ((0, 0), (0, 0), (high_one, 1 - high_one), (high_two, 1 - high_two), (0, 0)),
            )
    summed = summed.transpose(2, 0, 3, 1, 4)
    return summed.reshape(4 * size_one + 4, 4 * size_two + 4, lane_width)


def refine(padded, band_mats, rows_out, cols_out):
    size_one, size_two, depth_lanes = padded.shape
    quad_lanes = band_mats.shape[3]
    channels = quad_lanes // 4
    groups = depth_lanes // quad_lanes
    blocks = padded.reshape(size_one, size_two, groups, quad_lanes)
    before_cell = jnp.pad(blocks[:, :, :-1, 3 * channels :], ((0, 0), (0, 0), (1, 0), (0, 0)))
    after_cell = jnp.pad(blocks[:, :, 1:, :channels], ((0, 0), (0, 0), (0, 1), (0, 0)))
    widened = jnp.concatenate([blocks, before_cell, after_cell], axis=3)
    summed = jnp.zeros((rows_out * cols_out * groups, quad_lanes), jnp.float32)
    for shift_one in range(3):
        for shift_two in range(3):
            window = widened[shift_one : shift_one + rows_out, shift_two : shift_two + cols_out]
            summed = summed + jnp.dot(
                window.reshape(-1, 6 * channels),
                band_mats[shift_one, shift_two],
                preferred_element_type=jnp.float32,
            )
    return summed.reshape(rows_out, cols_out, depth_lanes)


def inside(axis, count, own, halo):
    place = lax.axis_index(axis)
    local = jnp.arange(count) - halo
    return ((local >= 0) | (place > 0)) & ((local < own) | (place < lax.axis_size(axis) - 1))


def masked_silu(values, own_rows, own_cols, halo):
    rows = inside("strike", values.shape[0], own_rows, halo)
    cols = inside("dip", values.shape[1], own_cols, halo)
    keep = rows[:, None, None] & cols[None, :, None]
    return jnp.where(keep, jax.nn.silu(values), 0.0).astype(jnp.bfloat16)


def body(coarse_field, up_weight, first_weight, second_weight):
    channels = up_weight.shape[3]
    coarse_depth = coarse_field.shape[2] // channels
    up_mats = up_tables(up_weight, coarse_depth)
    own_rows = 4 * coarse_field.shape[0]
    own_cols = 4 * coarse_field.shape[1]
    first_mats = band_tables(first_weight)
    second_mats = band_tables(second_weight)
    coarse_ext = extended_2(coarse_field, (("strike", 0), ("dip", 1)), 1)
    extended = spread(coarse_ext, up_mats)[4 : own_rows + 8, 4 : own_cols + 8]
    base = masked_silu(extended, own_rows, own_cols, 2)
    hidden = masked_silu(refine(base, first_mats, own_rows + 2, own_cols + 2), own_rows, own_cols, 1)
    second_out = refine(hidden, second_mats, own_rows, own_cols)
    own_base = base[2 : own_rows + 2, 2 : own_cols + 2]
    return (own_base.astype(jnp.float32) + second_out).astype(jnp.bfloat16)


def solution(mesh):
    return jax.shard_map(
        body,
        mesh=mesh,
        in_specs=(P("strike", "dip", None), P(), P(), P()),
        out_specs=P("strike", "dip", None),
        check_vma=False,
    )
```

```python
import jax
import jax.numpy as jnp
import numpy as np
from jax import lax
from jax.experimental import pallas as pl
from jax.experimental.pallas import tpu as pltpu
from jax.sharding import PartitionSpec as P

HIGHEST = lax.Precision.HIGHEST


def extended_2(cells, sides, width):
    for axis, dim in sides:
        count = lax.axis_size(axis)
        ends = count - 1
        head = lax.slice_in_dim(cells, 0, width, axis=dim)
        tail = lax.slice_in_dim(cells, cells.shape[dim] - width, cells.shape[dim], axis=dim)
        cells = jnp.concatenate(
            [
                lax.ppermute(tail, axis, [(i, (i + 1) % count) for i in range(ends)]),
                cells,
                lax.ppermute(head, axis, [((i + 1) % count, i) for i in range(ends)]),
            ],
            axis=dim,
        )
    return cells


def up_tables(up_weight, coarse_depth):
    channels = up_weight.shape[3]
    fine_depth = 4 * coarse_depth
    zero = jnp.zeros((), up_weight.dtype)
    taps = up_weight.reshape(2, 4, 2, 4, 8, channels, channels).transpose(0, 2, 1, 3, 5, 4, 6)
    taps = taps.reshape(2, 2, 4, 4, channels, 8 * channels)
    keep = [(0, 0, 0)] * 5
    return jnp.concatenate(
        [
            lax.pad(
                taps,
                zero,
                keep + [(channels * (4 * c - 2), channels * (fine_depth - 4 * c - 6), 0)],
            )
            for c in range(coarse_depth)
        ],
        axis=4,
    )


def spread(coarse_block, up_mats):
    size_one, size_two, depth_lanes = coarse_block.shape
    lane_width = up_mats.shape[5]
    flat_rows = coarse_block.reshape(size_one * size_two, depth_lanes)
    stacked = up_mats.reshape(64, depth_lanes, lane_width)
    product = jnp.einsum(
        "bpk,bkn->bpn",
        jnp.broadcast_to(flat_rows, (64,) + flat_rows.shape),
        stacked,
        preferred_element_type=jnp.float32,
    )
    product = product.reshape(2, 2, 4, 4, size_one, size_two, lane_width)
    summed = jnp.zeros((4, 4, size_one + 1, size_two + 1, lane_width), jnp.float32)
    for high_one in (0, 1):
        for high_two in (0, 1):
            summed = summed + jnp.pad(
                product[high_one, high_two],
                ((0, 0), (0, 0), (high_one, 1 - high_one), (high_two, 1 - high_two), (0, 0)),
            )
    summed = summed.transpose(2, 0, 3, 1, 4)
    return summed.reshape(4 * size_one + 4, 4 * size_two + 4, lane_width)


def full_band(weight):
    channels = weight.shape[3]
    depth = 16
    zero = jnp.zeros((), weight.dtype)
    taps = weight[:, :, ::-1].transpose(0, 1, 3, 2, 4).reshape(3, 3, channels, 3 * channels)
    keep = [(0, 0, 0)] * 3
    band = jnp.concatenate(
        [
            lax.pad(taps, zero, keep + [(channels * (c - 1), channels * (depth - c - 2), 0)])
            for c in range(depth)
        ],
        axis=2,
    )
    return band.reshape(9, depth * channels, depth * channels)


def inside(axis, count, own, halo):
    place = lax.axis_index(axis)
    local = jnp.arange(count) - halo
    return ((local >= 0) | (place > 0)) & ((local < own) | (place < lax.axis_size(axis) - 1))


def masked_silu(values, own_rows, own_cols, halo):
    rows = inside("strike", values.shape[0], own_rows, halo)
    cols = inside("dip", values.shape[1], own_cols, halo)
    keep = rows[:, None, None] & cols[None, :, None]
    return jnp.where(keep, jax.nn.silu(values), 0.0).astype(jnp.bfloat16)


def shifted(values, width):
    rows = values.shape[0]
    return (
        pltpu.roll(values, 1, 0).astype(jnp.bfloat16),
        values.astype(jnp.bfloat16),
        pltpu.roll(values, rows - 1, 0).astype(jnp.bfloat16),
    )


def conv_rows(parts, band_ref, width, count):
    total = None
    for one in range(3):
        for two in range(3):
            window = parts[two][one * width : one * width + count]
            term = jnp.dot(window, band_ref[one * 3 + two], preferred_element_type=jnp.float32)
            total = term if total is None else total + term
    return total


def convs_kernel(width, rows_out, cols_out, base_ref, keep_ref, first_ref, second_ref, out_ref):
    base = base_ref[...].astype(jnp.float32)
    hidden_count = (rows_out + 2) * width
    first = conv_rows(shifted(base, width), first_ref, width, hidden_count)
    hidden = jnp.where(keep_ref[...] > 0, first / (1.0 + jnp.exp(-first)), 0.0)
    out_count = rows_out * width
    second = conv_rows(shifted(hidden, width), second_ref, width, out_count)
    summed = base[2 * width : 2 * width + out_count] + second
    summed = pltpu.roll(summed, out_count - 2, 0).reshape(rows_out, width, summed.shape[1])
    out_ref[...] = summed[:, :cols_out].astype(out_ref.dtype)


def body(coarse_field, up_weight, first_weight, second_weight):
    channels = up_weight.shape[3]
    coarse_depth = coarse_field.shape[2] // channels
    up_mats = up_tables(up_weight, coarse_depth)
    own_rows = 4 * coarse_field.shape[0]
    own_cols = 4 * coarse_field.shape[1]
    lanes = 4 * coarse_depth * channels
    width = 32
    coarse_ext = extended_2(coarse_field, (("strike", 0), ("dip", 1)), 1)
    extended = spread(coarse_ext, up_mats)[4 : own_rows + 8, 4 : own_cols + 8]
    base = masked_silu(extended, own_rows, own_cols, 2)
    base = jnp.pad(base, ((0, 0), (0, width - own_cols - 4), (0, 0))).reshape(-1, lanes)
    rows_keep = inside("strike", own_rows + 4, own_rows, 2)[1 : own_rows + 3]
    cols_keep = inside("dip", own_cols + 4, own_cols, 2) & (jnp.arange(own_cols + 4) >= 1)
    cols_keep = jnp.pad(cols_keep & (jnp.arange(own_cols + 4) < own_cols + 3), (0, width - own_cols - 4))
    keep = (rows_keep[:, None] & cols_keep[None, :]).astype(jnp.float32).reshape(-1, 1)
    vmem = pl.BlockSpec(memory_space=pltpu.VMEM)
    return pl.pallas_call(
        lambda *refs: convs_kernel(width, own_rows, own_cols, *refs),
        out_shape=jax.ShapeDtypeStruct((own_rows, own_cols, lanes), jnp.bfloat16),
        in_specs=[vmem] * 4,
        out_specs=vmem,
    )(base, keep, full_band(first_weight), full_band(second_weight))


def solution(mesh):
    return jax.shard_map(
        body,
        mesh=mesh,
        in_specs=(P("strike", "dip", None), P(), P(), P()),
        out_specs=P("strike", "dip", None),
        check_vma=False,
    )
```

```python
import jax
import jax.numpy as jnp
import numpy as np
from jax import lax
from jax.experimental import pallas as pl
from jax.experimental.pallas import tpu as pltpu
from jax.sharding import PartitionSpec as P

HIGHEST = lax.Precision.HIGHEST


def extended_2(cells, sides, width):
    for axis, dim in sides:
        count = lax.axis_size(axis)
        ends = count - 1
        head = lax.slice_in_dim(cells, 0, width, axis=dim)
        tail = lax.slice_in_dim(cells, cells.shape[dim] - width, cells.shape[dim], axis=dim)
        cells = jnp.concatenate(
            [
                lax.ppermute(tail, axis, [(i, (i + 1) % count) for i in range(ends)]),
                cells,
                lax.ppermute(head, axis, [((i + 1) % count, i) for i in range(ends)]),
            ],
            axis=dim,
        )
    return cells


def up_tables(up_weight, coarse_depth):
    channels = up_weight.shape[3]
    fine_depth = 4 * coarse_depth
    zero = jnp.zeros((), up_weight.dtype)
    taps = up_weight.reshape(2, 4, 2, 4, 8, channels, channels).transpose(0, 2, 1, 3, 5, 4, 6)
    taps = taps.reshape(2, 2, 4, 4, channels, 8 * channels)
    keep = [(0, 0, 0)] * 5
    return jnp.concatenate(
        [
            lax.pad(
                taps,
                zero,
                keep + [(channels * (4 * c - 2), channels * (fine_depth - 4 * c - 6), 0)],
            )
            for c in range(coarse_depth)
        ],
        axis=4,
    )


def quad_band(weight):
    channels = weight.shape[3]
    zero = jnp.zeros((), weight.dtype)
    taps = weight.reshape(9, 3, channels, channels)
    keep = [(0, 0, 0)] * 2
    quads = jnp.stack(
        [lax.pad(taps, zero, [(0, 0, 0), (3 + o, 6 - o, 0)] + keep) for o in range(4)], axis=3
    )
    return quads.reshape(9, 12 * channels, 4 * channels)


def inside(axis, count, own, halo):
    place = lax.axis_index(axis)
    local = jnp.arange(count) - halo
    return ((local >= 0) | (place > 0)) & ((local < own) | (place < lax.axis_size(axis) - 1))


def fill_band(quad_ref, band_ref):
    rows = band_ref.shape[1]
    for tap in range(9):
        for group in range(rows // 128):
            low = 128 * (group - 1)
            top, bottom = max(low, 0), min(low + 384, rows)
            cols = pl.ds(128 * group, 128)
            band_ref[tap, top:bottom, cols] = quad_ref[tap, top - low : bottom - low, :]
            if top > 0:
                band_ref[tap, 0:top, cols] = jnp.zeros((top, 128), band_ref.dtype)
            if bottom < rows:
                band_ref[tap, bottom:rows, cols] = jnp.zeros((rows - bottom, 128), band_ref.dtype)


def shifted(values):
    rows = values.shape[0]
    return (
        pltpu.roll(values, 1, 0).astype(jnp.bfloat16),
        values.astype(jnp.bfloat16),
        pltpu.roll(values, rows - 1, 0).astype(jnp.bfloat16),
    )


def conv_rows(parts, band_ref, width, count):
    total = None
    for one in range(3):
        for two in range(3):
            window = parts[two][one * width : one * width + count]
            term = jnp.dot(window, band_ref[one * 3 + two], preferred_element_type=jnp.float32)
            total = term if total is None else total + term
    return total


def silu(values):
    return values / (1.0 + jnp.exp(-values))


def block_kernel(
    width, rows_out, cols_out,
    shifts_ref, up_ref, pick_ref, base_keep_ref, hidden_keep_ref, first_ref, second_ref,
    out_ref, band_ref,
):
    phases = []
    for phase in range(up_ref.shape[1]):
        total = None
        for high in range(up_ref.shape[0]):
            term = jnp.dot(shifts_ref[high], up_ref[high, phase], preferred_element_type=jnp.float32)
            total = term if total is None else total + term
        phases.append(total)
    phase_rows = silu(jnp.concatenate(phases, axis=0)).astype(jnp.bfloat16)
    base = jnp.dot(pick_ref[...], phase_rows, preferred_element_type=jnp.float32)
    base = jnp.where(base_keep_ref[...] > 0, base, 0.0)
    fill_band(first_ref, band_ref)
    hidden_count = (rows_out + 2) * width
    first = conv_rows(shifted(base), band_ref, width, hidden_count)
    hidden = jnp.where(hidden_keep_ref[...] > 0, silu(first), 0.0)
    fill_band(second_ref, band_ref)
    out_count = rows_out * width
    second = conv_rows(shifted(hidden), band_ref, width, out_count)
    summed = base[2 * width : 2 * width + out_count] + second
    summed = pltpu.roll(summed, out_count - 2, 0).reshape(rows_out, width, summed.shape[1])
    out_ref[...] = summed[:, :cols_out].astype(out_ref.dtype)


def picker(rows, cols, width, span):
    place = jnp.arange(rows * width)
    one, two = place // width, place % width
    source = ((one % 4) * 4 + two % 4) * (rows // 4) * span + (one // 4) * span + two // 4
    chosen = (jnp.arange(rows * width)[None, :] == source[:, None]) & (two < cols)[:, None]
    return chosen.astype(jnp.bfloat16)


def body(coarse_field, up_weight, first_weight, second_weight):
    channels = up_weight.shape[3]
    coarse_depth = coarse_field.shape[2] // channels
    size_one, size_two = coarse_field.shape[:2]
    own_rows, own_cols = 4 * size_one, 4 * size_two
    lanes = 4 * coarse_depth * channels
    width, span = 32, 8
    up_mats = up_tables(up_weight, coarse_depth).reshape(4, 16, coarse_depth * channels, lanes)
    coarse_ext = extended_2(coarse_field, (("strike", 0), ("dip", 1)), 1)
    shifts = jnp.stack(
        [
            jnp.pad(
                coarse_ext[1 - one : size_one + 2 - one, 1 - two : size_two + 2 - two],
                ((0, 0), (0, span - size_two - 1), (0, 0)),
            )
            for one in (0, 1)
            for two in (0, 1)
        ]
    ).reshape(4, (size_one + 1) * span, -1)
    rows_all = inside("strike", own_rows + 4, own_rows, 2)
    cols_all = inside("dip", own_cols + 4, own_cols, 2)
    cols_all = jnp.pad(cols_all, (0, width - own_cols - 4))
    base_keep = (rows_all[:, None] & cols_all[None, :]).astype(jnp.float32).reshape(-1, 1)
    position = jnp.arange(width)
    cols_hidden = cols_all & (position >= 1) & (position < own_cols + 3)
    hidden_keep = rows_all[1 : own_rows + 3, None] & cols_hidden[None, :]
    hidden_keep = hidden_keep.astype(jnp.float32).reshape(-1, 1)
    vmem = pl.BlockSpec(memory_space=pltpu.VMEM)
    return pl.pallas_call(
        lambda *refs: block_kernel(width, own_rows, own_cols, *refs),
        out_shape=jax.ShapeDtypeStruct((own_rows, own_cols, lanes), jnp.bfloat16),
        in_specs=[vmem] * 7,
        out_specs=vmem,
        scratch_shapes=[pltpu.VMEM((9, lanes, lanes), jnp.bfloat16)],
    )(
        shifts,
        up_mats,
        picker(own_rows + 4, own_cols + 4, width, span),
        base_keep,
        hidden_keep,
        quad_band(first_weight),
        quad_band(second_weight),
    )


def solution(mesh):
    return jax.shard_map(
        body,
        mesh=mesh,
        in_specs=(P("strike", "dip", None), P(), P(), P()),
        out_specs=P("strike", "dip", None),
        check_vma=False,
    )
```

```python
import jax
import jax.numpy as jnp
import numpy as np
from jax import lax
from jax.experimental import pallas as pl
from jax.experimental.pallas import tpu as pltpu
from jax.sharding import PartitionSpec as P

HIGHEST = lax.Precision.HIGHEST


def extended_2(cells, sides, width):
    for axis, dim in sides:
        count = lax.axis_size(axis)
        ends = count - 1
        head = lax.slice_in_dim(cells, 0, width, axis=dim)
        tail = lax.slice_in_dim(cells, cells.shape[dim] - width, cells.shape[dim], axis=dim)
        cells = jnp.concatenate(
            [
                lax.ppermute(tail, axis, [(i, (i + 1) % count) for i in range(ends)]),
                cells,
                lax.ppermute(head, axis, [((i + 1) % count, i) for i in range(ends)]),
            ],
            axis=dim,
        )
    return cells


def up_tables(up_weight, coarse_depth):
    channels = up_weight.shape[3]
    fine_depth = 4 * coarse_depth
    zero = jnp.zeros((), up_weight.dtype)
    taps = up_weight.reshape(2, 4, 2, 4, 8, channels, channels).transpose(0, 2, 1, 3, 5, 4, 6)
    taps = taps.reshape(2, 2, 4, 4, channels, 8 * channels)
    keep = [(0, 0, 0)] * 5
    return jnp.concatenate(
        [
            lax.pad(
                taps,
                zero,
                keep + [(channels * (4 * c - 2), channels * (fine_depth - 4 * c - 6), 0)],
            )
            for c in range(coarse_depth)
        ],
        axis=4,
    )


def inside(axis, count, own, halo):
    place = lax.axis_index(axis)
    local = jnp.arange(count) - halo
    return ((local >= 0) | (place > 0)) & ((local < own) | (place < lax.axis_size(axis) - 1))


def fill_band(weight_ref, band_ref):
    channels = weight_ref.shape[1]
    taps = weight_ref.shape[0] // (3 * channels)
    cells = band_ref.shape[1] // channels
    lane = lax.broadcasted_iota(jnp.int32, (channels, 128), 1)
    spread_out = (lane % channels == lax.broadcasted_iota(jnp.int32, (channels, 128), 0))
    tiled = jnp.dot(weight_ref[...], spread_out.astype(weight_ref.dtype), preferred_element_type=jnp.float32)
    quarter = lane // channels
    per_group = 128 // channels
    for tap in range(taps):
        for group in range(cells // per_group):
            for cell in range(max(0, per_group * group - 1), min(cells, per_group * group + per_group + 1)):
                block = jnp.zeros((channels, 128), jnp.float32)
                for out_cell in range(per_group):
                    depth = cell - per_group * group - out_cell + 1
                    if 0 <= depth <= 2:
                        row = (tap * 3 + depth) * channels
                        block = jnp.where(quarter == out_cell, tiled[row : row + channels], block)
                band_ref[tap, pl.ds(cell * channels, channels), pl.ds(128 * group, 128)] = block.astype(
                    band_ref.dtype
                )


def shifted(values):
    rows = values.shape[0]
    return (
        pltpu.roll(values, 1, 0).astype(jnp.bfloat16),
        values.astype(jnp.bfloat16),
        pltpu.roll(values, rows - 1, 0).astype(jnp.bfloat16),
    )


def conv_rows(parts, band_ref, width, count):
    total = None
    for one in range(3):
        for two in range(3):
            window = parts[two][one * width : one * width + count]
            term = jnp.dot(window, band_ref[one * 3 + two], preferred_element_type=jnp.float32)
            total = term if total is None else total + term
    return total


def silu(values):
    return values / (1.0 + jnp.exp(-values))


def block_kernel(
    width, rows_out, cols_out,
    shifts_ref, up_ref, pick_ref, base_keep_ref, hidden_keep_ref, first_ref, second_ref,
    out_ref, band_ref,
):
    phases = []
    for phase in range(up_ref.shape[1]):
        total = None
        for high in range(up_ref.shape[0]):
            term = jnp.dot(shifts_ref[high], up_ref[high, phase], preferred_element_type=jnp.float32)
            total = term if total is None else total + term
        phases.append(total)
    phase_rows = silu(jnp.concatenate(phases, axis=0)).astype(jnp.bfloat16)
    base = jnp.dot(pick_ref[...], phase_rows, preferred_element_type=jnp.float32)
    base = jnp.where(base_keep_ref[...] > 0, base, 0.0)
    band_ref[...] = jnp.zeros(band_ref.shape, band_ref.dtype)
    fill_band(first_ref, band_ref)
    hidden_count = (rows_out + 2) * width
    first = conv_rows(shifted(base), band_ref, width, hidden_count)
    hidden = jnp.where(hidden_keep_ref[...] > 0, silu(first), 0.0)
    fill_band(second_ref, band_ref)
    out_count = rows_out * width
    second = conv_rows(shifted(hidden), band_ref, width, out_count)
    summed = base[2 * width : 2 * width + out_count] + second
    summed = pltpu.roll(summed, out_count - 2, 0).reshape(rows_out, width, summed.shape[1])
    out_ref[...] = summed[:, :cols_out].astype(out_ref.dtype)


def picker(rows, cols, width, span):
    place = jnp.arange(rows * width)
    one, two = place // width, place % width
    source = ((one % 4) * 4 + two % 4) * (rows // 4) * span + (one // 4) * span + two // 4
    chosen = (jnp.arange(rows * width)[None, :] == source[:, None]) & (two < cols)[:, None]
    return chosen.astype(jnp.bfloat16)


def body(coarse_field, up_weight, first_weight, second_weight):
    channels = up_weight.shape[3]
    coarse_depth = coarse_field.shape[2] // channels
    size_one, size_two = coarse_field.shape[:2]
    own_rows, own_cols = 4 * size_one, 4 * size_two
    lanes = 4 * coarse_depth * channels
    width, span = 32, 8
    up_mats = up_tables(up_weight, coarse_depth).reshape(4, 16, coarse_depth * channels, lanes)
    coarse_ext = extended_2(coarse_field, (("strike", 0), ("dip", 1)), 1)
    shifts = jnp.stack(
        [
            jnp.pad(
                coarse_ext[1 - one : size_one + 2 - one, 1 - two : size_two + 2 - two],
                ((0, 0), (0, span - size_two - 1), (0, 0)),
            )
            for one in (0, 1)
            for two in (0, 1)
        ]
    ).reshape(4, (size_one + 1) * span, -1)
    rows_all = inside("strike", own_rows + 4, own_rows, 2)
    cols_all = inside("dip", own_cols + 4, own_cols, 2)
    cols_all = jnp.pad(cols_all, (0, width - own_cols - 4))
    base_keep = (rows_all[:, None] & cols_all[None, :]).astype(jnp.float32).reshape(-1, 1)
    position = jnp.arange(width)
    cols_hidden = cols_all & (position >= 1) & (position < own_cols + 3)
    hidden_keep = rows_all[1 : own_rows + 3, None] & cols_hidden[None, :]
    hidden_keep = hidden_keep.astype(jnp.float32).reshape(-1, 1)
    vmem = pl.BlockSpec(memory_space=pltpu.VMEM)
    return pl.pallas_call(
        lambda *refs: block_kernel(width, own_rows, own_cols, *refs),
        out_shape=jax.ShapeDtypeStruct((own_rows, own_cols, lanes), jnp.bfloat16),
        in_specs=[vmem] * 7,
        out_specs=vmem,
        scratch_shapes=[pltpu.VMEM((9, lanes, lanes), jnp.bfloat16)],
    )(
        shifts,
        up_mats,
        picker(own_rows + 4, own_cols + 4, width, span),
        base_keep,
        hidden_keep,
        first_weight.reshape(-1, channels),
        second_weight.reshape(-1, channels),
    )


def solution(mesh):
    return jax.shard_map(
        body,
        mesh=mesh,
        in_specs=(P("strike", "dip", None), P(), P(), P()),
        out_specs=P("strike", "dip", None),
        check_vma=False,
    )
```

```python
import jax
import jax.numpy as jnp
import numpy as np
from jax import lax
from jax.experimental import pallas as pl
from jax.experimental.pallas import tpu as pltpu
from jax.sharding import PartitionSpec as P

HIGHEST = lax.Precision.HIGHEST


def extended_2(cells, sides, width):
    for axis, dim in sides:
        count = lax.axis_size(axis)
        ends = count - 1
        head = lax.slice_in_dim(cells, 0, width, axis=dim)
        tail = lax.slice_in_dim(cells, cells.shape[dim] - width, cells.shape[dim], axis=dim)
        cells = jnp.concatenate(
            [
                lax.ppermute(tail, axis, [(i, (i + 1) % count) for i in range(ends)]),
                cells,
                lax.ppermute(head, axis, [((i + 1) % count, i) for i in range(ends)]),
            ],
            axis=dim,
        )
    return cells


def inside(axis, count, own, halo):
    place = lax.axis_index(axis)
    local = jnp.arange(count) - halo
    return ((local >= 0) | (place > 0)) & ((local < own) | (place < lax.axis_size(axis) - 1))


def fill_band(weight_ref, band_ref):
    channels = weight_ref.shape[1]
    taps = weight_ref.shape[0] // (3 * channels)
    cells = band_ref.shape[1] // channels
    lane = lax.broadcasted_iota(jnp.int32, (channels, 128), 1)
    spread_out = (lane % channels == lax.broadcasted_iota(jnp.int32, (channels, 128), 0))
    tiled = jnp.dot(weight_ref[...], spread_out.astype(weight_ref.dtype), preferred_element_type=jnp.float32)
    quarter = lane // channels
    per_group = 128 // channels
    for tap in range(taps):
        for group in range(cells // per_group):
            for cell in range(max(0, per_group * group - 1), min(cells, per_group * group + per_group + 1)):
                block = jnp.zeros((channels, 128), jnp.float32)
                for out_cell in range(per_group):
                    depth = cell - per_group * group - out_cell + 1
                    if 0 <= depth <= 2:
                        row = (tap * 3 + depth) * channels
                        block = jnp.where(quarter == out_cell, tiled[row : row + channels], block)
                band_ref[tap, pl.ds(cell * channels, channels), pl.ds(128 * group, 128)] = block.astype(
                    band_ref.dtype
                )


def shifted(values):
    rows = values.shape[0]
    return (
        pltpu.roll(values, 1, 0).astype(jnp.bfloat16),
        values.astype(jnp.bfloat16),
        pltpu.roll(values, rows - 1, 0).astype(jnp.bfloat16),
    )


def conv_rows(parts, band_ref, width, count):
    total = None
    for one in range(3):
        for two in range(3):
            window = parts[two][one * width : one * width + count]
            term = jnp.dot(window, band_ref[one * 3 + two], preferred_element_type=jnp.float32)
            total = term if total is None else total + term
    return total


def silu(values):
    return values / (1.0 + jnp.exp(-values))


def fill_up(weight_ref, table_ref):
    channels = weight_ref.shape[1]
    lane = lax.broadcasted_iota(jnp.int32, (channels, 128), 1)
    spread_out = (lane % channels == lax.broadcasted_iota(jnp.int32, (channels, 128), 0))
    spread_out = spread_out.astype(weight_ref.dtype)
    quarter = lane // channels
    per_group = 128 // channels
    span = 8 * channels

    def one(taps, carry):
        start = pl.multiple_of(taps * span, span)
        tiled = jnp.dot(weight_ref[pl.ds(start, span)], spread_out, preferred_element_type=jnp.float32)
        for cell in range(3):
            block = jnp.zeros((channels, 128), jnp.float32)
            for out_cell in range(per_group):
                depth = 6 - 4 * cell + out_cell
                if 0 <= depth < 8:
                    block = jnp.where(quarter == out_cell, tiled[depth * channels : (depth + 1) * channels], block)
            table_ref[taps, pl.ds(cell * channels, channels), :] = block.astype(table_ref.dtype)
        return carry

    lax.fori_loop(0, table_ref.shape[0], one, 0)


def block_kernel(
    width, rows_out, cols_out,
    shifts_ref, up_ref, pick_ref, base_keep_ref, hidden_keep_ref, first_ref, second_ref,
    out_ref, band_ref, table_ref,
):
    fill_up(up_ref, table_ref)
    groups = 4
    rows_in = shifts_ref.shape[1] // groups
    phases = []
    for phase_one in range(4):
        for phase_two in range(4):
            total = None
            for high_one in (0, 1):
                for high_two in (0, 1):
                    taps = (4 * high_one + phase_one) * 8 + 4 * high_two + phase_two
                    term = jnp.dot(
                        shifts_ref[high_one * 2 + high_two], table_ref[taps],
                        preferred_element_type=jnp.float32,
                    )
                    total = term if total is None else total + term
            phases.append(
                jnp.concatenate([total[g * rows_in : (g + 1) * rows_in] for g in range(groups)], axis=1)
            )
    phase_rows = silu(jnp.concatenate(phases, axis=0)).astype(jnp.bfloat16)
    base = jnp.dot(pick_ref[...], phase_rows, preferred_element_type=jnp.float32)
    base = jnp.where(base_keep_ref[...] > 0, base, 0.0)
    band_ref[...] = jnp.zeros(band_ref.shape, band_ref.dtype)
    fill_band(first_ref, band_ref)
    hidden_count = (rows_out + 2) * width
    first = conv_rows(shifted(base), band_ref, width, hidden_count)
    hidden = jnp.where(hidden_keep_ref[...] > 0, silu(first), 0.0)
    fill_band(second_ref, band_ref)
    out_count = rows_out * width
    second = conv_rows(shifted(hidden), band_ref, width, out_count)
    summed = base[2 * width : 2 * width + out_count] + second
    summed = pltpu.roll(summed, out_count - 2, 0).reshape(rows_out, width, summed.shape[1])
    out_ref[...] = summed[:, :cols_out].astype(out_ref.dtype)


def picker(rows, cols, width, span):
    place = jnp.arange(rows * width)
    one, two = place // width, place % width
    source = ((one % 4) * 4 + two % 4) * (rows // 4) * span + (one // 4) * span + two // 4
    chosen = (jnp.arange(rows * width)[None, :] == source[:, None]) & (two < cols)[:, None]
    return chosen.astype(jnp.bfloat16)


def body(coarse_field, up_weight, first_weight, second_weight):
    channels = up_weight.shape[3]
    coarse_depth = coarse_field.shape[2] // channels
    size_one, size_two = coarse_field.shape[:2]
    own_rows, own_cols = 4 * size_one, 4 * size_two
    lanes = 4 * coarse_depth * channels
    width, span = 32, 8
    coarse_ext = extended_2(coarse_field, (("strike", 0), ("dip", 1)), 1)
    shifts = jnp.stack(
        [
            jnp.pad(
                coarse_ext[1 - one : size_one + 2 - one, 1 - two : size_two + 2 - two],
                ((0, 0), (0, span - size_two - 1), (0, 0)),
            )
            for one in (0, 1)
            for two in (0, 1)
        ]
    ).reshape(4, (size_one + 1) * span, -1)
    shifts = jnp.pad(shifts, ((0, 0), (0, 0), (channels, channels)))
    shifts = jnp.stack(
        [shifts[:, :, channels * g : channels * (g + 3)] for g in range(coarse_depth)], axis=1
    ).reshape(4, coarse_depth * (size_one + 1) * span, 3 * channels)
    rows_all = inside("strike", own_rows + 4, own_rows, 2)
    cols_all = inside("dip", own_cols + 4, own_cols, 2)
    cols_all = jnp.pad(cols_all, (0, width - own_cols - 4))
    base_keep = (rows_all[:, None] & cols_all[None, :]).astype(jnp.float32).reshape(-1, 1)
    position = jnp.arange(width)
    cols_hidden = cols_all & (position >= 1) & (position < own_cols + 3)
    hidden_keep = rows_all[1 : own_rows + 3, None] & cols_hidden[None, :]
    hidden_keep = hidden_keep.astype(jnp.float32).reshape(-1, 1)
    vmem = pl.BlockSpec(memory_space=pltpu.VMEM)
    return pl.pallas_call(
        lambda *refs: block_kernel(width, own_rows, own_cols, *refs),
        out_shape=jax.ShapeDtypeStruct((own_rows, own_cols, lanes), jnp.bfloat16),
        in_specs=[vmem] * 7,
        out_specs=vmem,
        scratch_shapes=[
            pltpu.VMEM((9, lanes, lanes), jnp.bfloat16),
            pltpu.VMEM((64, 3 * channels, 128), jnp.bfloat16),
        ],
    )(
        shifts,
        up_weight.reshape(-1, channels),
        picker(own_rows + 4, own_cols + 4, width, span),
        base_keep,
        hidden_keep,
        first_weight.reshape(-1, channels),
        second_weight.reshape(-1, channels),
    )


def solution(mesh):
    return jax.shard_map(
        body,
        mesh=mesh,
        in_specs=(P("strike", "dip", None), P(), P(), P()),
        out_specs=P("strike", "dip", None),
        check_vma=False,
    )
```

```python
import jax
import jax.numpy as jnp
import numpy as np
from jax import lax
from jax.experimental import pallas as pl
from jax.experimental.pallas import tpu as pltpu
from jax.sharding import PartitionSpec as P

HIGHEST = lax.Precision.HIGHEST


def extended_2(cells, sides, width):
    for axis, dim in sides:
        count = lax.axis_size(axis)
        ends = count - 1
        head = lax.slice_in_dim(cells, 0, width, axis=dim)
        tail = lax.slice_in_dim(cells, cells.shape[dim] - width, cells.shape[dim], axis=dim)
        cells = jnp.concatenate(
            [
                lax.ppermute(tail, axis, [(i, (i + 1) % count) for i in range(ends)]),
                cells,
                lax.ppermute(head, axis, [((i + 1) % count, i) for i in range(ends)]),
            ],
            axis=dim,
        )
    return cells


def inside(axis, count, own, halo):
    place = lax.axis_index(axis)
    local = jnp.arange(count) - halo
    return ((local >= 0) | (place > 0)) & ((local < own) | (place < lax.axis_size(axis) - 1))


def fill_band(weight_ref, band_ref):
    channels = weight_ref.shape[1]
    taps = weight_ref.shape[0] // (3 * channels)
    cells = band_ref.shape[1] // channels
    lane = lax.broadcasted_iota(jnp.int32, (channels, 128), 1)
    spread_out = (lane % channels == lax.broadcasted_iota(jnp.int32, (channels, 128), 0))
    tiled = jnp.dot(weight_ref[...], spread_out.astype(weight_ref.dtype), preferred_element_type=jnp.float32)
    quarter = lane // channels
    per_group = 128 // channels
    for tap in range(taps):
        for group in range(cells // per_group):
            for cell in range(max(0, per_group * group - 1), min(cells, per_group * group + per_group + 1)):
                block = jnp.zeros((channels, 128), jnp.float32)
                for out_cell in range(per_group):
                    depth = cell - per_group * group - out_cell + 1
                    if 0 <= depth <= 2:
                        row = (tap * 3 + depth) * channels
                        block = jnp.where(quarter == out_cell, tiled[row : row + channels], block)
                band_ref[tap, pl.ds(cell * channels, channels), pl.ds(128 * group, 128)] = block.astype(
                    band_ref.dtype
                )


def shifted(values):
    rows = values.shape[0]
    return (
        pltpu.roll(values, 1, 0).astype(jnp.bfloat16),
        values.astype(jnp.bfloat16),
        pltpu.roll(values, rows - 1, 0).astype(jnp.bfloat16),
    )


def conv_rows(parts, band_ref, width, count):
    total = None
    for one in range(3):
        for two in range(3):
            window = parts[two][one * width : one * width + count]
            term = jnp.dot(window, band_ref[one * 3 + two], preferred_element_type=jnp.float32)
            total = term if total is None else total + term
    return total


def silu(values):
    return values / (1.0 + jnp.exp(-values))


def fill_up(weight_ref, table_ref):
    channels = weight_ref.shape[1]
    lane = lax.broadcasted_iota(jnp.int32, (channels, 128), 1)
    spread_out = (lane % channels == lax.broadcasted_iota(jnp.int32, (channels, 128), 0))
    spread_out = spread_out.astype(weight_ref.dtype)
    quarter = lane // channels
    per_group = 128 // channels
    span = 8 * channels

    def one(taps, carry):
        start = pl.multiple_of(taps * span, span)
        tiled = jnp.dot(weight_ref[pl.ds(start, span)], spread_out, preferred_element_type=jnp.float32)
        for cell in range(3):
            block = jnp.zeros((channels, 128), jnp.float32)
            for out_cell in range(per_group):
                depth = 6 - 4 * cell + out_cell
                if 0 <= depth < 8:
                    block = jnp.where(quarter == out_cell, tiled[depth * channels : (depth + 1) * channels], block)
            table_ref[taps, pl.ds(cell * channels, channels), :] = block.astype(table_ref.dtype)
        return carry

    lax.fori_loop(0, table_ref.shape[0], one, 0)


def block_kernel(
    width, rows_out, cols_out,
    shifts_ref, up_ref, pick_ref, base_keep_ref, hidden_keep_ref, first_ref, second_ref,
    out_ref, band_ref,
):
    table_ref = up_ref
    groups = 4
    rows_in = shifts_ref.shape[1] // groups
    phases = []
    for phase_one in range(4):
        for phase_two in range(4):
            total = None
            for high_one in (0, 1):
                for high_two in (0, 1):
                    taps = (4 * high_one + phase_one) * 8 + 4 * high_two + phase_two
                    term = jnp.dot(
                        shifts_ref[high_one * 2 + high_two], table_ref[taps],
                        preferred_element_type=jnp.float32,
                    )
                    total = term if total is None else total + term
            phases.append(
                jnp.concatenate([total[g * rows_in : (g + 1) * rows_in] for g in range(groups)], axis=1)
            )
    phase_rows = silu(jnp.concatenate(phases, axis=0)).astype(jnp.bfloat16)
    base = jnp.dot(pick_ref[...], phase_rows, preferred_element_type=jnp.float32)
    base = jnp.where(base_keep_ref[...] > 0, base, 0.0)
    band_ref[...] = jnp.zeros(band_ref.shape, band_ref.dtype)
    fill_band(first_ref, band_ref)
    hidden_count = (rows_out + 2) * width
    first = conv_rows(shifted(base), band_ref, width, hidden_count)
    hidden = jnp.where(hidden_keep_ref[...] > 0, silu(first), 0.0)
    fill_band(second_ref, band_ref)
    out_count = rows_out * width
    second = conv_rows(shifted(hidden), band_ref, width, out_count)
    summed = base[2 * width : 2 * width + out_count] + second
    summed = pltpu.roll(summed, out_count - 2, 0).reshape(rows_out, width, summed.shape[1])
    out_ref[...] = summed[:, :cols_out].astype(out_ref.dtype)


def picker(rows, cols, width, span):
    place = jnp.arange(rows * width)
    one, two = place // width, place % width
    source = ((one % 4) * 4 + two % 4) * (rows // 4) * span + (one // 4) * span + two // 4
    chosen = (jnp.arange(rows * width)[None, :] == source[:, None]) & (two < cols)[:, None]
    return chosen.astype(jnp.bfloat16)


def body(coarse_field, up_weight, first_weight, second_weight):
    channels = up_weight.shape[3]
    coarse_depth = coarse_field.shape[2] // channels
    size_one, size_two = coarse_field.shape[:2]
    own_rows, own_cols = 4 * size_one, 4 * size_two
    lanes = 4 * coarse_depth * channels
    width, span = 32, 8
    vmem = pl.BlockSpec(memory_space=pltpu.VMEM)
    table = pl.pallas_call(
        fill_up,
        out_shape=jax.ShapeDtypeStruct((64, 3 * channels, 128), jnp.bfloat16),
        in_specs=[vmem],
        out_specs=vmem,
        cost_estimate=pl.CostEstimate(
            flops=2 * up_weight.size * 128, transcendentals=0, bytes_accessed=2 * up_weight.size + 64 * 3 * channels * 256
        ),
    )(up_weight.reshape(-1, channels))
    coarse_ext = extended_2(coarse_field, (("strike", 0), ("dip", 1)), 1)
    shifts = jnp.stack(
        [
            jnp.pad(
                coarse_ext[1 - one : size_one + 2 - one, 1 - two : size_two + 2 - two],
                ((0, 0), (0, span - size_two - 1), (0, 0)),
            )
            for one in (0, 1)
            for two in (0, 1)
        ]
    ).reshape(4, (size_one + 1) * span, -1)
    shifts = jnp.pad(shifts, ((0, 0), (0, 0), (channels, channels)))
    shifts = jnp.stack(
        [shifts[:, :, channels * g : channels * (g + 3)] for g in range(coarse_depth)], axis=1
    ).reshape(4, coarse_depth * (size_one + 1) * span, 3 * channels)
    rows_all = inside("strike", own_rows + 4, own_rows, 2)
    cols_all = inside("dip", own_cols + 4, own_cols, 2)
    cols_all = jnp.pad(cols_all, (0, width - own_cols - 4))
    base_keep = (rows_all[:, None] & cols_all[None, :]).astype(jnp.float32).reshape(-1, 1)
    position = jnp.arange(width)
    cols_hidden = cols_all & (position >= 1) & (position < own_cols + 3)
    hidden_keep = rows_all[1 : own_rows + 3, None] & cols_hidden[None, :]
    hidden_keep = hidden_keep.astype(jnp.float32).reshape(-1, 1)
    vmem = pl.BlockSpec(memory_space=pltpu.VMEM)
    return pl.pallas_call(
        lambda *refs: block_kernel(width, own_rows, own_cols, *refs),
        out_shape=jax.ShapeDtypeStruct((own_rows, own_cols, lanes), jnp.bfloat16),
        in_specs=[vmem] * 7,
        out_specs=vmem,
        scratch_shapes=[
            pltpu.VMEM((9, lanes, lanes), jnp.bfloat16),
        ],
    )(
        shifts,
        table,
        picker(own_rows + 4, own_cols + 4, width, span),
        base_keep,
        hidden_keep,
        first_weight.reshape(-1, channels),
        second_weight.reshape(-1, channels),
    )


def solution(mesh):
    return jax.shard_map(
        body,
        mesh=mesh,
        in_specs=(P("strike", "dip", None), P(), P(), P()),
        out_specs=P("strike", "dip", None),
        check_vma=False,
    )
```

```python
import jax
import jax.numpy as jnp
import numpy as np
from jax import lax
from jax.experimental import pallas as pl
from jax.experimental.pallas import tpu as pltpu
from jax.sharding import PartitionSpec as P

HIGHEST = lax.Precision.HIGHEST


def extended_2(cells, sides, width):
    for axis, dim in sides:
        count = lax.axis_size(axis)
        ends = count - 1
        head = lax.slice_in_dim(cells, 0, width, axis=dim)
        tail = lax.slice_in_dim(cells, cells.shape[dim] - width, cells.shape[dim], axis=dim)
        cells = jnp.concatenate(
            [
                lax.ppermute(tail, axis, [(i, (i + 1) % count) for i in range(ends)]),
                cells,
                lax.ppermute(head, axis, [((i + 1) % count, i) for i in range(ends)]),
            ],
            axis=dim,
        )
    return cells


def inside(axis, count, own, halo):
    place = lax.axis_index(axis)
    local = jnp.arange(count) - halo
    return ((local >= 0) | (place > 0)) & ((local < own) | (place < lax.axis_size(axis) - 1))


def fill_band(weight_ref, band_ref):
    channels = weight_ref.shape[1]
    taps = weight_ref.shape[0] // (3 * channels)
    cells = band_ref.shape[1] // channels
    lane = lax.broadcasted_iota(jnp.int32, (channels, 128), 1)
    spread_out = (lane % channels == lax.broadcasted_iota(jnp.int32, (channels, 128), 0))
    tiled = jnp.dot(weight_ref[...], spread_out.astype(weight_ref.dtype), preferred_element_type=jnp.float32)
    quarter = lane // channels
    per_group = 128 // channels
    for tap in range(taps):
        for group in range(cells // per_group):
            for cell in range(max(0, per_group * group - 1), min(cells, per_group * group + per_group + 1)):
                block = jnp.zeros((channels, 128), jnp.float32)
                for out_cell in range(per_group):
                    depth = cell - per_group * group - out_cell + 1
                    if 0 <= depth <= 2:
                        row = (tap * 3 + depth) * channels
                        block = jnp.where(quarter == out_cell, tiled[row : row + channels], block)
                band_ref[tap, pl.ds(cell * channels, channels), pl.ds(128 * group, 128)] = block.astype(
                    band_ref.dtype
                )


def shifted(values):
    rows = values.shape[0]
    return (
        pltpu.roll(values, 1, 0).astype(jnp.bfloat16),
        values.astype(jnp.bfloat16),
        pltpu.roll(values, rows - 1, 0).astype(jnp.bfloat16),
    )


def conv_rows(parts, band_ref, width, count):
    total = None
    for one in range(3):
        for two in range(3):
            window = parts[two][one * width : one * width + count]
            term = jnp.dot(window, band_ref[one * 3 + two], preferred_element_type=jnp.float32)
            total = term if total is None else total + term
    return total


def silu(values):
    return values / (1.0 + jnp.exp(-values))


def fill_up(weight_ref, table_ref):
    channels = weight_ref.shape[1]
    lane = lax.broadcasted_iota(jnp.int32, (channels, 128), 1)
    spread_out = (lane % channels == lax.broadcasted_iota(jnp.int32, (channels, 128), 0))
    spread_out = spread_out.astype(weight_ref.dtype)
    quarter = lane // channels
    per_group = 128 // channels
    span = 8 * channels

    chunk = 8

    def one(step, carry):
        start = pl.multiple_of(step * chunk * span, chunk * span)
        tiled = jnp.dot(
            weight_ref[pl.ds(start, chunk * span)], spread_out, preferred_element_type=jnp.float32
        )
        for part in range(chunk):
            for cell in range(3):
                block = jnp.zeros((channels, 128), jnp.float32)
                for out_cell in range(per_group):
                    depth = 6 - 4 * cell + out_cell
                    if 0 <= depth < 8:
                        row = part * span + depth * channels
                        block = jnp.where(quarter == out_cell, tiled[row : row + channels], block)
                table_ref[step * chunk + part, pl.ds(cell * channels, channels), :] = block.astype(
                    table_ref.dtype
                )
        return carry

    lax.fori_loop(0, table_ref.shape[0] // chunk, one, 0)


def block_kernel(
    width, rows_out, cols_out,
    shifts_ref, up_ref, pick_ref, base_keep_ref, hidden_keep_ref, first_ref, second_ref,
    out_ref, band_ref, table_ref,
):
    fill_up(up_ref, table_ref)
    groups = 4
    rows_in = shifts_ref.shape[1] // groups
    phases = []
    for phase_one in range(4):
        for phase_two in range(4):
            total = None
            for high_one in (0, 1):
                for high_two in (0, 1):
                    taps = (4 * high_one + phase_one) * 8 + 4 * high_two + phase_two
                    term = jnp.dot(
                        shifts_ref[high_one * 2 + high_two], table_ref[taps],
                        preferred_element_type=jnp.float32,
                    )
                    total = term if total is None else total + term
            phases.append(
                jnp.concatenate([total[g * rows_in : (g + 1) * rows_in] for g in range(groups)], axis=1)
            )
    phase_rows = silu(jnp.concatenate(phases, axis=0)).astype(jnp.bfloat16)
    base = jnp.dot(pick_ref[...], phase_rows, preferred_element_type=jnp.float32)
    base = jnp.where(base_keep_ref[...] > 0, base, 0.0)
    band_ref[...] = jnp.zeros(band_ref.shape, band_ref.dtype)
    fill_band(first_ref, band_ref)
    hidden_count = (rows_out + 2) * width
    first = conv_rows(shifted(base), band_ref, width, hidden_count)
    hidden = jnp.where(hidden_keep_ref[...] > 0, silu(first), 0.0)
    fill_band(second_ref, band_ref)
    out_count = rows_out * width
    second = conv_rows(shifted(hidden), band_ref, width, out_count)
    summed = base[2 * width : 2 * width + out_count] + second
    summed = pltpu.roll(summed, out_count - 2, 0).reshape(rows_out, width, summed.shape[1])
    out_ref[...] = summed[:, :cols_out].astype(out_ref.dtype)


def picker(rows, cols, width, span):
    place = jnp.arange(rows * width)
    one, two = place // width, place % width
    source = ((one % 4) * 4 + two % 4) * (rows // 4) * span + (one // 4) * span + two // 4
    chosen = (jnp.arange(rows * width)[None, :] == source[:, None]) & (two < cols)[:, None]
    return chosen.astype(jnp.bfloat16)


def body(coarse_field, up_weight, first_weight, second_weight):
    channels = up_weight.shape[3]
    coarse_depth = coarse_field.shape[2] // channels
    size_one, size_two = coarse_field.shape[:2]
    own_rows, own_cols = 4 * size_one, 4 * size_two
    lanes = 4 * coarse_depth * channels
    width, span = 32, 8
    coarse_ext = extended_2(coarse_field, (("strike", 0), ("dip", 1)), 1)
    shifts = jnp.stack(
        [
            jnp.pad(
                coarse_ext[1 - one : size_one + 2 - one, 1 - two : size_two + 2 - two],
                ((0, 0), (0, span - size_two - 1), (0, 0)),
            )
            for one in (0, 1)
            for two in (0, 1)
        ]
    ).reshape(4, (size_one + 1) * span, -1)
    shifts = jnp.pad(shifts, ((0, 0), (0, 0), (channels, channels)))
    shifts = jnp.stack(
        [shifts[:, :, channels * g : channels * (g + 3)] for g in range(coarse_depth)], axis=1
    ).reshape(4, coarse_depth * (size_one + 1) * span, 3 * channels)
    rows_all = inside("strike", own_rows + 4, own_rows, 2)
    cols_all = inside("dip", own_cols + 4, own_cols, 2)
    cols_all = jnp.pad(cols_all, (0, width - own_cols - 4))
    base_keep = (rows_all[:, None] & cols_all[None, :]).astype(jnp.float32).reshape(-1, 1)
    position = jnp.arange(width)
    cols_hidden = cols_all & (position >= 1) & (position < own_cols + 3)
    hidden_keep = rows_all[1 : own_rows + 3, None] & cols_hidden[None, :]
    hidden_keep = hidden_keep.astype(jnp.float32).reshape(-1, 1)
    vmem = pl.BlockSpec(memory_space=pltpu.VMEM)
    return pl.pallas_call(
        lambda *refs: block_kernel(width, own_rows, own_cols, *refs),
        out_shape=jax.ShapeDtypeStruct((own_rows, own_cols, lanes), jnp.bfloat16),
        in_specs=[vmem] * 7,
        out_specs=vmem,
        scratch_shapes=[
            pltpu.VMEM((9, lanes, lanes), jnp.bfloat16),
            pltpu.VMEM((64, 3 * channels, 128), jnp.bfloat16),
        ],
    )(
        shifts,
        up_weight.reshape(-1, channels),
        picker(own_rows + 4, own_cols + 4, width, span),
        base_keep,
        hidden_keep,
        first_weight.reshape(-1, channels),
        second_weight.reshape(-1, channels),
    )


def solution(mesh):
    return jax.shard_map(
        body,
        mesh=mesh,
        in_specs=(P("strike", "dip", None), P(), P(), P()),
        out_specs=P("strike", "dip", None),
        check_vma=False,
    )
```

```python
import jax
import jax.numpy as jnp
import numpy as np
from jax import lax
from jax.experimental import pallas as pl
from jax.experimental.pallas import tpu as pltpu
from jax.sharding import PartitionSpec as P

HIGHEST = lax.Precision.HIGHEST


def inside(axis, count, own, halo):
    place = lax.axis_index(axis)
    local = jnp.arange(count) - halo
    return ((local >= 0) | (place > 0)) & ((local < own) | (place < lax.axis_size(axis) - 1))


def fill_band(weight_ref, band_ref):
    channels = weight_ref.shape[1]
    taps = weight_ref.shape[0] // (3 * channels)
    cells = band_ref.shape[1] // channels
    lane = lax.broadcasted_iota(jnp.int32, (channels, 128), 1)
    spread_out = (lane % channels == lax.broadcasted_iota(jnp.int32, (channels, 128), 0))
    tiled = jnp.dot(weight_ref[...], spread_out.astype(weight_ref.dtype), preferred_element_type=jnp.float32)
    quarter = lane // channels
    per_group = 128 // channels
    for tap in range(taps):
        for group in range(cells // per_group):
            for cell in range(max(0, per_group * group - 1), min(cells, per_group * group + per_group + 1)):
                block = jnp.zeros((channels, 128), jnp.float32)
                for out_cell in range(per_group):
                    depth = cell - per_group * group - out_cell + 1
                    if 0 <= depth <= 2:
                        row = (tap * 3 + depth) * channels
                        block = jnp.where(quarter == out_cell, tiled[row : row + channels], block)
                band_ref[tap, pl.ds(cell * channels, channels), pl.ds(128 * group, 128)] = block.astype(
                    band_ref.dtype
                )


def shifted(values):
    rows = values.shape[0]
    return (
        pltpu.roll(values, 1, 0).astype(jnp.bfloat16),
        values.astype(jnp.bfloat16),
        pltpu.roll(values, rows - 1, 0).astype(jnp.bfloat16),
    )


def conv_rows(parts, band_ref, width, count):
    total = None
    for one in range(3):
        for two in range(3):
            window = parts[two][one * width : one * width + count]
            term = jnp.dot(window, band_ref[one * 3 + two], preferred_element_type=jnp.float32)
            total = term if total is None else total + term
    return total


def silu(values):
    return values / (1.0 + jnp.exp(-values))


def fill_up(weight_ref, table_ref):
    channels = weight_ref.shape[1]
    lane = lax.broadcasted_iota(jnp.int32, (channels, 128), 1)
    spread_out = (lane % channels == lax.broadcasted_iota(jnp.int32, (channels, 128), 0))
    spread_out = spread_out.astype(weight_ref.dtype)
    quarter = lane // channels
    per_group = 128 // channels
    span = 8 * channels

    chunk = 8

    def one(step, carry):
        start = pl.multiple_of(step * chunk * span, chunk * span)
        tiled = jnp.dot(
            weight_ref[pl.ds(start, chunk * span)], spread_out, preferred_element_type=jnp.float32
        )
        for part in range(chunk):
            table_ref[step * chunk + part, pl.ds(3 * channels, channels), :] = jnp.zeros(
                (channels, 128), table_ref.dtype
            )
            for cell in range(3):
                block = jnp.zeros((channels, 128), jnp.float32)
                for out_cell in range(per_group):
                    depth = 6 - 4 * cell + out_cell
                    if 0 <= depth < 8:
                        row = part * span + depth * channels
                        block = jnp.where(quarter == out_cell, tiled[row : row + channels], block)
                table_ref[step * chunk + part, pl.ds(cell * channels, channels), :] = block.astype(
                    table_ref.dtype
                )
        return carry

    lax.fori_loop(0, table_ref.shape[0] // chunk, one, 0)


DIRECTIONS = [(-1, -1), (-1, 0), (-1, 1), (0, -1), (0, 1), (1, -1), (1, 0), (1, 1)]


def halo_rows(own_ref, staging_ref, size_one):
    sub = lax.broadcasted_iota(jnp.int32, own_ref.shape[1:], 0)

    def block_row(one, two, row):
        if (one, two) == (0, 0):
            return own_ref[row]
        return staging_ref[DIRECTIONS.index((one, two)), row]

    rows = []
    for ext in range(size_one + 2):
        one = -1 if ext == 0 else (1 if ext == size_one + 1 else 0)
        row = size_one - 1 if ext == 0 else (0 if ext == size_one + 1 else ext - 1)
        left = pltpu.roll(block_row(one, -1, row), 5, 0)
        middle = pltpu.roll(block_row(one, 0, row), 1, 0)
        right = pltpu.roll(block_row(one, 1, row), 5, 0)
        value = jnp.where(sub == 5, right, 0.0)
        value = jnp.where((sub >= 1) & (sub <= 4), middle, value)
        rows.append(jnp.where(sub == 0, left, value))
    return rows


def block_kernel(
    width, rows_out, cols_out, grid_shape,
    own_ref, up_ref, pick_ref, base_keep_ref, hidden_keep_ref, first_ref, second_ref,
    out_ref, band_ref, table_ref, staging_ref, send_sems, recv_sems,
):
    place = (lax.axis_index("strike"), lax.axis_index("dip"))
    present = [
        (place[0] + one >= 0) & (place[0] + one < grid_shape[0]) & (place[1] + two >= 0) & (place[1] + two < grid_shape[1])
        for one, two in DIRECTIONS
    ]
    for slot in range(len(DIRECTIONS)):
        @pl.when(jnp.logical_not(present[slot]))
        def _():
            staging_ref[slot] = jnp.zeros(staging_ref.shape[1:], staging_ref.dtype)

    barrier = pltpu.get_barrier_semaphore()
    for slot, (one, two) in enumerate(DIRECTIONS):
        @pl.when(present[slot])
        def _():
            pl.semaphore_signal(
                barrier, 1, device_id=(place[0] + one, place[1] + two),
                device_id_type=pl.DeviceIdType.MESH,
            )
    count = sum(p.astype(jnp.int32) for p in present)
    pl.semaphore_wait(barrier, count)

    copies = []
    for slot, (one, two) in enumerate(DIRECTIONS):
        far = len(DIRECTIONS) - 1 - slot
        copy = pltpu.make_async_remote_copy(
            src_ref=own_ref, dst_ref=staging_ref.at[far], send_sem=send_sems.at[slot],
            recv_sem=recv_sems.at[far], device_id=(place[0] + one, place[1] + two),
            device_id_type=pl.DeviceIdType.MESH,
        )
        pl.when(present[slot])(copy.start)
        copies.append(copy)

    fill_up(up_ref, table_ref)
    band_ref[...] = jnp.zeros(band_ref.shape, band_ref.dtype)
    fill_band(first_ref, band_ref)

    for slot, (one, two) in enumerate(DIRECTIONS):
        incoming = pltpu.make_async_remote_copy(
            src_ref=own_ref, dst_ref=staging_ref.at[slot], send_sem=send_sems.at[slot],
            recv_sem=recv_sems.at[slot], device_id=(place[0] + one, place[1] + two),
            device_id_type=pl.DeviceIdType.MESH,
        )

        @pl.when(present[slot])
        def _():
            copies[slot].wait_send()
            incoming.wait_recv()

    size_one = own_ref.shape[0]
    ext = halo_rows(own_ref, staging_ref, size_one)
    groups = 4
    channels = table_ref.shape[1] // groups
    lane = lax.broadcasted_iota(jnp.int32, ((size_one + 1) * own_ref.shape[1], 128), 1)
    windows = []
    for high_one in (0, 1):
        for high_two in (0, 1):
            shifted_rows = [
                ext[m + 1 - high_one] if high_two else pltpu.roll(ext[m + 1 - high_one], own_ref.shape[1] - 1, 0)
                for m in range(size_one + 1)
            ]
            rows = jnp.concatenate(shifted_rows, axis=0)
            parts = []
            for g in range(groups):
                rolled = pltpu.roll(rows, (channels - channels * g) % 128, 1)
                keep = lane < 3 * channels
                if g == 0:
                    keep = keep & (lane >= channels)
                if g == groups - 1:
                    keep = keep & (lane < 2 * channels)
                parts.append(jnp.where(keep, rolled, 0.0))
            windows.append(jnp.concatenate(parts, axis=0).astype(jnp.bfloat16))
    rows_in = (size_one + 1) * own_ref.shape[1]
    phases = []
    for phase_one in range(4):
        for phase_two in range(4):
            total = None
            for high_one in (0, 1):
                for high_two in (0, 1):
                    taps = (4 * high_one + phase_one) * 8 + 4 * high_two + phase_two
                    term = jnp.dot(
                        windows[high_one * 2 + high_two], table_ref[taps],
                        preferred_element_type=jnp.float32,
                    )
                    total = term if total is None else total + term
            phases.append(
                jnp.concatenate([total[g * rows_in : (g + 1) * rows_in] for g in range(groups)], axis=1)
            )
    phase_rows = silu(jnp.concatenate(phases, axis=0)).astype(jnp.bfloat16)
    base = jnp.dot(pick_ref[...], phase_rows, preferred_element_type=jnp.float32)
    base = jnp.where(base_keep_ref[...] > 0, base, 0.0)
    hidden_count = (rows_out + 2) * width
    first = conv_rows(shifted(base), band_ref, width, hidden_count)
    hidden = jnp.where(hidden_keep_ref[...] > 0, silu(first), 0.0)
    fill_band(second_ref, band_ref)
    out_count = rows_out * width
    second = conv_rows(shifted(hidden), band_ref, width, out_count)
    summed = base[2 * width : 2 * width + out_count] + second
    summed = pltpu.roll(summed, out_count - 2, 0).reshape(rows_out, width, summed.shape[1])
    out_ref[...] = summed[:, :cols_out].astype(out_ref.dtype)


def picker(rows, cols, width, span):
    place = jnp.arange(rows * width)
    one, two = place // width, place % width
    source = ((one % 4) * 4 + two % 4) * (rows // 4) * span + (one // 4) * span + two // 4
    chosen = (jnp.arange(rows * width)[None, :] == source[:, None]) & (two < cols)[:, None]
    return chosen.astype(jnp.bfloat16)


def body(coarse_field, up_weight, first_weight, second_weight):
    channels = up_weight.shape[3]
    coarse_depth = coarse_field.shape[2] // channels
    size_one, size_two = coarse_field.shape[:2]
    own_rows, own_cols = 4 * size_one, 4 * size_two
    lanes = 4 * coarse_depth * channels
    width, span = 32, 8
    own = jnp.pad(coarse_field.astype(jnp.float32), ((0, 0), (0, span - size_two), (0, 0)))
    rows_all = inside("strike", own_rows + 4, own_rows, 2)
    cols_all = inside("dip", own_cols + 4, own_cols, 2)
    cols_all = jnp.pad(cols_all, (0, width - own_cols - 4))
    base_keep = (rows_all[:, None] & cols_all[None, :]).astype(jnp.float32).reshape(-1, 1)
    position = jnp.arange(width)
    cols_hidden = cols_all & (position >= 1) & (position < own_cols + 3)
    hidden_keep = rows_all[1 : own_rows + 3, None] & cols_hidden[None, :]
    hidden_keep = hidden_keep.astype(jnp.float32).reshape(-1, 1)
    vmem = pl.BlockSpec(memory_space=pltpu.VMEM)
    grid_shape = (lax.axis_size("strike"), lax.axis_size("dip"))
    return pl.pallas_call(
        lambda *refs: block_kernel(width, own_rows, own_cols, grid_shape, *refs),
        out_shape=jax.ShapeDtypeStruct((own_rows, own_cols, lanes), jnp.bfloat16),
        in_specs=[vmem] * 7,
        out_specs=vmem,
        scratch_shapes=[
            pltpu.VMEM((9, lanes, lanes), jnp.bfloat16),
            pltpu.VMEM((64, 4 * channels, 128), jnp.bfloat16),
            pltpu.VMEM((len(DIRECTIONS),) + own.shape, jnp.float32),
            pltpu.SemaphoreType.DMA((len(DIRECTIONS),)),
            pltpu.SemaphoreType.DMA((len(DIRECTIONS),)),
        ],
        compiler_params=pltpu.CompilerParams(collective_id=0, has_side_effects=True),
    )(
        own,
        up_weight.reshape(-1, channels),
        picker(own_rows + 4, own_cols + 4, width, span),
        base_keep,
        hidden_keep,
        first_weight.reshape(-1, channels),
        second_weight.reshape(-1, channels),
    )


def solution(mesh):
    return jax.shard_map(
        body,
        mesh=mesh,
        in_specs=(P("strike", "dip", None), P(), P(), P()),
        out_specs=P("strike", "dip", None),
        check_vma=False,
    )
```

```python
import jax
import jax.numpy as jnp
import ml_dtypes
import numpy as np
from jax import lax
from jax.experimental import pallas as pl
from jax.experimental.pallas import tpu as pltpu
from jax.sharding import PartitionSpec as P

HIGHEST = lax.Precision.HIGHEST


def fill_band(weight_ref, band_ref):
    channels = weight_ref.shape[1]
    taps = weight_ref.shape[0] // (3 * channels)
    cells = band_ref.shape[1] // channels
    lane = lax.broadcasted_iota(jnp.int32, (channels, 128), 1)
    spread_out = (lane % channels == lax.broadcasted_iota(jnp.int32, (channels, 128), 0))
    tiled = jnp.dot(weight_ref[...], spread_out.astype(weight_ref.dtype), preferred_element_type=jnp.float32)
    quarter = lane // channels
    per_group = 128 // channels
    for tap in range(taps):
        for group in range(cells // per_group):
            for cell in range(max(0, per_group * group - 1), min(cells, per_group * group + per_group + 1)):
                block = jnp.zeros((channels, 128), jnp.float32)
                for out_cell in range(per_group):
                    depth = cell - per_group * group - out_cell + 1
                    if 0 <= depth <= 2:
                        row = (tap * 3 + depth) * channels
                        block = jnp.where(quarter == out_cell, tiled[row : row + channels], block)
                band_ref[tap, pl.ds(cell * channels, channels), pl.ds(128 * group, 128)] = block.astype(
                    band_ref.dtype
                )


def shifted(values):
    rows = values.shape[0]
    return (
        pltpu.roll(values, 1, 0).astype(jnp.bfloat16),
        values.astype(jnp.bfloat16),
        pltpu.roll(values, rows - 1, 0).astype(jnp.bfloat16),
    )


def conv_rows(parts, band_ref, width, count):
    lanes = band_ref.shape[1]
    halves = []
    for half in range(lanes // 256):
        low = min(max(256 * half - 128, 0), lanes - 384)
        total = None
        for one in range(3):
            for two in range(3):
                window = parts[two][one * width : one * width + count, low : low + 384]
                term = jnp.dot(
                    window, band_ref[one * 3 + two, low : low + 384, 256 * half : 256 * half + 256],
                    preferred_element_type=jnp.float32,
                )
                total = term if total is None else total + term
        halves.append(total)
    return jnp.concatenate(halves, axis=1)


def keep_rows(place, grid_shape, own, first, count, width, low, high):
    index = lax.broadcasted_iota(jnp.int32, (count * width, 1), 0)
    one = lax.shift_right_logical(index, 5) + first - 2
    two = jnp.bitwise_and(index, 31) - 2
    keep = ((one >= 0) | (place[0] > 0)) & ((one < own[0]) | (place[0] < grid_shape[0] - 1))
    keep = keep & ((two >= 0) | (place[1] > 0)) & ((two < own[1]) | (place[1] < grid_shape[1] - 1))
    return keep & (two + 2 >= low) & (two + 2 < high)


def silu(values):
    return values / (1.0 + jnp.exp(-values))


def fill_up(weight_ref, table_ref):
    channels = weight_ref.shape[1]
    lane = lax.broadcasted_iota(jnp.int32, (channels, 128), 1)
    spread_out = (lane % channels == lax.broadcasted_iota(jnp.int32, (channels, 128), 0))
    spread_out = spread_out.astype(weight_ref.dtype)
    quarter = lane // channels
    per_group = 128 // channels
    span = 8 * channels

    chunk = 8

    def one(step, carry):
        start = pl.multiple_of(step * chunk * span, chunk * span)
        tiled = jnp.dot(
            weight_ref[pl.ds(start, chunk * span)], spread_out, preferred_element_type=jnp.float32
        )
        for part in range(chunk):
            table_ref[step * chunk + part, pl.ds(3 * channels, channels), :] = jnp.zeros(
                (channels, 128), table_ref.dtype
            )
            for cell in range(3):
                block = jnp.zeros((channels, 128), jnp.float32)
                for out_cell in range(per_group):
                    depth = 6 - 4 * cell + out_cell
                    if 0 <= depth < 8:
                        row = part * span + depth * channels
                        block = jnp.where(quarter == out_cell, tiled[row : row + channels], block)
                table_ref[step * chunk + part, pl.ds(cell * channels, channels), :] = block.astype(
                    table_ref.dtype
                )
        return carry

    lax.fori_loop(0, table_ref.shape[0] // chunk, one, 0)


DIRECTIONS = [(-1, -1), (-1, 0), (-1, 1), (0, -1), (0, 1), (1, -1), (1, 0), (1, 1)]


def halo_rows(own_ref, staging_ref, size_one):
    sub = lax.broadcasted_iota(jnp.int32, own_ref.shape[1:], 0)

    def block_row(one, two, row):
        if (one, two) == (0, 0):
            return own_ref[row]
        return staging_ref[DIRECTIONS.index((one, two)), row]

    rows = []
    for ext in range(size_one + 2):
        one = -1 if ext == 0 else (1 if ext == size_one + 1 else 0)
        row = size_one - 1 if ext == 0 else (0 if ext == size_one + 1 else ext - 1)
        left = pltpu.roll(block_row(one, -1, row), 5, 0)
        middle = pltpu.roll(block_row(one, 0, row), 1, 0)
        right = pltpu.roll(block_row(one, 1, row), 5, 0)
        value = jnp.where(sub == 5, right, 0.0)
        value = jnp.where((sub >= 1) & (sub <= 4), middle, value)
        rows.append(jnp.where(sub == 0, left, value))
    return rows


def block_kernel(
    width, rows_out, cols_out, grid_shape,
    own_ref, up_ref, pick_ref, first_ref, second_ref,
    out_ref, band_ref, table_ref, staging_ref, send_sems, recv_sems,
):
    place = (lax.axis_index("strike"), lax.axis_index("dip"))
    present = [
        (place[0] + one >= 0) & (place[0] + one < grid_shape[0]) & (place[1] + two >= 0) & (place[1] + two < grid_shape[1])
        for one, two in DIRECTIONS
    ]
    for slot in range(len(DIRECTIONS)):
        @pl.when(jnp.logical_not(present[slot]))
        def _():
            staging_ref[slot] = jnp.zeros(staging_ref.shape[1:], staging_ref.dtype)

    barrier = pltpu.get_barrier_semaphore()
    for slot, (one, two) in enumerate(DIRECTIONS):
        @pl.when(present[slot])
        def _():
            pl.semaphore_signal(
                barrier, 1, device_id=(place[0] + one, place[1] + two),
                device_id_type=pl.DeviceIdType.MESH,
            )
    count = sum(p.astype(jnp.int32) for p in present)
    pl.semaphore_wait(barrier, count)

    copies = []
    for slot, (one, two) in enumerate(DIRECTIONS):
        far = len(DIRECTIONS) - 1 - slot
        copy = pltpu.make_async_remote_copy(
            src_ref=own_ref, dst_ref=staging_ref.at[far], send_sem=send_sems.at[slot],
            recv_sem=recv_sems.at[far], device_id=(place[0] + one, place[1] + two),
            device_id_type=pl.DeviceIdType.MESH,
        )
        pl.when(present[slot])(copy.start)
        copies.append(copy)

    fill_up(up_ref, table_ref)
    band_ref[...] = jnp.zeros(band_ref.shape, band_ref.dtype)
    fill_band(first_ref, band_ref)

    for slot, (one, two) in enumerate(DIRECTIONS):
        incoming = pltpu.make_async_remote_copy(
            src_ref=own_ref, dst_ref=staging_ref.at[slot], send_sem=send_sems.at[slot],
            recv_sem=recv_sems.at[slot], device_id=(place[0] + one, place[1] + two),
            device_id_type=pl.DeviceIdType.MESH,
        )

        @pl.when(present[slot])
        def _():
            copies[slot].wait_send()
            incoming.wait_recv()

    size_one = own_ref.shape[0]
    ext = halo_rows(own_ref, staging_ref, size_one)
    groups = 4
    channels = table_ref.shape[1] // groups
    lane = lax.broadcasted_iota(jnp.int32, ((size_one + 1) * own_ref.shape[1], 128), 1)
    windows = []
    for high_one in (0, 1):
        for high_two in (0, 1):
            shifted_rows = [
                ext[m + 1 - high_one] if high_two else pltpu.roll(ext[m + 1 - high_one], own_ref.shape[1] - 1, 0)
                for m in range(size_one + 1)
            ]
            rows = jnp.concatenate(shifted_rows, axis=0)
            parts = []
            for g in range(groups):
                rolled = pltpu.roll(rows, (channels - channels * g) % 128, 1)
                keep = lane < 3 * channels
                if g == 0:
                    keep = keep & (lane >= channels)
                if g == groups - 1:
                    keep = keep & (lane < 2 * channels)
                parts.append(jnp.where(keep, rolled, 0.0))
            windows.append(jnp.concatenate(parts, axis=0).astype(jnp.bfloat16))
    rows_in = (size_one + 1) * own_ref.shape[1]
    phases = []
    for phase_one in range(4):
        for phase_two in range(4):
            total = None
            for high_one in (0, 1):
                for high_two in (0, 1):
                    taps = (4 * high_one + phase_one) * 8 + 4 * high_two + phase_two
                    term = jnp.dot(
                        windows[high_one * 2 + high_two], table_ref[taps],
                        preferred_element_type=jnp.float32,
                    )
                    total = term if total is None else total + term
            phases.append(
                jnp.concatenate([total[g * rows_in : (g + 1) * rows_in] for g in range(groups)], axis=1)
            )
    phase_rows = silu(jnp.concatenate(phases, axis=0)).astype(jnp.bfloat16)
    base = jnp.dot(pick_ref[...], phase_rows, preferred_element_type=jnp.float32)
    own = (rows_out, cols_out)
    base = jnp.where(keep_rows(place, grid_shape, own, 0, rows_out + 4, width, 0, cols_out + 4), base, 0.0)
    hidden_count = (rows_out + 2) * width
    first = conv_rows(shifted(base), band_ref, width, hidden_count)
    hidden_keep = keep_rows(place, grid_shape, own, 1, rows_out + 2, width, 1, cols_out + 3)
    hidden = jnp.where(hidden_keep, silu(first), 0.0)
    fill_band(second_ref, band_ref)
    out_count = rows_out * width
    second = conv_rows(shifted(hidden), band_ref, width, out_count)
    summed = base[2 * width : 2 * width + out_count] + second
    summed = pltpu.roll(summed, out_count - 2, 0).reshape(rows_out, width, summed.shape[1])
    out_ref[...] = summed[:, :cols_out].astype(out_ref.dtype)


def picker(rows, cols, width, span):
    place = np.arange(rows * width)
    one, two = place // width, place % width
    source = ((one % 4) * 4 + two % 4) * (rows // 4) * span + (one // 4) * span + two // 4
    chosen = (np.arange(16 * (rows // 4) * span)[None, :] == source[:, None]) & (two < cols)[:, None]
    return chosen.astype(ml_dtypes.bfloat16)


def body(coarse_field, up_weight, first_weight, second_weight):
    channels = up_weight.shape[3]
    coarse_depth = coarse_field.shape[2] // channels
    size_one, size_two = coarse_field.shape[:2]
    own_rows, own_cols = 4 * size_one, 4 * size_two
    lanes = 4 * coarse_depth * channels
    width, span = 32, 8
    own = jnp.pad(coarse_field.astype(jnp.float32), ((0, 0), (0, span - size_two), (0, 0)))
    vmem = pl.BlockSpec(memory_space=pltpu.VMEM)
    grid_shape = (lax.axis_size("strike"), lax.axis_size("dip"))
    return pl.pallas_call(
        lambda *refs: block_kernel(width, own_rows, own_cols, grid_shape, *refs),
        out_shape=jax.ShapeDtypeStruct((own_rows, own_cols, lanes), jnp.bfloat16),
        in_specs=[vmem] * 5,
        out_specs=vmem,
        scratch_shapes=[
            pltpu.VMEM((9, lanes, lanes), jnp.bfloat16),
            pltpu.VMEM((64, 4 * channels, 128), jnp.bfloat16),
            pltpu.VMEM((len(DIRECTIONS),) + own.shape, jnp.float32),
            pltpu.SemaphoreType.DMA((len(DIRECTIONS),)),
            pltpu.SemaphoreType.DMA((len(DIRECTIONS),)),
        ],
        compiler_params=pltpu.CompilerParams(collective_id=0, has_side_effects=True),
    )(
        own,
        up_weight.reshape(-1, channels),
        jnp.asarray(picker(own_rows + 4, own_cols + 4, width, span)),
        first_weight.reshape(-1, channels),
        second_weight.reshape(-1, channels),
    )


def solution(mesh):
    return jax.shard_map(
        body,
        mesh=mesh,
        in_specs=(P("strike", "dip", None), P(), P(), P()),
        out_specs=P("strike", "dip", None),
        check_vma=False,
    )
```

```python
import jax
import jax.numpy as jnp
import ml_dtypes
import numpy as np
from jax import lax
from jax.experimental import pallas as pl
from jax.experimental.pallas import tpu as pltpu
from jax.sharding import PartitionSpec as P

HIGHEST = lax.Precision.HIGHEST


def fill_band(weight_ref, band_ref):
    channels = weight_ref.shape[1]
    taps = weight_ref.shape[0] // (3 * channels)
    cells = band_ref.shape[1] // channels
    lane = lax.broadcasted_iota(jnp.int32, (channels, 128), 1)
    spread_out = (lane % channels == lax.broadcasted_iota(jnp.int32, (channels, 128), 0))
    tiled = jnp.dot(weight_ref[...], spread_out.astype(weight_ref.dtype), preferred_element_type=jnp.float32)
    quarter = lane // channels
    per_group = 128 // channels
    for tap in range(taps):
        for group in range(cells // per_group):
            for cell in range(max(0, per_group * group - 1), min(cells, per_group * group + per_group + 1)):
                block = jnp.zeros((channels, 128), jnp.float32)
                for out_cell in range(per_group):
                    depth = cell - per_group * group - out_cell + 1
                    if 0 <= depth <= 2:
                        row = (tap * 3 + depth) * channels
                        block = jnp.where(quarter == out_cell, tiled[row : row + channels], block)
                band_ref[tap, pl.ds(cell * channels, channels), pl.ds(128 * group, 128)] = block.astype(
                    band_ref.dtype
                )


def shifted(values):
    rows = values.shape[0]
    return (
        pltpu.roll(values, 1, 0).astype(jnp.bfloat16),
        values.astype(jnp.bfloat16),
        pltpu.roll(values, rows - 1, 0).astype(jnp.bfloat16),
    )


def conv_rows(parts, band_ref, width, count):
    lanes = band_ref.shape[1]
    halves = []
    for half in range(lanes // 256):
        low = min(max(256 * half - 128, 0), lanes - 384)
        total = None
        for one in range(3):
            for two in range(3):
                window = parts[two][one * width : one * width + count, low : low + 384]
                term = jnp.dot(
                    window, band_ref[one * 3 + two, low : low + 384, 256 * half : 256 * half + 256],
                    preferred_element_type=jnp.float32,
                )
                total = term if total is None else total + term
        halves.append(total)
    return jnp.concatenate(halves, axis=1)


def keep_rows(place, grid_shape, own, first, count, width, low, high):
    index = lax.broadcasted_iota(jnp.int32, (count * width, 1), 0)
    one = lax.shift_right_logical(index, 5) + first - 2
    two = jnp.bitwise_and(index, 31) - 2
    keep = ((one >= 0) | (place[0] > 0)) & ((one < own[0]) | (place[0] < grid_shape[0] - 1))
    keep = keep & ((two >= 0) | (place[1] > 0)) & ((two < own[1]) | (place[1] < grid_shape[1] - 1))
    return keep & (two + 2 >= low) & (two + 2 < high)


def silu(values):
    return values / (1.0 + jnp.exp(-values))


def fill_up(weight_ref, table_ref):
    channels = weight_ref.shape[1]
    lane = lax.broadcasted_iota(jnp.int32, (channels, 128), 1)
    spread_out = (lane % channels == lax.broadcasted_iota(jnp.int32, (channels, 128), 0))
    spread_out = spread_out.astype(weight_ref.dtype)
    quarter = lane // channels
    per_group = 128 // channels
    span = 8 * channels

    chunk = 8

    def one(step, carry):
        start = pl.multiple_of(step * chunk * span, chunk * span)
        tiled = jnp.dot(
            weight_ref[pl.ds(start, chunk * span)], spread_out, preferred_element_type=jnp.float32
        )
        for part in range(chunk):
            table_ref[step * chunk + part, pl.ds(3 * channels, channels), :] = jnp.zeros(
                (channels, 128), table_ref.dtype
            )
            for cell in range(3):
                block = jnp.zeros((channels, 128), jnp.float32)
                for out_cell in range(per_group):
                    depth = 6 - 4 * cell + out_cell
                    if 0 <= depth < 8:
                        row = part * span + depth * channels
                        block = jnp.where(quarter == out_cell, tiled[row : row + channels], block)
                table_ref[step * chunk + part, pl.ds(cell * channels, channels), :] = block.astype(
                    table_ref.dtype
                )
        return carry

    lax.fori_loop(0, table_ref.shape[0] // chunk, one, 0)


DIRECTIONS = [(-1, -1), (-1, 0), (-1, 1), (0, -1), (0, 1), (1, -1), (1, 0), (1, 1)]


def halo_rows(own_ref, staging_ref, size_one, span):
    sub = lax.broadcasted_iota(jnp.int32, (span, own_ref.shape[2]), 0)

    def block_row(one, two, row):
        if (one, two) == (0, 0):
            values = own_ref[row]
        else:
            values = staging_ref[DIRECTIONS.index((one, two)), row]
        values = values.astype(jnp.float32)
        return jnp.concatenate([values, jnp.zeros((span - values.shape[0], values.shape[1]), jnp.float32)], axis=0)

    rows = []
    for ext in range(size_one + 2):
        one = -1 if ext == 0 else (1 if ext == size_one + 1 else 0)
        row = size_one - 1 if ext == 0 else (0 if ext == size_one + 1 else ext - 1)
        left = pltpu.roll(block_row(one, -1, row), 5, 0)
        middle = pltpu.roll(block_row(one, 0, row), 1, 0)
        right = pltpu.roll(block_row(one, 1, row), 5, 0)
        value = jnp.where(sub == 5, right, 0.0)
        value = jnp.where((sub >= 1) & (sub <= 4), middle, value)
        rows.append(jnp.where(sub == 0, left, value))
    return rows


def block_kernel(
    width, rows_out, cols_out, grid_shape,
    own_ref, up_ref, pick_ref, first_ref, second_ref,
    out_ref, band_ref, table_ref, staging_ref, send_sems, recv_sems,
):
    place = (lax.axis_index("strike"), lax.axis_index("dip"))
    present = [
        (place[0] + one >= 0) & (place[0] + one < grid_shape[0]) & (place[1] + two >= 0) & (place[1] + two < grid_shape[1])
        for one, two in DIRECTIONS
    ]
    for slot in range(len(DIRECTIONS)):
        @pl.when(jnp.logical_not(present[slot]))
        def _():
            staging_ref[slot] = jnp.zeros(staging_ref.shape[1:], staging_ref.dtype)

    barrier = pltpu.get_barrier_semaphore()
    for slot, (one, two) in enumerate(DIRECTIONS):
        @pl.when(present[slot])
        def _():
            pl.semaphore_signal(
                barrier, 1, device_id=(place[0] + one, place[1] + two),
                device_id_type=pl.DeviceIdType.MESH,
            )
    count = sum(p.astype(jnp.int32) for p in present)
    pl.semaphore_wait(barrier, count)

    copies = []
    for slot, (one, two) in enumerate(DIRECTIONS):
        far = len(DIRECTIONS) - 1 - slot
        copy = pltpu.make_async_remote_copy(
            src_ref=own_ref, dst_ref=staging_ref.at[far], send_sem=send_sems.at[slot],
            recv_sem=recv_sems.at[far], device_id=(place[0] + one, place[1] + two),
            device_id_type=pl.DeviceIdType.MESH,
        )
        pl.when(present[slot])(copy.start)
        copies.append(copy)

    fill_up(up_ref, table_ref)
    band_ref[...] = jnp.zeros(band_ref.shape, band_ref.dtype)
    fill_band(first_ref, band_ref)

    for slot, (one, two) in enumerate(DIRECTIONS):
        incoming = pltpu.make_async_remote_copy(
            src_ref=own_ref, dst_ref=staging_ref.at[slot], send_sem=send_sems.at[slot],
            recv_sem=recv_sems.at[slot], device_id=(place[0] + one, place[1] + two),
            device_id_type=pl.DeviceIdType.MESH,
        )

        @pl.when(present[slot])
        def _():
            copies[slot].wait_send()
            incoming.wait_recv()

    size_one = own_ref.shape[0]
    span = 8
    ext = halo_rows(own_ref, staging_ref, size_one, span)
    groups = 4
    channels = table_ref.shape[1] // groups
    lane = lax.broadcasted_iota(jnp.int32, ((size_one + 1) * span, 128), 1)
    windows = []
    for high_one in (0, 1):
        for high_two in (0, 1):
            shifted_rows = [
                ext[m + 1 - high_one] if high_two else pltpu.roll(ext[m + 1 - high_one], span - 1, 0)
                for m in range(size_one + 1)
            ]
            rows = jnp.concatenate(shifted_rows, axis=0)
            parts = []
            for g in range(groups):
                rolled = pltpu.roll(rows, (channels - channels * g) % 128, 1)
                keep = lane < 3 * channels
                if g == 0:
                    keep = keep & (lane >= channels)
                if g == groups - 1:
                    keep = keep & (lane < 2 * channels)
                parts.append(jnp.where(keep, rolled, 0.0))
            windows.append(jnp.concatenate(parts, axis=0).astype(jnp.bfloat16))
    rows_in = (size_one + 1) * span
    phases = []
    for phase_one in range(4):
        for phase_two in range(4):
            total = None
            for high_one in (0, 1):
                for high_two in (0, 1):
                    taps = (4 * high_one + phase_one) * 8 + 4 * high_two + phase_two
                    term = jnp.dot(
                        windows[high_one * 2 + high_two], table_ref[taps],
                        preferred_element_type=jnp.float32,
                    )
                    total = term if total is None else total + term
            phases.append(
                jnp.concatenate([total[g * rows_in : (g + 1) * rows_in] for g in range(groups)], axis=1)
            )
    phase_rows = silu(jnp.concatenate(phases, axis=0)).astype(jnp.bfloat16)
    base = jnp.dot(pick_ref[...], phase_rows, preferred_element_type=jnp.float32)
    own = (rows_out, cols_out)
    base = jnp.where(keep_rows(place, grid_shape, own, 0, rows_out + 4, width, 0, cols_out + 4), base, 0.0)
    hidden_count = (rows_out + 2) * width
    first = conv_rows(shifted(base), band_ref, width, hidden_count)
    hidden_keep = keep_rows(place, grid_shape, own, 1, rows_out + 2, width, 1, cols_out + 3)
    hidden = jnp.where(hidden_keep, silu(first), 0.0)
    fill_band(second_ref, band_ref)
    out_count = rows_out * width
    second = conv_rows(shifted(hidden), band_ref, width, out_count)
    summed = base[2 * width : 2 * width + out_count] + second
    summed = pltpu.roll(summed, out_count - 2, 0).reshape(rows_out, width, summed.shape[1])
    out_ref[...] = summed[:, :cols_out].astype(out_ref.dtype)


def picker(rows, cols, width, span):
    place = np.arange(rows * width)
    one, two = place // width, place % width
    source = ((one % 4) * 4 + two % 4) * (rows // 4) * span + (one // 4) * span + two // 4
    chosen = (np.arange(16 * (rows // 4) * span)[None, :] == source[:, None]) & (two < cols)[:, None]
    return chosen.astype(ml_dtypes.bfloat16)


def body(coarse_field, up_weight, first_weight, second_weight):
    channels = up_weight.shape[3]
    coarse_depth = coarse_field.shape[2] // channels
    size_one, size_two = coarse_field.shape[:2]
    own_rows, own_cols = 4 * size_one, 4 * size_two
    lanes = 4 * coarse_depth * channels
    width, span = 32, 8
    vmem = pl.BlockSpec(memory_space=pltpu.VMEM)
    grid_shape = (lax.axis_size("strike"), lax.axis_size("dip"))
    return pl.pallas_call(
        lambda *refs: block_kernel(width, own_rows, own_cols, grid_shape, *refs),
        out_shape=jax.ShapeDtypeStruct((own_rows, own_cols, lanes), jnp.bfloat16),
        in_specs=[vmem] * 5,
        out_specs=vmem,
        scratch_shapes=[
            pltpu.VMEM((9, lanes, lanes), jnp.bfloat16),
            pltpu.VMEM((64, 4 * channels, 128), jnp.bfloat16),
            pltpu.VMEM((len(DIRECTIONS),) + coarse_field.shape, coarse_field.dtype),
            pltpu.SemaphoreType.DMA((len(DIRECTIONS),)),
            pltpu.SemaphoreType.DMA((len(DIRECTIONS),)),
        ],
        compiler_params=pltpu.CompilerParams(collective_id=0, has_side_effects=True),
    )(
        coarse_field,
        up_weight.reshape(-1, channels),
        jnp.asarray(picker(own_rows + 4, own_cols + 4, width, span)),
        first_weight.reshape(-1, channels),
        second_weight.reshape(-1, channels),
    )


def solution(mesh):
    return jax.shard_map(
        body,
        mesh=mesh,
        in_specs=(P("strike", "dip", None), P(), P(), P()),
        out_specs=P("strike", "dip", None),
        check_vma=False,
    )
```

```python
import jax
import jax.numpy as jnp
import ml_dtypes
import numpy as np
from jax import lax
from jax.experimental import pallas as pl
from jax.experimental.pallas import tpu as pltpu
from jax.sharding import PartitionSpec as P

HIGHEST = lax.Precision.HIGHEST


def fill_band(weight_ref, band_ref):
    channels = weight_ref.shape[1]
    taps = weight_ref.shape[0] // (3 * channels)
    cells = band_ref.shape[1] // channels
    lane = lax.broadcasted_iota(jnp.int32, (channels, 128), 1)
    spread_out = (lane % channels == lax.broadcasted_iota(jnp.int32, (channels, 128), 0))
    tiled = jnp.dot(weight_ref[...], spread_out.astype(weight_ref.dtype), preferred_element_type=jnp.float32)
    quarter = lane // channels
    per_group = 128 // channels
    for tap in range(taps):
        for group in range(cells // per_group):
            for cell in range(max(0, per_group * group - 1), min(cells, per_group * group + per_group + 1)):
                block = jnp.zeros((channels, 128), jnp.float32)
                for out_cell in range(per_group):
                    depth = cell - per_group * group - out_cell + 1
                    if 0 <= depth <= 2:
                        row = (tap * 3 + depth) * channels
                        block = jnp.where(quarter == out_cell, tiled[row : row + channels], block)
                band_ref[tap, pl.ds(cell * channels, channels), pl.ds(128 * group, 128)] = block.astype(
                    band_ref.dtype
                )


def shifted(values):
    rows = values.shape[0]
    return (
        pltpu.roll(values, 1, 0).astype(jnp.bfloat16),
        values.astype(jnp.bfloat16),
        pltpu.roll(values, rows - 1, 0).astype(jnp.bfloat16),
    )


def conv_rows(parts, band_ref, width, count):
    lanes = band_ref.shape[1]
    halves = []
    for half in range(lanes // 256):
        low = min(max(256 * half - 128, 0), lanes - 384)
        total = None
        for one in range(3):
            for two in range(3):
                window = parts[two][one * width : one * width + count, low : low + 384]
                term = jnp.dot(
                    window, band_ref[one * 3 + two, low : low + 384, 256 * half : 256 * half + 256],
                    preferred_element_type=jnp.float32,
                )
                total = term if total is None else total + term
        halves.append(total)
    return jnp.concatenate(halves, axis=1)


def keep_rows(place, grid_shape, own, first, count, width, low, high):
    index = lax.broadcasted_iota(jnp.int32, (count * width, 1), 0)
    one = lax.shift_right_logical(index, 5) + first - 2
    two = jnp.bitwise_and(index, 31) - 2
    keep = ((one >= 0) | (place[0] > 0)) & ((one < own[0]) | (place[0] < grid_shape[0] - 1))
    keep = keep & ((two >= 0) | (place[1] > 0)) & ((two < own[1]) | (place[1] < grid_shape[1] - 1))
    return keep & (two + 2 >= low) & (two + 2 < high)


def silu(values):
    return values / (1.0 + jnp.exp(-values))


def fill_up(weight_ref, table_ref):
    channels = weight_ref.shape[1]
    lane = lax.broadcasted_iota(jnp.int32, (channels, 128), 1)
    spread_out = (lane % channels == lax.broadcasted_iota(jnp.int32, (channels, 128), 0))
    spread_out = spread_out.astype(weight_ref.dtype)
    quarter = lane // channels
    per_group = 128 // channels
    span = 8 * channels

    chunk = 8

    def one(step, carry):
        start = pl.multiple_of(step * chunk * span, chunk * span)
        tiled = jnp.dot(
            weight_ref[pl.ds(start, chunk * span)], spread_out, preferred_element_type=jnp.float32
        )
        for part in range(chunk):
            table_ref[step * chunk + part, pl.ds(3 * channels, channels), :] = jnp.zeros(
                (channels, 128), table_ref.dtype
            )
            for cell in range(3):
                block = jnp.zeros((channels, 128), jnp.float32)
                for out_cell in range(per_group):
                    depth = 6 - 4 * cell + out_cell
                    if 0 <= depth < 8:
                        row = part * span + depth * channels
                        block = jnp.where(quarter == out_cell, tiled[row : row + channels], block)
                table_ref[step * chunk + part, pl.ds(cell * channels, channels), :] = block.astype(
                    table_ref.dtype
                )
        return carry

    lax.fori_loop(0, table_ref.shape[0] // chunk, one, 0)


DIRECTIONS = [(-1, -1), (-1, 0), (-1, 1), (0, -1), (0, 1), (1, -1), (1, 0), (1, 1)]


def halo_rows(own_ref, staging_ref, size_one, span):
    sub = lax.broadcasted_iota(jnp.int32, (span, own_ref.shape[2]), 0)

    def block_row(one, two, row):
        if (one, two) == (0, 0):
            values = own_ref[row]
        else:
            values = staging_ref[DIRECTIONS.index((one, two)), row]
        values = values.astype(jnp.float32)
        return jnp.concatenate([values, jnp.zeros((span - values.shape[0], values.shape[1]), jnp.float32)], axis=0)

    rows = []
    for ext in range(size_one + 2):
        one = -1 if ext == 0 else (1 if ext == size_one + 1 else 0)
        row = size_one - 1 if ext == 0 else (0 if ext == size_one + 1 else ext - 1)
        left = pltpu.roll(block_row(one, -1, row), 5, 0)
        middle = pltpu.roll(block_row(one, 0, row), 1, 0)
        right = pltpu.roll(block_row(one, 1, row), 5, 0)
        value = jnp.where(sub == 5, right, 0.0)
        value = jnp.where((sub >= 1) & (sub <= 4), middle, value)
        rows.append(jnp.where(sub == 0, left, value))
    return rows


def block_kernel(
    width, rows_out, cols_out, grid_shape,
    own_ref, up_ref, pick_ref, first_ref, second_ref,
    out_ref, band_ref, table_ref, staging_ref, send_sems, recv_sems,
):
    place = (lax.axis_index("strike"), lax.axis_index("dip"))
    present = [
        (place[0] + one >= 0) & (place[0] + one < grid_shape[0]) & (place[1] + two >= 0) & (place[1] + two < grid_shape[1])
        for one, two in DIRECTIONS
    ]
    for slot in range(len(DIRECTIONS)):
        @pl.when(jnp.logical_not(present[slot]))
        def _():
            staging_ref[slot] = jnp.zeros(staging_ref.shape[1:], staging_ref.dtype)

    barrier = pltpu.get_barrier_semaphore()
    for slot, (one, two) in enumerate(DIRECTIONS):
        @pl.when(present[slot])
        def _():
            pl.semaphore_signal(
                barrier, 1, device_id=(place[0] + one, place[1] + two),
                device_id_type=pl.DeviceIdType.MESH,
            )
    fill_up(up_ref, table_ref)
    count = sum(p.astype(jnp.int32) for p in present)
    pl.semaphore_wait(barrier, count)

    copies = []
    for slot, (one, two) in enumerate(DIRECTIONS):
        far = len(DIRECTIONS) - 1 - slot
        copy = pltpu.make_async_remote_copy(
            src_ref=own_ref, dst_ref=staging_ref.at[far], send_sem=send_sems.at[slot],
            recv_sem=recv_sems.at[far], device_id=(place[0] + one, place[1] + two),
            device_id_type=pl.DeviceIdType.MESH,
        )
        pl.when(present[slot])(copy.start)
        copies.append(copy)

    band_ref[...] = jnp.zeros(band_ref.shape, band_ref.dtype)
    fill_band(first_ref, band_ref)

    for slot, (one, two) in enumerate(DIRECTIONS):
        incoming = pltpu.make_async_remote_copy(
            src_ref=own_ref, dst_ref=staging_ref.at[slot], send_sem=send_sems.at[slot],
            recv_sem=recv_sems.at[slot], device_id=(place[0] + one, place[1] + two),
            device_id_type=pl.DeviceIdType.MESH,
        )

        @pl.when(present[slot])
        def _():
            copies[slot].wait_send()
            incoming.wait_recv()

    size_one = own_ref.shape[0]
    span = 8
    ext = halo_rows(own_ref, staging_ref, size_one, span)
    groups = 4
    channels = table_ref.shape[1] // groups
    lane = lax.broadcasted_iota(jnp.int32, ((size_one + 1) * span, 128), 1)
    windows = []
    for high_one in (0, 1):
        for high_two in (0, 1):
            shifted_rows = [
                ext[m + 1 - high_one] if high_two else pltpu.roll(ext[m + 1 - high_one], span - 1, 0)
                for m in range(size_one + 1)
            ]
            rows = jnp.concatenate(shifted_rows, axis=0)
            parts = []
            for g in range(groups):
                rolled = pltpu.roll(rows, (channels - channels * g) % 128, 1)
                keep = lane < 3 * channels
                if g == 0:
                    keep = keep & (lane >= channels)
                if g == groups - 1:
                    keep = keep & (lane < 2 * channels)
                parts.append(jnp.where(keep, rolled, 0.0))
            windows.append(jnp.concatenate(parts, axis=0).astype(jnp.bfloat16))
    rows_in = (size_one + 1) * span
    phases = []
    for phase_one in range(4):
        for phase_two in range(4):
            total = None
            for high_one in (0, 1):
                for high_two in (0, 1):
                    taps = (4 * high_one + phase_one) * 8 + 4 * high_two + phase_two
                    term = jnp.dot(
                        windows[high_one * 2 + high_two], table_ref[taps],
                        preferred_element_type=jnp.float32,
                    )
                    total = term if total is None else total + term
            phases.append(
                jnp.concatenate([total[g * rows_in : (g + 1) * rows_in] for g in range(groups)], axis=1)
            )
    phase_rows = silu(jnp.concatenate(phases, axis=0)).astype(jnp.bfloat16)
    base = jnp.dot(pick_ref[...], phase_rows, preferred_element_type=jnp.float32)
    own = (rows_out, cols_out)
    base = jnp.where(keep_rows(place, grid_shape, own, 0, rows_out + 4, width, 0, cols_out + 4), base, 0.0)
    hidden_count = (rows_out + 2) * width
    first = conv_rows(shifted(base), band_ref, width, hidden_count)
    hidden_keep = keep_rows(place, grid_shape, own, 1, rows_out + 2, width, 1, cols_out + 3)
    hidden = jnp.where(hidden_keep, silu(first), 0.0)
    fill_band(second_ref, band_ref)
    out_count = rows_out * width
    second = conv_rows(shifted(hidden), band_ref, width, out_count)
    summed = base[2 * width : 2 * width + out_count] + second
    summed = pltpu.roll(summed, out_count - 2, 0).reshape(rows_out, width, summed.shape[1])
    out_ref[...] = summed[:, :cols_out].astype(out_ref.dtype)


def picker(rows, cols, width, span):
    place = np.arange(rows * width)
    one, two = place // width, place % width
    source = ((one % 4) * 4 + two % 4) * (rows // 4) * span + (one // 4) * span + two // 4
    chosen = (np.arange(16 * (rows // 4) * span)[None, :] == source[:, None]) & (two < cols)[:, None]
    return chosen.astype(ml_dtypes.bfloat16)


def body(coarse_field, up_weight, first_weight, second_weight):
    channels = up_weight.shape[3]
    coarse_depth = coarse_field.shape[2] // channels
    size_one, size_two = coarse_field.shape[:2]
    own_rows, own_cols = 4 * size_one, 4 * size_two
    lanes = 4 * coarse_depth * channels
    width, span = 32, 8
    vmem = pl.BlockSpec(memory_space=pltpu.VMEM)
    grid_shape = (lax.axis_size("strike"), lax.axis_size("dip"))
    return pl.pallas_call(
        lambda *refs: block_kernel(width, own_rows, own_cols, grid_shape, *refs),
        out_shape=jax.ShapeDtypeStruct((own_rows, own_cols, lanes), jnp.bfloat16),
        in_specs=[vmem] * 5,
        out_specs=vmem,
        scratch_shapes=[
            pltpu.VMEM((9, lanes, lanes), jnp.bfloat16),
            pltpu.VMEM((64, 4 * channels, 128), jnp.bfloat16),
            pltpu.VMEM((len(DIRECTIONS),) + coarse_field.shape, coarse_field.dtype),
            pltpu.SemaphoreType.DMA((len(DIRECTIONS),)),
            pltpu.SemaphoreType.DMA((len(DIRECTIONS),)),
        ],
        compiler_params=pltpu.CompilerParams(collective_id=0, has_side_effects=True),
    )(
        coarse_field,
        up_weight.reshape(-1, channels),
        jnp.asarray(picker(own_rows + 4, own_cols + 4, width, span)),
        first_weight.reshape(-1, channels),
        second_weight.reshape(-1, channels),
    )


def solution(mesh):
    return jax.shard_map(
        body,
        mesh=mesh,
        in_specs=(P("strike", "dip", None), P(), P(), P()),
        out_specs=P("strike", "dip", None),
        check_vma=False,
    )
```

```python
import jax
import jax.numpy as jnp
import ml_dtypes
import numpy as np
from jax import lax
from jax.experimental import pallas as pl
from jax.experimental.pallas import tpu as pltpu
from jax.sharding import PartitionSpec as P

HIGHEST = lax.Precision.HIGHEST


def fill_band(weight_ref, band_ref):
    channels = weight_ref.shape[1]
    taps = weight_ref.shape[0] // (3 * channels)
    cells = band_ref.shape[1] // channels
    lane = lax.broadcasted_iota(jnp.int32, (channels, 128), 1)
    spread_out = (lane % channels == lax.broadcasted_iota(jnp.int32, (channels, 128), 0))
    tiled = jnp.dot(weight_ref[...], spread_out.astype(weight_ref.dtype), preferred_element_type=jnp.float32)
    quarter = lane // channels
    per_group = 128 // channels
    for tap in range(taps):
        for group in range(cells // per_group):
            for cell in range(max(0, per_group * group - 1), min(cells, per_group * group + per_group + 1)):
                block = jnp.zeros((channels, 128), jnp.float32)
                for out_cell in range(per_group):
                    depth = cell - per_group * group - out_cell + 1
                    if 0 <= depth <= 2:
                        row = (tap * 3 + depth) * channels
                        block = jnp.where(quarter == out_cell, tiled[row : row + channels], block)
                band_ref[tap, pl.ds(cell * channels, channels), pl.ds(128 * group, 128)] = block.astype(
                    band_ref.dtype
                )


def shifted(values):
    rows = values.shape[0]
    return (
        pltpu.roll(values, 1, 0).astype(jnp.bfloat16),
        values.astype(jnp.bfloat16),
        pltpu.roll(values, rows - 1, 0).astype(jnp.bfloat16),
    )


def conv_rows(parts, band_ref, width, count):
    lanes = band_ref.shape[1]
    halves = []
    for half in range(lanes // 256):
        low = min(max(256 * half - 128, 0), lanes - 384)
        total = None
        for one in range(3):
            for two in range(3):
                window = parts[two][one * width : one * width + count, low : low + 384]
                term = jnp.dot(
                    window, band_ref[one * 3 + two, low : low + 384, 256 * half : 256 * half + 256],
                    preferred_element_type=jnp.float32,
                )
                total = term if total is None else total + term
        halves.append(total)
    return jnp.concatenate(halves, axis=1)


def keep_rows(place, grid_shape, own, first, count, width, low, high):
    index = lax.broadcasted_iota(jnp.int32, (count * width, 1), 0)
    one = lax.shift_right_logical(index, 5) + first - 2
    two = jnp.bitwise_and(index, 31) - 2
    keep = ((one >= 0) | (place[0] > 0)) & ((one < own[0]) | (place[0] < grid_shape[0] - 1))
    keep = keep & ((two >= 0) | (place[1] > 0)) & ((two < own[1]) | (place[1] < grid_shape[1] - 1))
    return keep & (two + 2 >= low) & (two + 2 < high)


def silu(values):
    return values / (1.0 + jnp.exp(-values))


def fill_up(weight_ref, table_ref, source_ref=None, copy_sems=None):
    channels = weight_ref.shape[1]
    lane = lax.broadcasted_iota(jnp.int32, (channels, 128), 1)
    spread_out = (lane % channels == lax.broadcasted_iota(jnp.int32, (channels, 128), 0))
    spread_out = spread_out.astype(weight_ref.dtype)
    quarter = lane // channels
    per_group = 128 // channels
    span = 8 * channels

    chunk = 8

    def one(step, carry):
        start = pl.multiple_of(step * chunk * span, chunk * span)
        if source_ref is not None:
            pltpu.make_async_copy(
                source_ref.at[pl.ds(start, chunk * span)], weight_ref.at[pl.ds(start, chunk * span)],
                copy_sems.at[step],
            ).wait()
        tiled = jnp.dot(
            weight_ref[pl.ds(start, chunk * span)], spread_out, preferred_element_type=jnp.float32
        )
        for part in range(chunk):
            table_ref[step * chunk + part, pl.ds(3 * channels, channels), :] = jnp.zeros(
                (channels, 128), table_ref.dtype
            )
            for cell in range(3):
                block = jnp.zeros((channels, 128), jnp.float32)
                for out_cell in range(per_group):
                    depth = 6 - 4 * cell + out_cell
                    if 0 <= depth < 8:
                        row = part * span + depth * channels
                        block = jnp.where(quarter == out_cell, tiled[row : row + channels], block)
                table_ref[step * chunk + part, pl.ds(cell * channels, channels), :] = block.astype(
                    table_ref.dtype
                )
        return carry

    lax.fori_loop(0, table_ref.shape[0] // chunk, one, 0)


DIRECTIONS = [(-1, -1), (-1, 0), (-1, 1), (0, -1), (0, 1), (1, -1), (1, 0), (1, 1)]


def halo_rows(own_ref, staging_ref, size_one, span):
    sub = lax.broadcasted_iota(jnp.int32, (span, own_ref.shape[2]), 0)

    def block_row(one, two, row):
        if (one, two) == (0, 0):
            values = own_ref[row]
        else:
            values = staging_ref[DIRECTIONS.index((one, two)), row]
        values = values.astype(jnp.float32)
        return jnp.concatenate([values, jnp.zeros((span - values.shape[0], values.shape[1]), jnp.float32)], axis=0)

    rows = []
    for ext in range(size_one + 2):
        one = -1 if ext == 0 else (1 if ext == size_one + 1 else 0)
        row = size_one - 1 if ext == 0 else (0 if ext == size_one + 1 else ext - 1)
        left = pltpu.roll(block_row(one, -1, row), 5, 0)
        middle = pltpu.roll(block_row(one, 0, row), 1, 0)
        right = pltpu.roll(block_row(one, 1, row), 5, 0)
        value = jnp.where(sub == 5, right, 0.0)
        value = jnp.where((sub >= 1) & (sub <= 4), middle, value)
        rows.append(jnp.where(sub == 0, left, value))
    return rows


def block_kernel(
    width, rows_out, cols_out, grid_shape,
    own_ref, up_ref, pick_ref, first_ref, second_ref,
    out_ref, band_ref, table_ref, staging_ref, send_sems, recv_sems, up_vmem, up_sems,
):
    pieces = up_sems.shape[0]
    piece = up_vmem.shape[0] // pieces
    for step in range(pieces):
        pltpu.make_async_copy(
            up_ref.at[pl.ds(step * piece, piece)], up_vmem.at[pl.ds(step * piece, piece)], up_sems.at[step]
        ).start()
    place = (lax.axis_index("strike"), lax.axis_index("dip"))
    present = [
        (place[0] + one >= 0) & (place[0] + one < grid_shape[0]) & (place[1] + two >= 0) & (place[1] + two < grid_shape[1])
        for one, two in DIRECTIONS
    ]
    for slot in range(len(DIRECTIONS)):
        @pl.when(jnp.logical_not(present[slot]))
        def _():
            staging_ref[slot] = jnp.zeros(staging_ref.shape[1:], staging_ref.dtype)

    barrier = pltpu.get_barrier_semaphore()
    for slot, (one, two) in enumerate(DIRECTIONS):
        @pl.when(present[slot])
        def _():
            pl.semaphore_signal(
                barrier, 1, device_id=(place[0] + one, place[1] + two),
                device_id_type=pl.DeviceIdType.MESH,
            )
    band_ref[...] = jnp.zeros(band_ref.shape, band_ref.dtype)
    fill_up(up_vmem, table_ref, up_ref, up_sems)
    count = sum(p.astype(jnp.int32) for p in present)
    pl.semaphore_wait(barrier, count)

    copies = []
    for slot, (one, two) in enumerate(DIRECTIONS):
        far = len(DIRECTIONS) - 1 - slot
        copy = pltpu.make_async_remote_copy(
            src_ref=own_ref, dst_ref=staging_ref.at[far], send_sem=send_sems.at[slot],
            recv_sem=recv_sems.at[far], device_id=(place[0] + one, place[1] + two),
            device_id_type=pl.DeviceIdType.MESH,
        )
        pl.when(present[slot])(copy.start)
        copies.append(copy)

    fill_band(first_ref, band_ref)

    for slot, (one, two) in enumerate(DIRECTIONS):
        incoming = pltpu.make_async_remote_copy(
            src_ref=own_ref, dst_ref=staging_ref.at[slot], send_sem=send_sems.at[slot],
            recv_sem=recv_sems.at[slot], device_id=(place[0] + one, place[1] + two),
            device_id_type=pl.DeviceIdType.MESH,
        )

        @pl.when(present[slot])
        def _():
            copies[slot].wait_send()
            incoming.wait_recv()

    size_one = own_ref.shape[0]
    span = 8
    ext = halo_rows(own_ref, staging_ref, size_one, span)
    groups = 4
    channels = table_ref.shape[1] // groups
    lane = lax.broadcasted_iota(jnp.int32, ((size_one + 1) * span, 128), 1)
    windows = []
    for high_one in (0, 1):
        for high_two in (0, 1):
            shifted_rows = [
                ext[m + 1 - high_one] if high_two else pltpu.roll(ext[m + 1 - high_one], span - 1, 0)
                for m in range(size_one + 1)
            ]
            rows = jnp.concatenate(shifted_rows, axis=0)
            parts = []
            for g in range(groups):
                rolled = pltpu.roll(rows, (channels - channels * g) % 128, 1)
                keep = lane < 3 * channels
                if g == 0:
                    keep = keep & (lane >= channels)
                if g == groups - 1:
                    keep = keep & (lane < 2 * channels)
                parts.append(jnp.where(keep, rolled, 0.0))
            windows.append(jnp.concatenate(parts, axis=0).astype(jnp.bfloat16))
    rows_in = (size_one + 1) * span
    phases = []
    for phase_one in range(4):
        for phase_two in range(4):
            total = None
            for high_one in (0, 1):
                for high_two in (0, 1):
                    taps = (4 * high_one + phase_one) * 8 + 4 * high_two + phase_two
                    term = jnp.dot(
                        windows[high_one * 2 + high_two], table_ref[taps],
                        preferred_element_type=jnp.float32,
                    )
                    total = term if total is None else total + term
            phases.append(
                jnp.concatenate([total[g * rows_in : (g + 1) * rows_in] for g in range(groups)], axis=1)
            )
    phase_rows = silu(jnp.concatenate(phases, axis=0)).astype(jnp.bfloat16)
    base = jnp.dot(pick_ref[...], phase_rows, preferred_element_type=jnp.float32)
    own = (rows_out, cols_out)
    base = jnp.where(keep_rows(place, grid_shape, own, 0, rows_out + 4, width, 0, cols_out + 4), base, 0.0)
    hidden_count = (rows_out + 2) * width
    first = conv_rows(shifted(base), band_ref, width, hidden_count)
    hidden_keep = keep_rows(place, grid_shape, own, 1, rows_out + 2, width, 1, cols_out + 3)
    hidden = jnp.where(hidden_keep, silu(first), 0.0)
    fill_band(second_ref, band_ref)
    out_count = rows_out * width
    second = conv_rows(shifted(hidden), band_ref, width, out_count)
    summed = base[2 * width : 2 * width + out_count] + second
    summed = pltpu.roll(summed, out_count - 2, 0).reshape(rows_out, width, summed.shape[1])
    out_ref[...] = summed[:, :cols_out].astype(out_ref.dtype)


def picker(rows, cols, width, span):
    place = np.arange(rows * width)
    one, two = place // width, place % width
    source = ((one % 4) * 4 + two % 4) * (rows // 4) * span + (one // 4) * span + two // 4
    chosen = (np.arange(16 * (rows // 4) * span)[None, :] == source[:, None]) & (two < cols)[:, None]
    return chosen.astype(ml_dtypes.bfloat16)


def body(coarse_field, up_weight, first_weight, second_weight):
    channels = up_weight.shape[3]
    coarse_depth = coarse_field.shape[2] // channels
    size_one, size_two = coarse_field.shape[:2]
    own_rows, own_cols = 4 * size_one, 4 * size_two
    lanes = 4 * coarse_depth * channels
    width, span = 32, 8
    vmem = pl.BlockSpec(memory_space=pltpu.VMEM)
    grid_shape = (lax.axis_size("strike"), lax.axis_size("dip"))
    return pl.pallas_call(
        lambda *refs: block_kernel(width, own_rows, own_cols, grid_shape, *refs),
        out_shape=jax.ShapeDtypeStruct((own_rows, own_cols, lanes), jnp.bfloat16),
        in_specs=[vmem, pl.BlockSpec(memory_space=pl.ANY)] + [vmem] * 3,
        out_specs=vmem,
        scratch_shapes=[
            pltpu.VMEM((9, lanes, lanes), jnp.bfloat16),
            pltpu.VMEM((64, 4 * channels, 128), jnp.bfloat16),
            pltpu.VMEM((len(DIRECTIONS),) + coarse_field.shape, coarse_field.dtype),
            pltpu.SemaphoreType.DMA((len(DIRECTIONS),)),
            pltpu.SemaphoreType.DMA((len(DIRECTIONS),)),
            pltpu.VMEM((up_weight.size // channels, channels), up_weight.dtype),
            pltpu.SemaphoreType.DMA((8,)),
        ],
        compiler_params=pltpu.CompilerParams(collective_id=0, has_side_effects=True),
    )(
        coarse_field,
        up_weight.reshape(-1, channels),
        jnp.asarray(picker(own_rows + 4, own_cols + 4, width, span)),
        first_weight.reshape(-1, channels),
        second_weight.reshape(-1, channels),
    )


def solution(mesh):
    return jax.shard_map(
        body,
        mesh=mesh,
        in_specs=(P("strike", "dip", None), P(), P(), P()),
        out_specs=P("strike", "dip", None),
        check_vma=False,
    )
```

```python
import jax
import jax.numpy as jnp
import ml_dtypes
import numpy as np
from jax import lax
from jax.experimental import pallas as pl
from jax.experimental.pallas import tpu as pltpu
from jax.sharding import PartitionSpec as P

HIGHEST = lax.Precision.HIGHEST


def fill_band(weight_ref, band_ref):
    channels = weight_ref.shape[1]
    taps = weight_ref.shape[0] // (3 * channels)
    cells = band_ref.shape[1] // channels
    lane = lax.broadcasted_iota(jnp.int32, (channels, 128), 1)
    spread_out = (lane % channels == lax.broadcasted_iota(jnp.int32, (channels, 128), 0))
    tiled = jnp.dot(weight_ref[...], spread_out.astype(weight_ref.dtype), preferred_element_type=jnp.float32)
    quarter = lane // channels
    per_group = 128 // channels
    for tap in range(taps):
        for group in range(cells // per_group):
            for cell in range(max(0, per_group * group - 1), min(cells, per_group * group + per_group + 1)):
                block = jnp.zeros((channels, 128), jnp.float32)
                for out_cell in range(per_group):
                    depth = cell - per_group * group - out_cell + 1
                    if 0 <= depth <= 2:
                        row = (tap * 3 + depth) * channels
                        block = jnp.where(quarter == out_cell, tiled[row : row + channels], block)
                band_ref[tap, pl.ds(cell * channels, channels), pl.ds(128 * group, 128)] = block.astype(
                    band_ref.dtype
                )


def shifted(values):
    rows = values.shape[0]
    return (
        pltpu.roll(values, 1, 0).astype(jnp.bfloat16),
        values.astype(jnp.bfloat16),
        pltpu.roll(values, rows - 1, 0).astype(jnp.bfloat16),
    )


def conv_rows(parts, band_ref, width, count):
    lanes = band_ref.shape[1]
    halves = []
    for half in range(lanes // 256):
        low = min(max(256 * half - 128, 0), lanes - 384)
        total = None
        for one in range(3):
            for two in range(3):
                window = parts[two][one * width : one * width + count, low : low + 384]
                term = jnp.dot(
                    window, band_ref[one * 3 + two, low : low + 384, 256 * half : 256 * half + 256],
                    preferred_element_type=jnp.float32,
                )
                total = term if total is None else total + term
        halves.append(total)
    return jnp.concatenate(halves, axis=1)


def keep_rows(place, grid_shape, own, first, count, width, low, high):
    index = lax.broadcasted_iota(jnp.int32, (count * width, 1), 0)
    one = lax.shift_right_logical(index, 5) + first - 2
    two = jnp.bitwise_and(index, 31) - 2
    keep = ((one >= 0) | (place[0] > 0)) & ((one < own[0]) | (place[0] < grid_shape[0] - 1))
    keep = keep & ((two >= 0) | (place[1] > 0)) & ((two < own[1]) | (place[1] < grid_shape[1] - 1))
    return keep & (two + 2 >= low) & (two + 2 < high)


def silu(values):
    return values / (1.0 + jnp.exp(-values))


def fill_up(weight_ref, table_ref, source_ref=None, copy_sems=None):
    channels = weight_ref.shape[1]
    lane = lax.broadcasted_iota(jnp.int32, (channels, 128), 1)
    spread_out = (lane % channels == lax.broadcasted_iota(jnp.int32, (channels, 128), 0))
    spread_out = spread_out.astype(weight_ref.dtype)
    quarter = lane // channels
    per_group = 128 // channels
    span = 8 * channels

    chunk = 64

    def one(step, carry):
        start = pl.multiple_of(step * chunk * span, chunk * span)
        if source_ref is not None:
            pltpu.make_async_copy(
                source_ref.at[pl.ds(start, chunk * span)], weight_ref.at[pl.ds(start, chunk * span)],
                copy_sems.at[step],
            ).wait()
        tiled = jnp.dot(
            weight_ref[pl.ds(start, chunk * span)], spread_out, preferred_element_type=jnp.float32
        )
        for part in range(chunk):
            table_ref[step * chunk + part, pl.ds(3 * channels, channels), :] = jnp.zeros(
                (channels, 128), table_ref.dtype
            )
            for cell in range(3):
                block = jnp.zeros((channels, 128), jnp.float32)
                for out_cell in range(per_group):
                    depth = 6 - 4 * cell + out_cell
                    if 0 <= depth < 8:
                        row = part * span + depth * channels
                        block = jnp.where(quarter == out_cell, tiled[row : row + channels], block)
                table_ref[step * chunk + part, pl.ds(cell * channels, channels), :] = block.astype(
                    table_ref.dtype
                )
        return carry

    lax.fori_loop(0, table_ref.shape[0] // chunk, one, 0)


DIRECTIONS = [(-1, -1), (-1, 0), (-1, 1), (0, -1), (0, 1), (1, -1), (1, 0), (1, 1)]


def halo_rows(own_ref, staging_ref, size_one, span):
    sub = lax.broadcasted_iota(jnp.int32, (span, own_ref.shape[2]), 0)

    def block_row(one, two, row):
        if (one, two) == (0, 0):
            values = own_ref[row]
        else:
            values = staging_ref[DIRECTIONS.index((one, two)), row]
        values = values.astype(jnp.float32)
        return jnp.concatenate([values, jnp.zeros((span - values.shape[0], values.shape[1]), jnp.float32)], axis=0)

    rows = []
    for ext in range(size_one + 2):
        one = -1 if ext == 0 else (1 if ext == size_one + 1 else 0)
        row = size_one - 1 if ext == 0 else (0 if ext == size_one + 1 else ext - 1)
        left = pltpu.roll(block_row(one, -1, row), 5, 0)
        middle = pltpu.roll(block_row(one, 0, row), 1, 0)
        right = pltpu.roll(block_row(one, 1, row), 5, 0)
        value = jnp.where(sub == 5, right, 0.0)
        value = jnp.where((sub >= 1) & (sub <= 4), middle, value)
        rows.append(jnp.where(sub == 0, left, value))
    return rows


def block_kernel(
    width, rows_out, cols_out, grid_shape,
    own_ref, up_ref, pick_ref, first_ref, second_ref,
    out_ref, band_ref, table_ref, staging_ref, send_sems, recv_sems, up_vmem, up_sems,
):
    pieces = up_sems.shape[0]
    piece = up_vmem.shape[0] // pieces
    for step in range(pieces):
        pltpu.make_async_copy(
            up_ref.at[pl.ds(step * piece, piece)], up_vmem.at[pl.ds(step * piece, piece)], up_sems.at[step]
        ).start()
    place = (lax.axis_index("strike"), lax.axis_index("dip"))
    present = [
        (place[0] + one >= 0) & (place[0] + one < grid_shape[0]) & (place[1] + two >= 0) & (place[1] + two < grid_shape[1])
        for one, two in DIRECTIONS
    ]
    for slot in range(len(DIRECTIONS)):
        @pl.when(jnp.logical_not(present[slot]))
        def _():
            staging_ref[slot] = jnp.zeros(staging_ref.shape[1:], staging_ref.dtype)

    barrier = pltpu.get_barrier_semaphore()
    for slot, (one, two) in enumerate(DIRECTIONS):
        @pl.when(present[slot])
        def _():
            pl.semaphore_signal(
                barrier, 1, device_id=(place[0] + one, place[1] + two),
                device_id_type=pl.DeviceIdType.MESH,
            )
    band_ref[...] = jnp.zeros(band_ref.shape, band_ref.dtype)
    fill_up(up_vmem, table_ref, up_ref, up_sems)
    count = sum(p.astype(jnp.int32) for p in present)
    pl.semaphore_wait(barrier, count)

    copies = []
    for slot, (one, two) in enumerate(DIRECTIONS):
        far = len(DIRECTIONS) - 1 - slot
        copy = pltpu.make_async_remote_copy(
            src_ref=own_ref, dst_ref=staging_ref.at[far], send_sem=send_sems.at[slot],
            recv_sem=recv_sems.at[far], device_id=(place[0] + one, place[1] + two),
            device_id_type=pl.DeviceIdType.MESH,
        )
        pl.when(present[slot])(copy.start)
        copies.append(copy)

    fill_band(first_ref, band_ref)

    for slot, (one, two) in enumerate(DIRECTIONS):
        incoming = pltpu.make_async_remote_copy(
            src_ref=own_ref, dst_ref=staging_ref.at[slot], send_sem=send_sems.at[slot],
            recv_sem=recv_sems.at[slot], device_id=(place[0] + one, place[1] + two),
            device_id_type=pl.DeviceIdType.MESH,
        )

        @pl.when(present[slot])
        def _():
            copies[slot].wait_send()
            incoming.wait_recv()

    size_one = own_ref.shape[0]
    span = 8
    ext = halo_rows(own_ref, staging_ref, size_one, span)
    groups = 4
    channels = table_ref.shape[1] // groups
    lane = lax.broadcasted_iota(jnp.int32, ((size_one + 1) * span, 128), 1)
    windows = []
    for high_one in (0, 1):
        for high_two in (0, 1):
            shifted_rows = [
                ext[m + 1 - high_one] if high_two else pltpu.roll(ext[m + 1 - high_one], span - 1, 0)
                for m in range(size_one + 1)
            ]
            rows = jnp.concatenate(shifted_rows, axis=0)
            parts = []
            for g in range(groups):
                rolled = pltpu.roll(rows, (channels - channels * g) % 128, 1)
                keep = lane < 3 * channels
                if g == 0:
                    keep = keep & (lane >= channels)
                if g == groups - 1:
                    keep = keep & (lane < 2 * channels)
                parts.append(jnp.where(keep, rolled, 0.0))
            windows.append(jnp.concatenate(parts, axis=0).astype(jnp.bfloat16))
    rows_in = (size_one + 1) * span
    phases = []
    for phase_one in range(4):
        for phase_two in range(4):
            total = None
            for high_one in (0, 1):
                for high_two in (0, 1):
                    taps = (4 * high_one + phase_one) * 8 + 4 * high_two + phase_two
                    term = jnp.dot(
                        windows[high_one * 2 + high_two], table_ref[taps],
                        preferred_element_type=jnp.float32,
                    )
                    total = term if total is None else total + term
            phases.append(
                jnp.concatenate([total[g * rows_in : (g + 1) * rows_in] for g in range(groups)], axis=1)
            )
    phase_rows = silu(jnp.concatenate(phases, axis=0)).astype(jnp.bfloat16)
    base = jnp.dot(pick_ref[...], phase_rows, preferred_element_type=jnp.float32)
    own = (rows_out, cols_out)
    base = jnp.where(keep_rows(place, grid_shape, own, 0, rows_out + 4, width, 0, cols_out + 4), base, 0.0)
    hidden_count = (rows_out + 2) * width
    first = conv_rows(shifted(base), band_ref, width, hidden_count)
    hidden_keep = keep_rows(place, grid_shape, own, 1, rows_out + 2, width, 1, cols_out + 3)
    hidden = jnp.where(hidden_keep, silu(first), 0.0)
    fill_band(second_ref, band_ref)
    out_count = rows_out * width
    second = conv_rows(shifted(hidden), band_ref, width, out_count)
    summed = base[2 * width : 2 * width + out_count] + second
    summed = pltpu.roll(summed, out_count - 2, 0).reshape(rows_out, width, summed.shape[1])
    out_ref[...] = summed[:, :cols_out].astype(out_ref.dtype)


def picker(rows, cols, width, span):
    place = np.arange(rows * width)
    one, two = place // width, place % width
    source = ((one % 4) * 4 + two % 4) * (rows // 4) * span + (one // 4) * span + two // 4
    chosen = (np.arange(16 * (rows // 4) * span)[None, :] == source[:, None]) & (two < cols)[:, None]
    return chosen.astype(ml_dtypes.bfloat16)


def body(coarse_field, up_weight, first_weight, second_weight):
    channels = up_weight.shape[3]
    coarse_depth = coarse_field.shape[2] // channels
    size_one, size_two = coarse_field.shape[:2]
    own_rows, own_cols = 4 * size_one, 4 * size_two
    lanes = 4 * coarse_depth * channels
    width, span = 32, 8
    vmem = pl.BlockSpec(memory_space=pltpu.VMEM)
    grid_shape = (lax.axis_size("strike"), lax.axis_size("dip"))
    return pl.pallas_call(
        lambda *refs: block_kernel(width, own_rows, own_cols, grid_shape, *refs),
        out_shape=jax.ShapeDtypeStruct((own_rows, own_cols, lanes), jnp.bfloat16),
        in_specs=[vmem, pl.BlockSpec(memory_space=pl.ANY)] + [vmem] * 3,
        out_specs=vmem,
        scratch_shapes=[
            pltpu.VMEM((9, lanes, lanes), jnp.bfloat16),
            pltpu.VMEM((64, 4 * channels, 128), jnp.bfloat16),
            pltpu.VMEM((len(DIRECTIONS),) + coarse_field.shape, coarse_field.dtype),
            pltpu.SemaphoreType.DMA((len(DIRECTIONS),)),
            pltpu.SemaphoreType.DMA((len(DIRECTIONS),)),
            pltpu.VMEM((up_weight.size // channels, channels), up_weight.dtype),
            pltpu.SemaphoreType.DMA((1,)),
        ],
        compiler_params=pltpu.CompilerParams(collective_id=0, has_side_effects=True),
    )(
        coarse_field,
        up_weight.reshape(-1, channels),
        jnp.asarray(picker(own_rows + 4, own_cols + 4, width, span)),
        first_weight.reshape(-1, channels),
        second_weight.reshape(-1, channels),
    )


def solution(mesh):
    return jax.shard_map(
        body,
        mesh=mesh,
        in_specs=(P("strike", "dip", None), P(), P(), P()),
        out_specs=P("strike", "dip", None),
        check_vma=False,
    )
```

```python
import jax
import jax.numpy as jnp
import ml_dtypes
import numpy as np
from jax import lax
from jax.experimental import pallas as pl
from jax.experimental.pallas import tpu as pltpu
from jax.sharding import PartitionSpec as P

HIGHEST = lax.Precision.HIGHEST


def fill_band(weight_ref, band_ref):
    channels = weight_ref.shape[1]
    taps = weight_ref.shape[0] // (3 * channels)
    cells = band_ref.shape[1] // channels
    lane = lax.broadcasted_iota(jnp.int32, (channels, 128), 1)
    spread_out = (lane % channels == lax.broadcasted_iota(jnp.int32, (channels, 128), 0))
    tiled = jnp.dot(weight_ref[...], spread_out.astype(weight_ref.dtype), preferred_element_type=jnp.float32)
    quarter = lane // channels
    per_group = 128 // channels
    for tap in range(taps):
        for group in range(cells // per_group):
            for cell in range(max(0, per_group * group - 1), min(cells, per_group * group + per_group + 1)):
                block = jnp.zeros((channels, 128), jnp.float32)
                for out_cell in range(per_group):
                    depth = cell - per_group * group - out_cell + 1
                    if 0 <= depth <= 2:
                        row = (tap * 3 + depth) * channels
                        block = jnp.where(quarter == out_cell, tiled[row : row + channels], block)
                band_ref[tap, pl.ds(cell * channels, channels), pl.ds(128 * group, 128)] = block.astype(
                    band_ref.dtype
                )


def shifted(values):
    rows = values.shape[0]
    return (
        pltpu.roll(values, 1, 0).astype(jnp.bfloat16),
        values.astype(jnp.bfloat16),
        pltpu.roll(values, rows - 1, 0).astype(jnp.bfloat16),
    )


def conv_rows(parts, band_ref, width, count):
    lanes = band_ref.shape[1]
    halves = []
    for half in range(lanes // 256):
        low = min(max(256 * half - 128, 0), lanes - 384)
        total = None
        for one in range(3):
            for two in range(3):
                window = parts[two][one * width : one * width + count, low : low + 384]
                term = jnp.dot(
                    window, band_ref[one * 3 + two, low : low + 384, 256 * half : 256 * half + 256],
                    preferred_element_type=jnp.float32,
                )
                total = term if total is None else total + term
        halves.append(total)
    return jnp.concatenate(halves, axis=1)


def keep_rows(place, grid_shape, own, first, count, width, low, high):
    index = lax.broadcasted_iota(jnp.int32, (count * width, 1), 0)
    one = lax.shift_right_logical(index, 5) + first - 2
    two = jnp.bitwise_and(index, 31) - 2
    keep = ((one >= 0) | (place[0] > 0)) & ((one < own[0]) | (place[0] < grid_shape[0] - 1))
    keep = keep & ((two >= 0) | (place[1] > 0)) & ((two < own[1]) | (place[1] < grid_shape[1] - 1))
    return keep & (two + 2 >= low) & (two + 2 < high)


def silu(values):
    return values / (1.0 + jnp.exp(-values))


def fill_up(weight_ref, table_ref, source_ref=None, copy_sems=None):
    channels = weight_ref.shape[1]
    lane = lax.broadcasted_iota(jnp.int32, (channels, 128), 1)
    spread_out = (lane % channels == lax.broadcasted_iota(jnp.int32, (channels, 128), 0))
    spread_out = spread_out.astype(weight_ref.dtype)
    quarter = lane // channels
    per_group = 128 // channels
    span = 8 * channels

    chunk = 16

    def one(step, carry):
        start = pl.multiple_of(step * chunk * span, chunk * span)
        if source_ref is not None:
            pltpu.make_async_copy(
                source_ref.at[pl.ds(start, chunk * span)], weight_ref.at[pl.ds(start, chunk * span)],
                copy_sems.at[step],
            ).wait()
        tiled = jnp.dot(
            weight_ref[pl.ds(start, chunk * span)], spread_out, preferred_element_type=jnp.float32
        )
        for part in range(chunk):
            table_ref[step * chunk + part, pl.ds(3 * channels, channels), :] = jnp.zeros(
                (channels, 128), table_ref.dtype
            )
            for cell in range(3):
                block = jnp.zeros((channels, 128), jnp.float32)
                for out_cell in range(per_group):
                    depth = 6 - 4 * cell + out_cell
                    if 0 <= depth < 8:
                        row = part * span + depth * channels
                        block = jnp.where(quarter == out_cell, tiled[row : row + channels], block)
                table_ref[step * chunk + part, pl.ds(cell * channels, channels), :] = block.astype(
                    table_ref.dtype
                )
        return carry

    lax.fori_loop(0, table_ref.shape[0] // chunk, one, 0)


DIRECTIONS = [(-1, -1), (-1, 0), (-1, 1), (0, -1), (0, 1), (1, -1), (1, 0), (1, 1)]


def halo_rows(own_ref, staging_ref, size_one, span):
    sub = lax.broadcasted_iota(jnp.int32, (span, own_ref.shape[2]), 0)

    def block_row(one, two, row):
        if (one, two) == (0, 0):
            values = own_ref[row]
        else:
            values = staging_ref[DIRECTIONS.index((one, two)), row]
        values = values.astype(jnp.float32)
        return jnp.concatenate([values, jnp.zeros((span - values.shape[0], values.shape[1]), jnp.float32)], axis=0)

    rows = []
    for ext in range(size_one + 2):
        one = -1 if ext == 0 else (1 if ext == size_one + 1 else 0)
        row = size_one - 1 if ext == 0 else (0 if ext == size_one + 1 else ext - 1)
        left = pltpu.roll(block_row(one, -1, row), 5, 0)
        middle = pltpu.roll(block_row(one, 0, row), 1, 0)
        right = pltpu.roll(block_row(one, 1, row), 5, 0)
        value = jnp.where(sub == 5, right, 0.0)
        value = jnp.where((sub >= 1) & (sub <= 4), middle, value)
        rows.append(jnp.where(sub == 0, left, value))
    return rows


def block_kernel(
    width, rows_out, cols_out, grid_shape,
    own_ref, up_ref, pick_ref, first_ref, second_ref,
    out_ref, band_ref, table_ref, staging_ref, send_sems, recv_sems, up_vmem, up_sems,
):
    pieces = up_sems.shape[0]
    piece = up_vmem.shape[0] // pieces
    for step in range(pieces):
        pltpu.make_async_copy(
            up_ref.at[pl.ds(step * piece, piece)], up_vmem.at[pl.ds(step * piece, piece)], up_sems.at[step]
        ).start()
    place = (lax.axis_index("strike"), lax.axis_index("dip"))
    present = [
        (place[0] + one >= 0) & (place[0] + one < grid_shape[0]) & (place[1] + two >= 0) & (place[1] + two < grid_shape[1])
        for one, two in DIRECTIONS
    ]
    for slot in range(len(DIRECTIONS)):
        @pl.when(jnp.logical_not(present[slot]))
        def _():
            staging_ref[slot] = jnp.zeros(staging_ref.shape[1:], staging_ref.dtype)

    barrier = pltpu.get_barrier_semaphore()
    for slot, (one, two) in enumerate(DIRECTIONS):
        @pl.when(present[slot])
        def _():
            pl.semaphore_signal(
                barrier, 1, device_id=(place[0] + one, place[1] + two),
                device_id_type=pl.DeviceIdType.MESH,
            )
    band_ref[...] = jnp.zeros(band_ref.shape, band_ref.dtype)
    fill_up(up_vmem, table_ref, up_ref, up_sems)
    count = sum(p.astype(jnp.int32) for p in present)
    pl.semaphore_wait(barrier, count)

    copies = []
    for slot, (one, two) in enumerate(DIRECTIONS):
        far = len(DIRECTIONS) - 1 - slot
        copy = pltpu.make_async_remote_copy(
            src_ref=own_ref, dst_ref=staging_ref.at[far], send_sem=send_sems.at[slot],
            recv_sem=recv_sems.at[far], device_id=(place[0] + one, place[1] + two),
            device_id_type=pl.DeviceIdType.MESH,
        )
        pl.when(present[slot])(copy.start)
        copies.append(copy)

    fill_band(first_ref, band_ref)

    for slot, (one, two) in enumerate(DIRECTIONS):
        incoming = pltpu.make_async_remote_copy(
            src_ref=own_ref, dst_ref=staging_ref.at[slot], send_sem=send_sems.at[slot],
            recv_sem=recv_sems.at[slot], device_id=(place[0] + one, place[1] + two),
            device_id_type=pl.DeviceIdType.MESH,
        )

        @pl.when(present[slot])
        def _():
            copies[slot].wait_send()
            incoming.wait_recv()

    size_one = own_ref.shape[0]
    span = 8
    ext = halo_rows(own_ref, staging_ref, size_one, span)
    groups = 4
    channels = table_ref.shape[1] // groups
    lane = lax.broadcasted_iota(jnp.int32, ((size_one + 1) * span, 128), 1)
    windows = []
    for high_one in (0, 1):
        for high_two in (0, 1):
            shifted_rows = [
                ext[m + 1 - high_one] if high_two else pltpu.roll(ext[m + 1 - high_one], span - 1, 0)
                for m in range(size_one + 1)
            ]
            rows = jnp.concatenate(shifted_rows, axis=0)
            parts = []
            for g in range(groups):
                rolled = pltpu.roll(rows, (channels - channels * g) % 128, 1)
                keep = lane < 3 * channels
                if g == 0:
                    keep = keep & (lane >= channels)
                if g == groups - 1:
                    keep = keep & (lane < 2 * channels)
                parts.append(jnp.where(keep, rolled, 0.0))
            windows.append(jnp.concatenate(parts, axis=0).astype(jnp.bfloat16))
    rows_in = (size_one + 1) * span
    phases = []
    for phase_one in range(4):
        for phase_two in range(4):
            total = None
            for high_one in (0, 1):
                for high_two in (0, 1):
                    taps = (4 * high_one + phase_one) * 8 + 4 * high_two + phase_two
                    term = jnp.dot(
                        windows[high_one * 2 + high_two], table_ref[taps],
                        preferred_element_type=jnp.float32,
                    )
                    total = term if total is None else total + term
            phases.append(
                jnp.concatenate([total[g * rows_in : (g + 1) * rows_in] for g in range(groups)], axis=1)
            )
    phase_rows = silu(jnp.concatenate(phases, axis=0)).astype(jnp.bfloat16)
    base = jnp.dot(pick_ref[...], phase_rows, preferred_element_type=jnp.float32)
    own = (rows_out, cols_out)
    base = jnp.where(keep_rows(place, grid_shape, own, 0, rows_out + 4, width, 0, cols_out + 4), base, 0.0)
    hidden_count = (rows_out + 2) * width
    first = conv_rows(shifted(base), band_ref, width, hidden_count)
    hidden_keep = keep_rows(place, grid_shape, own, 1, rows_out + 2, width, 1, cols_out + 3)
    hidden = jnp.where(hidden_keep, silu(first), 0.0)
    fill_band(second_ref, band_ref)
    out_count = rows_out * width
    second = conv_rows(shifted(hidden), band_ref, width, out_count)
    summed = base[2 * width : 2 * width + out_count] + second
    summed = pltpu.roll(summed, out_count - 2, 0).reshape(rows_out, width, summed.shape[1])
    out_ref[...] = summed[:, :cols_out].astype(out_ref.dtype)


def picker(rows, cols, width, span):
    place = np.arange(rows * width)
    one, two = place // width, place % width
    source = ((one % 4) * 4 + two % 4) * (rows // 4) * span + (one // 4) * span + two // 4
    chosen = (np.arange(16 * (rows // 4) * span)[None, :] == source[:, None]) & (two < cols)[:, None]
    return chosen.astype(ml_dtypes.bfloat16)


def body(coarse_field, up_weight, first_weight, second_weight):
    channels = up_weight.shape[3]
    coarse_depth = coarse_field.shape[2] // channels
    size_one, size_two = coarse_field.shape[:2]
    own_rows, own_cols = 4 * size_one, 4 * size_two
    lanes = 4 * coarse_depth * channels
    width, span = 32, 8
    vmem = pl.BlockSpec(memory_space=pltpu.VMEM)
    grid_shape = (lax.axis_size("strike"), lax.axis_size("dip"))
    return pl.pallas_call(
        lambda *refs: block_kernel(width, own_rows, own_cols, grid_shape, *refs),
        out_shape=jax.ShapeDtypeStruct((own_rows, own_cols, lanes), jnp.bfloat16),
        in_specs=[vmem, pl.BlockSpec(memory_space=pl.ANY)] + [vmem] * 3,
        out_specs=vmem,
        scratch_shapes=[
            pltpu.VMEM((9, lanes, lanes), jnp.bfloat16),
            pltpu.VMEM((64, 4 * channels, 128), jnp.bfloat16),
            pltpu.VMEM((len(DIRECTIONS),) + coarse_field.shape, coarse_field.dtype),
            pltpu.SemaphoreType.DMA((len(DIRECTIONS),)),
            pltpu.SemaphoreType.DMA((len(DIRECTIONS),)),
            pltpu.VMEM((up_weight.size // channels, channels), up_weight.dtype),
            pltpu.SemaphoreType.DMA((4,)),
        ],
        compiler_params=pltpu.CompilerParams(collective_id=0, has_side_effects=True),
    )(
        coarse_field,
        up_weight.reshape(-1, channels),
        jnp.asarray(picker(own_rows + 4, own_cols + 4, width, span)),
        first_weight.reshape(-1, channels),
        second_weight.reshape(-1, channels),
    )


def solution(mesh):
    return jax.shard_map(
        body,
        mesh=mesh,
        in_specs=(P("strike", "dip", None), P(), P(), P()),
        out_specs=P("strike", "dip", None),
        check_vma=False,
    )
```

```python
import jax
import jax.numpy as jnp
import ml_dtypes
import numpy as np
from jax import lax
from jax.experimental import pallas as pl
from jax.experimental.pallas import tpu as pltpu
from jax.sharding import PartitionSpec as P

HIGHEST = lax.Precision.HIGHEST


def fill_band(weight_ref, band_ref):
    channels = weight_ref.shape[1]
    taps = weight_ref.shape[0] // (3 * channels)
    cells = band_ref.shape[1] // channels
    lane = lax.broadcasted_iota(jnp.int32, (channels, 128), 1)
    spread_out = (lane % channels == lax.broadcasted_iota(jnp.int32, (channels, 128), 0))
    tiled = jnp.dot(weight_ref[...], spread_out.astype(weight_ref.dtype), preferred_element_type=jnp.float32)
    quarter = lane // channels
    per_group = 128 // channels
    for tap in range(taps):
        for group in range(cells // per_group):
            for cell in range(max(0, per_group * group - 1), min(cells, per_group * group + per_group + 1)):
                block = jnp.zeros((channels, 128), jnp.float32)
                for out_cell in range(per_group):
                    depth = cell - per_group * group - out_cell + 1
                    if 0 <= depth <= 2:
                        row = (tap * 3 + depth) * channels
                        block = jnp.where(quarter == out_cell, tiled[row : row + channels], block)
                band_ref[tap, pl.ds(cell * channels, channels), pl.ds(128 * group, 128)] = block.astype(
                    band_ref.dtype
                )


def shifted(values):
    rows = values.shape[0]
    return (
        pltpu.roll(values, 1, 0).astype(jnp.bfloat16),
        values.astype(jnp.bfloat16),
        pltpu.roll(values, rows - 1, 0).astype(jnp.bfloat16),
    )


def conv_rows(parts, band_ref, width, count):
    lanes = band_ref.shape[1]
    halves = []
    for half in range(lanes // 256):
        low = min(max(256 * half - 128, 0), lanes - 384)
        total = None
        for one in range(3):
            for two in range(3):
                window = parts[two][one * width : one * width + count, low : low + 384]
                term = jnp.dot(
                    window, band_ref[one * 3 + two, low : low + 384, 256 * half : 256 * half + 256],
                    preferred_element_type=jnp.float32,
                )
                total = term if total is None else total + term
        halves.append(total)
    return jnp.concatenate(halves, axis=1)


def keep_rows(place, grid_shape, own, first, count, width, low, high):
    index = lax.broadcasted_iota(jnp.int32, (count * width, 1), 0)
    one = lax.shift_right_logical(index, 5) + first - 2
    two = jnp.bitwise_and(index, 31) - 2
    keep = ((one >= 0) | (place[0] > 0)) & ((one < own[0]) | (place[0] < grid_shape[0] - 1))
    keep = keep & ((two >= 0) | (place[1] > 0)) & ((two < own[1]) | (place[1] < grid_shape[1] - 1))
    return keep & (two + 2 >= low) & (two + 2 < high)


def silu(values):
    return 0.5 * values * (1.0 + jnp.tanh(0.5 * values))


def fill_up(weight_ref, table_ref, source_ref=None, copy_sems=None):
    channels = weight_ref.shape[1]
    lane = lax.broadcasted_iota(jnp.int32, (channels, 128), 1)
    spread_out = (lane % channels == lax.broadcasted_iota(jnp.int32, (channels, 128), 0))
    spread_out = spread_out.astype(weight_ref.dtype)
    quarter = lane // channels
    per_group = 128 // channels
    span = 8 * channels

    chunk = 16

    def one(step, carry):
        start = pl.multiple_of(step * chunk * span, chunk * span)
        if source_ref is not None:
            pltpu.make_async_copy(
                source_ref.at[pl.ds(start, chunk * span)], weight_ref.at[pl.ds(start, chunk * span)],
                copy_sems.at[step],
            ).wait()
        tiled = jnp.dot(
            weight_ref[pl.ds(start, chunk * span)], spread_out, preferred_element_type=jnp.float32
        )
        for part in range(chunk):
            table_ref[step * chunk + part, pl.ds(3 * channels, channels), :] = jnp.zeros(
                (channels, 128), table_ref.dtype
            )
            for cell in range(3):
                block = jnp.zeros((channels, 128), jnp.float32)
                for out_cell in range(per_group):
                    depth = 6 - 4 * cell + out_cell
                    if 0 <= depth < 8:
                        row = part * span + depth * channels
                        block = jnp.where(quarter == out_cell, tiled[row : row + channels], block)
                table_ref[step * chunk + part, pl.ds(cell * channels, channels), :] = block.astype(
                    table_ref.dtype
                )
        return carry

    lax.fori_loop(0, table_ref.shape[0] // chunk, one, 0)


DIRECTIONS = [(-1, -1), (-1, 0), (-1, 1), (0, -1), (0, 1), (1, -1), (1, 0), (1, 1)]


def halo_rows(own_ref, staging_ref, size_one, span):
    sub = lax.broadcasted_iota(jnp.int32, (span, own_ref.shape[2]), 0)

    def block_row(one, two, row):
        if (one, two) == (0, 0):
            values = own_ref[row]
        else:
            values = staging_ref[DIRECTIONS.index((one, two)), row]
        values = values.astype(jnp.float32)
        return jnp.concatenate([values, jnp.zeros((span - values.shape[0], values.shape[1]), jnp.float32)], axis=0)

    rows = []
    for ext in range(size_one + 2):
        one = -1 if ext == 0 else (1 if ext == size_one + 1 else 0)
        row = size_one - 1 if ext == 0 else (0 if ext == size_one + 1 else ext - 1)
        left = pltpu.roll(block_row(one, -1, row), 5, 0)
        middle = pltpu.roll(block_row(one, 0, row), 1, 0)
        right = pltpu.roll(block_row(one, 1, row), 5, 0)
        value = jnp.where(sub == 5, right, 0.0)
        value = jnp.where((sub >= 1) & (sub <= 4), middle, value)
        rows.append(jnp.where(sub == 0, left, value))
    return rows


def block_kernel(
    width, rows_out, cols_out, grid_shape,
    own_ref, up_ref, pick_ref, first_ref, second_ref,
    out_ref, band_ref, table_ref, staging_ref, send_sems, recv_sems, up_vmem, up_sems,
):
    pieces = up_sems.shape[0]
    piece = up_vmem.shape[0] // pieces
    for step in range(pieces):
        pltpu.make_async_copy(
            up_ref.at[pl.ds(step * piece, piece)], up_vmem.at[pl.ds(step * piece, piece)], up_sems.at[step]
        ).start()
    place = (lax.axis_index("strike"), lax.axis_index("dip"))
    present = [
        (place[0] + one >= 0) & (place[0] + one < grid_shape[0]) & (place[1] + two >= 0) & (place[1] + two < grid_shape[1])
        for one, two in DIRECTIONS
    ]
    for slot in range(len(DIRECTIONS)):
        @pl.when(jnp.logical_not(present[slot]))
        def _():
            staging_ref[slot] = jnp.zeros(staging_ref.shape[1:], staging_ref.dtype)

    barrier = pltpu.get_barrier_semaphore()
    for slot, (one, two) in enumerate(DIRECTIONS):
        @pl.when(present[slot])
        def _():
            pl.semaphore_signal(
                barrier, 1, device_id=(place[0] + one, place[1] + two),
                device_id_type=pl.DeviceIdType.MESH,
            )
    band_ref[...] = jnp.zeros(band_ref.shape, band_ref.dtype)
    fill_up(up_vmem, table_ref, up_ref, up_sems)
    count = sum(p.astype(jnp.int32) for p in present)
    pl.semaphore_wait(barrier, count)

    copies = []
    for slot, (one, two) in enumerate(DIRECTIONS):
        far = len(DIRECTIONS) - 1 - slot
        copy = pltpu.make_async_remote_copy(
            src_ref=own_ref, dst_ref=staging_ref.at[far], send_sem=send_sems.at[slot],
            recv_sem=recv_sems.at[far], device_id=(place[0] + one, place[1] + two),
            device_id_type=pl.DeviceIdType.MESH,
        )
        pl.when(present[slot])(copy.start)
        copies.append(copy)

    fill_band(first_ref, band_ref)

    for slot, (one, two) in enumerate(DIRECTIONS):
        incoming = pltpu.make_async_remote_copy(
            src_ref=own_ref, dst_ref=staging_ref.at[slot], send_sem=send_sems.at[slot],
            recv_sem=recv_sems.at[slot], device_id=(place[0] + one, place[1] + two),
            device_id_type=pl.DeviceIdType.MESH,
        )

        @pl.when(present[slot])
        def _():
            copies[slot].wait_send()
            incoming.wait_recv()

    size_one = own_ref.shape[0]
    span = 8
    ext = halo_rows(own_ref, staging_ref, size_one, span)
    groups = 4
    channels = table_ref.shape[1] // groups
    lane = lax.broadcasted_iota(jnp.int32, ((size_one + 1) * span, 128), 1)
    windows = []
    for high_one in (0, 1):
        for high_two in (0, 1):
            shifted_rows = [
                ext[m + 1 - high_one] if high_two else pltpu.roll(ext[m + 1 - high_one], span - 1, 0)
                for m in range(size_one + 1)
            ]
            rows = jnp.concatenate(shifted_rows, axis=0)
            parts = []
            for g in range(groups):
                rolled = pltpu.roll(rows, (channels - channels * g) % 128, 1)
                keep = lane < 3 * channels
                if g == 0:
                    keep = keep & (lane >= channels)
                if g == groups - 1:
                    keep = keep & (lane < 2 * channels)
                parts.append(jnp.where(keep, rolled, 0.0))
            windows.append(jnp.concatenate(parts, axis=0).astype(jnp.bfloat16))
    rows_in = (size_one + 1) * span
    phases = []
    for phase_one in range(4):
        for phase_two in range(4):
            total = None
            for high_one in (0, 1):
                for high_two in (0, 1):
                    taps = (4 * high_one + phase_one) * 8 + 4 * high_two + phase_two
                    term = jnp.dot(
                        windows[high_one * 2 + high_two], table_ref[taps],
                        preferred_element_type=jnp.float32,
                    )
                    total = term if total is None else total + term
            phases.append(
                jnp.concatenate([total[g * rows_in : (g + 1) * rows_in] for g in range(groups)], axis=1)
            )
    phase_rows = silu(jnp.concatenate(phases, axis=0)).astype(jnp.bfloat16)
    base = jnp.dot(pick_ref[...], phase_rows, preferred_element_type=jnp.float32)
    own = (rows_out, cols_out)
    base = jnp.where(keep_rows(place, grid_shape, own, 0, rows_out + 4, width, 0, cols_out + 4), base, 0.0)
    hidden_count = (rows_out + 2) * width
    first = conv_rows(shifted(base), band_ref, width, hidden_count)
    hidden_keep = keep_rows(place, grid_shape, own, 1, rows_out + 2, width, 1, cols_out + 3)
    hidden = jnp.where(hidden_keep, silu(first), 0.0)
    fill_band(second_ref, band_ref)
    out_count = rows_out * width
    second = conv_rows(shifted(hidden), band_ref, width, out_count)
    summed = base[2 * width : 2 * width + out_count] + second
    summed = pltpu.roll(summed, out_count - 2, 0).reshape(rows_out, width, summed.shape[1])
    out_ref[...] = summed[:, :cols_out].astype(out_ref.dtype)


def picker(rows, cols, width, span):
    place = np.arange(rows * width)
    one, two = place // width, place % width
    source = ((one % 4) * 4 + two % 4) * (rows // 4) * span + (one // 4) * span + two // 4
    chosen = (np.arange(16 * (rows // 4) * span)[None, :] == source[:, None]) & (two < cols)[:, None]
    return chosen.astype(ml_dtypes.bfloat16)


def body(coarse_field, up_weight, first_weight, second_weight):
    channels = up_weight.shape[3]
    coarse_depth = coarse_field.shape[2] // channels
    size_one, size_two = coarse_field.shape[:2]
    own_rows, own_cols = 4 * size_one, 4 * size_two
    lanes = 4 * coarse_depth * channels
    width, span = 32, 8
    vmem = pl.BlockSpec(memory_space=pltpu.VMEM)
    grid_shape = (lax.axis_size("strike"), lax.axis_size("dip"))
    return pl.pallas_call(
        lambda *refs: block_kernel(width, own_rows, own_cols, grid_shape, *refs),
        out_shape=jax.ShapeDtypeStruct((own_rows, own_cols, lanes), jnp.bfloat16),
        in_specs=[vmem, pl.BlockSpec(memory_space=pl.ANY)] + [vmem] * 3,
        out_specs=vmem,
        scratch_shapes=[
            pltpu.VMEM((9, lanes, lanes), jnp.bfloat16),
            pltpu.VMEM((64, 4 * channels, 128), jnp.bfloat16),
            pltpu.VMEM((len(DIRECTIONS),) + coarse_field.shape, coarse_field.dtype),
            pltpu.SemaphoreType.DMA((len(DIRECTIONS),)),
            pltpu.SemaphoreType.DMA((len(DIRECTIONS),)),
            pltpu.VMEM((up_weight.size // channels, channels), up_weight.dtype),
            pltpu.SemaphoreType.DMA((4,)),
        ],
        compiler_params=pltpu.CompilerParams(collective_id=0, has_side_effects=True),
    )(
        coarse_field,
        up_weight.reshape(-1, channels),
        jnp.asarray(picker(own_rows + 4, own_cols + 4, width, span)),
        first_weight.reshape(-1, channels),
        second_weight.reshape(-1, channels),
    )


def solution(mesh):
    return jax.shard_map(
        body,
        mesh=mesh,
        in_specs=(P("strike", "dip", None), P(), P(), P()),
        out_specs=P("strike", "dip", None),
        check_vma=False,
    )
```

```python
import jax
import jax.numpy as jnp
import ml_dtypes
import numpy as np
from jax import lax
from jax.experimental import pallas as pl
from jax.experimental.pallas import tpu as pltpu
from jax.sharding import PartitionSpec as P

HIGHEST = lax.Precision.HIGHEST


def fill_band(weight_ref, band_ref):
    channels = weight_ref.shape[1]
    taps = weight_ref.shape[0] // (3 * channels)
    cells = band_ref.shape[1] // channels
    lane = lax.broadcasted_iota(jnp.int32, (channels, 128), 1)
    spread_out = (lane % channels == lax.broadcasted_iota(jnp.int32, (channels, 128), 0))
    tiled = jnp.dot(weight_ref[...], spread_out.astype(weight_ref.dtype), preferred_element_type=jnp.float32)
    quarter = lane // channels
    per_group = 128 // channels
    for tap in range(taps):
        for group in range(cells // per_group):
            for cell in range(max(0, per_group * group - 1), min(cells, per_group * group + per_group + 1)):
                block = jnp.zeros((channels, 128), jnp.float32)
                for out_cell in range(per_group):
                    depth = cell - per_group * group - out_cell + 1
                    if 0 <= depth <= 2:
                        row = (tap * 3 + depth) * channels
                        block = jnp.where(quarter == out_cell, tiled[row : row + channels], block)
                band_ref[tap, pl.ds(cell * channels, channels), pl.ds(128 * group, 128)] = block.astype(
                    band_ref.dtype
                )


def shifted(values):
    rows = values.shape[0]
    return (pltpu.roll(values, 1, 0), values, pltpu.roll(values, rows - 1, 0))


def conv_rows(parts, band_ref, width, count):
    lanes = band_ref.shape[1]
    totals = [None] * (lanes // 256)
    for one in range(3):
        for two in range(3):
            window = parts[two][one * width : one * width + count].astype(jnp.bfloat16)
            for half in range(lanes // 256):
                low = min(max(256 * half - 128, 0), lanes - 384)
                term = jnp.dot(
                    window[:, low : low + 384],
                    band_ref[one * 3 + two, low : low + 384, 256 * half : 256 * half + 256],
                    preferred_element_type=jnp.float32,
                )
                totals[half] = term if totals[half] is None else totals[half] + term
    return jnp.concatenate(totals, axis=1)


def keep_rows(place, grid_shape, own, first, count, width, low, high):
    index = lax.broadcasted_iota(jnp.int32, (count * width, 1), 0)
    whole = jnp.floor((index.astype(jnp.float32) + 0.5) / width).astype(jnp.int32)
    one = whole + first - 2
    two = index - whole * width - 2
    keep = ((one >= 0) | (place[0] > 0)) & ((one < own[0]) | (place[0] < grid_shape[0] - 1))
    keep = keep & ((two >= 0) | (place[1] > 0)) & ((two < own[1]) | (place[1] < grid_shape[1] - 1))
    return keep & (two + 2 >= low) & (two + 2 < high)


def silu(values):
    return 0.5 * values * (1.0 + jnp.tanh(0.5 * values))


def fill_up(weight_ref, table_ref, source_ref=None, copy_sems=None):
    channels = weight_ref.shape[1]
    lane = lax.broadcasted_iota(jnp.int32, (channels, 128), 1)
    spread_out = (lane % channels == lax.broadcasted_iota(jnp.int32, (channels, 128), 0))
    spread_out = spread_out.astype(weight_ref.dtype)
    quarter = lane // channels
    per_group = 128 // channels
    span = 8 * channels

    chunk = 16

    def one(step, carry):
        start = pl.multiple_of(step * chunk * span, chunk * span)
        if source_ref is not None:
            pltpu.make_async_copy(
                source_ref.at[pl.ds(start, chunk * span)], weight_ref.at[pl.ds(start, chunk * span)],
                copy_sems.at[step],
            ).wait()
        tiled = jnp.dot(
            weight_ref[pl.ds(start, chunk * span)], spread_out, preferred_element_type=jnp.float32
        )
        for part in range(chunk):
            table_ref[step * chunk + part, pl.ds(3 * channels, channels), :] = jnp.zeros(
                (channels, 128), table_ref.dtype
            )
            for cell in range(3):
                block = jnp.zeros((channels, 128), jnp.float32)
                for out_cell in range(per_group):
                    depth = 6 - 4 * cell + out_cell
                    if 0 <= depth < 8:
                        row = part * span + depth * channels
                        block = jnp.where(quarter == out_cell, tiled[row : row + channels], block)
                table_ref[step * chunk + part, pl.ds(cell * channels, channels), :] = block.astype(
                    table_ref.dtype
                )
        return carry

    lax.fori_loop(0, table_ref.shape[0] // chunk, one, 0)


DIRECTIONS = [(-1, -1), (-1, 0), (-1, 1), (0, -1), (0, 1), (1, -1), (1, 0), (1, 1)]


def halo_rows(own_ref, staging_ref, size_one, span):
    sub = lax.broadcasted_iota(jnp.int32, (span, own_ref.shape[2]), 0)

    def block_row(one, two, row):
        if (one, two) == (0, 0):
            values = own_ref[row]
        else:
            values = staging_ref[DIRECTIONS.index((one, two)), row]
        values = values.astype(jnp.float32)
        return jnp.concatenate([values, jnp.zeros((span - values.shape[0], values.shape[1]), jnp.float32)], axis=0)

    rows = []
    for ext in range(size_one + 2):
        one = -1 if ext == 0 else (1 if ext == size_one + 1 else 0)
        row = size_one - 1 if ext == 0 else (0 if ext == size_one + 1 else ext - 1)
        left = pltpu.roll(block_row(one, -1, row), 5, 0)
        middle = pltpu.roll(block_row(one, 0, row), 1, 0)
        right = pltpu.roll(block_row(one, 1, row), 5, 0)
        value = jnp.where(sub == 5, right, 0.0)
        value = jnp.where((sub >= 1) & (sub <= 4), middle, value)
        rows.append(jnp.where(sub == 0, left, value))
    return rows


def block_kernel(
    width, rows_out, cols_out, grid_shape,
    own_ref, up_ref, pick_ref, first_ref, second_ref,
    out_ref, band_ref, table_ref, staging_ref, send_sems, recv_sems, up_vmem, up_sems,
):
    pieces = up_sems.shape[0]
    piece = up_vmem.shape[0] // pieces
    for step in range(pieces):
        pltpu.make_async_copy(
            up_ref.at[pl.ds(step * piece, piece)], up_vmem.at[pl.ds(step * piece, piece)], up_sems.at[step]
        ).start()
    place = (lax.axis_index("strike"), lax.axis_index("dip"))
    present = [
        (place[0] + one >= 0) & (place[0] + one < grid_shape[0]) & (place[1] + two >= 0) & (place[1] + two < grid_shape[1])
        for one, two in DIRECTIONS
    ]
    for slot in range(len(DIRECTIONS)):
        @pl.when(jnp.logical_not(present[slot]))
        def _():
            staging_ref[slot] = jnp.zeros(staging_ref.shape[1:], staging_ref.dtype)

    barrier = pltpu.get_barrier_semaphore()
    for slot, (one, two) in enumerate(DIRECTIONS):
        @pl.when(present[slot])
        def _():
            pl.semaphore_signal(
                barrier, 1, device_id=(place[0] + one, place[1] + two),
                device_id_type=pl.DeviceIdType.MESH,
            )
    band_ref[...] = jnp.zeros(band_ref.shape, band_ref.dtype)
    fill_up(up_vmem, table_ref, up_ref, up_sems)
    count = sum(p.astype(jnp.int32) for p in present)
    pl.semaphore_wait(barrier, count)

    copies = []
    for slot, (one, two) in enumerate(DIRECTIONS):
        far = len(DIRECTIONS) - 1 - slot
        copy = pltpu.make_async_remote_copy(
            src_ref=own_ref, dst_ref=staging_ref.at[far], send_sem=send_sems.at[slot],
            recv_sem=recv_sems.at[far], device_id=(place[0] + one, place[1] + two),
            device_id_type=pl.DeviceIdType.MESH,
        )
        pl.when(present[slot])(copy.start)
        copies.append(copy)

    fill_band(first_ref, band_ref)

    for slot, (one, two) in enumerate(DIRECTIONS):
        incoming = pltpu.make_async_remote_copy(
            src_ref=own_ref, dst_ref=staging_ref.at[slot], send_sem=send_sems.at[slot],
            recv_sem=recv_sems.at[slot], device_id=(place[0] + one, place[1] + two),
            device_id_type=pl.DeviceIdType.MESH,
        )

        @pl.when(present[slot])
        def _():
            copies[slot].wait_send()
            incoming.wait_recv()

    size_one = own_ref.shape[0]
    span = 8
    ext = halo_rows(own_ref, staging_ref, size_one, span)
    groups = 4
    channels = table_ref.shape[1] // groups
    lane = lax.broadcasted_iota(jnp.int32, ((size_one + 1) * span, 128), 1)
    windows = []
    for high_one in (0, 1):
        for high_two in (0, 1):
            shifted_rows = [
                ext[m + 1 - high_one] if high_two else pltpu.roll(ext[m + 1 - high_one], span - 1, 0)
                for m in range(size_one + 1)
            ]
            rows = jnp.concatenate(shifted_rows, axis=0)
            parts = []
            for g in range(groups):
                rolled = pltpu.roll(rows, (channels - channels * g) % 128, 1)
                keep = lane < 3 * channels
                if g == 0:
                    keep = keep & (lane >= channels)
                if g == groups - 1:
                    keep = keep & (lane < 2 * channels)
                parts.append(jnp.where(keep, rolled, 0.0))
            windows.append(jnp.concatenate(parts, axis=0).astype(jnp.bfloat16))
    rows_in = (size_one + 1) * span
    phases = []
    for phase_one in range(4):
        for phase_two in range(4):
            total = None
            for high_one in (0, 1):
                for high_two in (0, 1):
                    taps = (4 * high_one + phase_one) * 8 + 4 * high_two + phase_two
                    term = jnp.dot(
                        windows[high_one * 2 + high_two], table_ref[taps],
                        preferred_element_type=jnp.float32,
                    )
                    total = term if total is None else total + term
            phases.append(
                jnp.concatenate([total[g * rows_in : (g + 1) * rows_in] for g in range(groups)], axis=1)
            )
    phase_rows = silu(jnp.concatenate(phases, axis=0)).astype(jnp.bfloat16)
    base = jnp.dot(pick_ref[...], phase_rows, preferred_element_type=jnp.float32)
    own = (rows_out, cols_out)
    base = jnp.where(keep_rows(place, grid_shape, own, 0, rows_out + 4, width, 0, cols_out + 4), base, 0.0)
    hidden_count = (rows_out + 2) * width
    first = conv_rows(shifted(base), band_ref, width, hidden_count)
    hidden_keep = keep_rows(place, grid_shape, own, 1, rows_out + 2, width, 1, cols_out + 3)
    hidden = jnp.where(hidden_keep, silu(first), 0.0)
    fill_band(second_ref, band_ref)
    out_count = rows_out * width
    second = conv_rows(shifted(hidden), band_ref, width, out_count)
    summed = base[2 * width : 2 * width + out_count] + second
    summed = pltpu.roll(summed, out_count - 2, 0).reshape(rows_out, width, summed.shape[1])
    out_ref[...] = summed[:, :cols_out].astype(out_ref.dtype)


def picker(rows, cols, width, span):
    place = np.arange(rows * width)
    one, two = place // width, place % width
    source = ((one % 4) * 4 + two % 4) * (rows // 4) * span + (one // 4) * span + two // 4
    chosen = (np.arange(16 * (rows // 4) * span)[None, :] == source[:, None]) & (two < cols)[:, None]
    return chosen.astype(ml_dtypes.bfloat16)


def body(coarse_field, up_weight, first_weight, second_weight):
    channels = up_weight.shape[3]
    coarse_depth = coarse_field.shape[2] // channels
    size_one, size_two = coarse_field.shape[:2]
    own_rows, own_cols = 4 * size_one, 4 * size_two
    lanes = 4 * coarse_depth * channels
    width, span = 24, 8
    vmem = pl.BlockSpec(memory_space=pltpu.VMEM)
    grid_shape = (lax.axis_size("strike"), lax.axis_size("dip"))
    return pl.pallas_call(
        lambda *refs: block_kernel(width, own_rows, own_cols, grid_shape, *refs),
        out_shape=jax.ShapeDtypeStruct((own_rows, own_cols, lanes), jnp.bfloat16),
        in_specs=[vmem, pl.BlockSpec(memory_space=pl.ANY)] + [vmem] * 3,
        out_specs=vmem,
        scratch_shapes=[
            pltpu.VMEM((9, lanes, lanes), jnp.bfloat16),
            pltpu.VMEM((64, 4 * channels, 128), jnp.bfloat16),
            pltpu.VMEM((len(DIRECTIONS),) + coarse_field.shape, coarse_field.dtype),
            pltpu.SemaphoreType.DMA((len(DIRECTIONS),)),
            pltpu.SemaphoreType.DMA((len(DIRECTIONS),)),
            pltpu.VMEM((up_weight.size // channels, channels), up_weight.dtype),
            pltpu.SemaphoreType.DMA((4,)),
        ],
        compiler_params=pltpu.CompilerParams(collective_id=0, has_side_effects=True),
    )(
        coarse_field,
        up_weight.reshape(-1, channels),
        jnp.asarray(picker(own_rows + 4, own_cols + 4, width, span)),
        first_weight.reshape(-1, channels),
        second_weight.reshape(-1, channels),
    )


def solution(mesh):
    return jax.shard_map(
        body,
        mesh=mesh,
        in_specs=(P("strike", "dip", None), P(), P(), P()),
        out_specs=P("strike", "dip", None),
        check_vma=False,
    )
```

```python
import jax
import jax.numpy as jnp
import ml_dtypes
import numpy as np
from jax import lax
from jax.experimental import pallas as pl
from jax.experimental.pallas import tpu as pltpu
from jax.sharding import PartitionSpec as P

HIGHEST = lax.Precision.HIGHEST


def fill_band(weight_ref, band_ref):
    channels = weight_ref.shape[1]
    taps = weight_ref.shape[0] // (3 * channels)
    cells = band_ref.shape[1] // channels
    lane = lax.broadcasted_iota(jnp.int32, (channels, 128), 1)
    spread_out = (lane % channels == lax.broadcasted_iota(jnp.int32, (channels, 128), 0))
    tiled = jnp.dot(weight_ref[...], spread_out.astype(weight_ref.dtype), preferred_element_type=jnp.float32)
    quarter = lane // channels
    per_group = 128 // channels
    for tap in range(taps):
        for group in range(cells // per_group):
            for cell in range(max(0, per_group * group - 1), min(cells, per_group * group + per_group + 1)):
                block = jnp.zeros((channels, 128), jnp.float32)
                for out_cell in range(per_group):
                    depth = cell - per_group * group - out_cell + 1
                    if 0 <= depth <= 2:
                        row = (tap * 3 + depth) * channels
                        block = jnp.where(quarter == out_cell, tiled[row : row + channels], block)
                band_ref[tap, pl.ds(cell * channels, channels), pl.ds(128 * group, 128)] = block.astype(
                    band_ref.dtype
                )


def shifted(values):
    rows = values.shape[0]
    return (pltpu.roll(values, 1, 0), values, pltpu.roll(values, rows - 1, 0))


def conv_rows(parts, band_ref, width, count):
    lanes = band_ref.shape[1]
    totals = [None] * (lanes // 256)
    narrow = [part.astype(jnp.bfloat16) for part in parts]
    for one in range(3):
        for two in range(3):
            if (one * width) % 16 == 0:
                window = narrow[two][one * width : one * width + count]
            else:
                window = parts[two][one * width : one * width + count].astype(jnp.bfloat16)
            for half in range(lanes // 256):
                low = min(max(256 * half - 128, 0), lanes - 384)
                term = jnp.dot(
                    window[:, low : low + 384],
                    band_ref[one * 3 + two, low : low + 384, 256 * half : 256 * half + 256],
                    preferred_element_type=jnp.float32,
                )
                totals[half] = term if totals[half] is None else totals[half] + term
    return jnp.concatenate(totals, axis=1)


def keep_rows(place, grid_shape, own, first, count, width, low, high):
    index = lax.broadcasted_iota(jnp.int32, (count * width, 1), 0)
    whole = jnp.floor((index.astype(jnp.float32) + 0.5) / width).astype(jnp.int32)
    one = whole + first - 2
    two = index - whole * width - 2
    keep = ((one >= 0) | (place[0] > 0)) & ((one < own[0]) | (place[0] < grid_shape[0] - 1))
    keep = keep & ((two >= 0) | (place[1] > 0)) & ((two < own[1]) | (place[1] < grid_shape[1] - 1))
    return keep & (two + 2 >= low) & (two + 2 < high)


def silu(values):
    return 0.5 * values * (1.0 + jnp.tanh(0.5 * values))


def fill_up(weight_ref, table_ref, source_ref=None, copy_sems=None):
    channels = weight_ref.shape[1]
    lane = lax.broadcasted_iota(jnp.int32, (channels, 128), 1)
    spread_out = (lane % channels == lax.broadcasted_iota(jnp.int32, (channels, 128), 0))
    spread_out = spread_out.astype(weight_ref.dtype)
    quarter = lane // channels
    per_group = 128 // channels
    span = 8 * channels

    chunk = 16

    def one(step, carry):
        start = pl.multiple_of(step * chunk * span, chunk * span)
        if source_ref is not None:
            pltpu.make_async_copy(
                source_ref.at[pl.ds(start, chunk * span)], weight_ref.at[pl.ds(start, chunk * span)],
                copy_sems.at[step],
            ).wait()
        tiled = jnp.dot(
            weight_ref[pl.ds(start, chunk * span)], spread_out, preferred_element_type=jnp.float32
        )
        for part in range(chunk):
            table_ref[step * chunk + part, pl.ds(3 * channels, channels), :] = jnp.zeros(
                (channels, 128), table_ref.dtype
            )
            for cell in range(3):
                block = jnp.zeros((channels, 128), jnp.float32)
                for out_cell in range(per_group):
                    depth = 6 - 4 * cell + out_cell
                    if 0 <= depth < 8:
                        row = part * span + depth * channels
                        block = jnp.where(quarter == out_cell, tiled[row : row + channels], block)
                table_ref[step * chunk + part, pl.ds(cell * channels, channels), :] = block.astype(
                    table_ref.dtype
                )
        return carry

    lax.fori_loop(0, table_ref.shape[0] // chunk, one, 0)


DIRECTIONS = [(-1, -1), (-1, 0), (-1, 1), (0, -1), (0, 1), (1, -1), (1, 0), (1, 1)]


def halo_rows(own_ref, staging_ref, size_one, span):
    sub = lax.broadcasted_iota(jnp.int32, (span, own_ref.shape[2]), 0)

    def block_row(one, two, row):
        if (one, two) == (0, 0):
            values = own_ref[row]
        else:
            values = staging_ref[DIRECTIONS.index((one, two)), row]
        values = values.astype(jnp.float32)
        return jnp.concatenate([values, jnp.zeros((span - values.shape[0], values.shape[1]), jnp.float32)], axis=0)

    rows = []
    for ext in range(size_one + 2):
        one = -1 if ext == 0 else (1 if ext == size_one + 1 else 0)
        row = size_one - 1 if ext == 0 else (0 if ext == size_one + 1 else ext - 1)
        left = pltpu.roll(block_row(one, -1, row), 5, 0)
        middle = pltpu.roll(block_row(one, 0, row), 1, 0)
        right = pltpu.roll(block_row(one, 1, row), 5, 0)
        value = jnp.where(sub == 5, right, 0.0)
        value = jnp.where((sub >= 1) & (sub <= 4), middle, value)
        rows.append(jnp.where(sub == 0, left, value))
    return rows


def block_kernel(
    width, rows_out, cols_out, grid_shape,
    own_ref, up_ref, pick_ref, first_ref, second_ref,
    out_ref, band_ref, table_ref, staging_ref, send_sems, recv_sems, up_vmem, up_sems,
):
    pieces = up_sems.shape[0]
    piece = up_vmem.shape[0] // pieces
    for step in range(pieces):
        pltpu.make_async_copy(
            up_ref.at[pl.ds(step * piece, piece)], up_vmem.at[pl.ds(step * piece, piece)], up_sems.at[step]
        ).start()
    place = (lax.axis_index("strike"), lax.axis_index("dip"))
    present = [
        (place[0] + one >= 0) & (place[0] + one < grid_shape[0]) & (place[1] + two >= 0) & (place[1] + two < grid_shape[1])
        for one, two in DIRECTIONS
    ]
    for slot in range(len(DIRECTIONS)):
        @pl.when(jnp.logical_not(present[slot]))
        def _():
            staging_ref[slot] = jnp.zeros(staging_ref.shape[1:], staging_ref.dtype)

    barrier = pltpu.get_barrier_semaphore()
    for slot, (one, two) in enumerate(DIRECTIONS):
        @pl.when(present[slot])
        def _():
            pl.semaphore_signal(
                barrier, 1, device_id=(place[0] + one, place[1] + two),
                device_id_type=pl.DeviceIdType.MESH,
            )
    band_ref[...] = jnp.zeros(band_ref.shape, band_ref.dtype)
    fill_up(up_vmem, table_ref, up_ref, up_sems)
    count = sum(p.astype(jnp.int32) for p in present)
    pl.semaphore_wait(barrier, count)

    copies = []
    for slot, (one, two) in enumerate(DIRECTIONS):
        far = len(DIRECTIONS) - 1 - slot
        copy = pltpu.make_async_remote_copy(
            src_ref=own_ref, dst_ref=staging_ref.at[far], send_sem=send_sems.at[slot],
            recv_sem=recv_sems.at[far], device_id=(place[0] + one, place[1] + two),
            device_id_type=pl.DeviceIdType.MESH,
        )
        pl.when(present[slot])(copy.start)
        copies.append(copy)

    fill_band(first_ref, band_ref)

    for slot, (one, two) in enumerate(DIRECTIONS):
        incoming = pltpu.make_async_remote_copy(
            src_ref=own_ref, dst_ref=staging_ref.at[slot], send_sem=send_sems.at[slot],
            recv_sem=recv_sems.at[slot], device_id=(place[0] + one, place[1] + two),
            device_id_type=pl.DeviceIdType.MESH,
        )

        @pl.when(present[slot])
        def _():
            copies[slot].wait_send()
            incoming.wait_recv()

    size_one = own_ref.shape[0]
    span = 8
    ext = halo_rows(own_ref, staging_ref, size_one, span)
    groups = 4
    channels = table_ref.shape[1] // groups
    lane = lax.broadcasted_iota(jnp.int32, ((size_one + 1) * span, 128), 1)
    windows = []
    for high_one in (0, 1):
        for high_two in (0, 1):
            shifted_rows = [
                ext[m + 1 - high_one] if high_two else pltpu.roll(ext[m + 1 - high_one], span - 1, 0)
                for m in range(size_one + 1)
            ]
            rows = jnp.concatenate(shifted_rows, axis=0)
            parts = []
            for g in range(groups):
                rolled = pltpu.roll(rows, (channels - channels * g) % 128, 1)
                keep = lane < 3 * channels
                if g == 0:
                    keep = keep & (lane >= channels)
                if g == groups - 1:
                    keep = keep & (lane < 2 * channels)
                parts.append(jnp.where(keep, rolled, 0.0))
            windows.append(jnp.concatenate(parts, axis=0).astype(jnp.bfloat16))
    rows_in = (size_one + 1) * span
    phases = []
    for phase_one in range(4):
        for phase_two in range(4):
            total = None
            for high_one in (0, 1):
                for high_two in (0, 1):
                    taps = (4 * high_one + phase_one) * 8 + 4 * high_two + phase_two
                    term = jnp.dot(
                        windows[high_one * 2 + high_two], table_ref[taps],
                        preferred_element_type=jnp.float32,
                    )
                    total = term if total is None else total + term
            phases.append(
                jnp.concatenate([total[g * rows_in : (g + 1) * rows_in] for g in range(groups)], axis=1)
            )
    phase_rows = silu(jnp.concatenate(phases, axis=0)).astype(jnp.bfloat16)
    base = jnp.dot(pick_ref[...], phase_rows, preferred_element_type=jnp.float32)
    own = (rows_out, cols_out)
    base = jnp.where(keep_rows(place, grid_shape, own, 0, rows_out + 4, width, 0, cols_out + 4), base, 0.0)
    hidden_count = (rows_out + 2) * width
    first = conv_rows(shifted(base), band_ref, width, hidden_count)
    hidden_keep = keep_rows(place, grid_shape, own, 1, rows_out + 2, width, 1, cols_out + 3)
    hidden = jnp.where(hidden_keep, silu(first), 0.0)
    fill_band(second_ref, band_ref)
    out_count = rows_out * width
    second = conv_rows(shifted(hidden), band_ref, width, out_count)
    summed = base[2 * width : 2 * width + out_count] + second
    summed = pltpu.roll(summed, out_count - 2, 0).reshape(rows_out, width, summed.shape[1])
    out_ref[...] = summed[:, :cols_out].astype(out_ref.dtype)


def picker(rows, cols, width, span):
    place = np.arange(rows * width)
    one, two = place // width, place % width
    source = ((one % 4) * 4 + two % 4) * (rows // 4) * span + (one // 4) * span + two // 4
    chosen = (np.arange(16 * (rows // 4) * span)[None, :] == source[:, None]) & (two < cols)[:, None]
    return chosen.astype(ml_dtypes.bfloat16)


def body(coarse_field, up_weight, first_weight, second_weight):
    channels = up_weight.shape[3]
    coarse_depth = coarse_field.shape[2] // channels
    size_one, size_two = coarse_field.shape[:2]
    own_rows, own_cols = 4 * size_one, 4 * size_two
    lanes = 4 * coarse_depth * channels
    width, span = 24, 8
    vmem = pl.BlockSpec(memory_space=pltpu.VMEM)
    grid_shape = (lax.axis_size("strike"), lax.axis_size("dip"))
    return pl.pallas_call(
        lambda *refs: block_kernel(width, own_rows, own_cols, grid_shape, *refs),
        out_shape=jax.ShapeDtypeStruct((own_rows, own_cols, lanes), jnp.bfloat16),
        in_specs=[vmem, pl.BlockSpec(memory_space=pl.ANY)] + [vmem] * 3,
        out_specs=vmem,
        scratch_shapes=[
            pltpu.VMEM((9, lanes, lanes), jnp.bfloat16),
            pltpu.VMEM((64, 4 * channels, 128), jnp.bfloat16),
            pltpu.VMEM((len(DIRECTIONS),) + coarse_field.shape, coarse_field.dtype),
            pltpu.SemaphoreType.DMA((len(DIRECTIONS),)),
            pltpu.SemaphoreType.DMA((len(DIRECTIONS),)),
            pltpu.VMEM((up_weight.size // channels, channels), up_weight.dtype),
            pltpu.SemaphoreType.DMA((4,)),
        ],
        compiler_params=pltpu.CompilerParams(collective_id=0, has_side_effects=True),
    )(
        coarse_field,
        up_weight.reshape(-1, channels),
        jnp.asarray(picker(own_rows + 4, own_cols + 4, width, span)),
        first_weight.reshape(-1, channels),
        second_weight.reshape(-1, channels),
    )


def solution(mesh):
    return jax.shard_map(
        body,
        mesh=mesh,
        in_specs=(P("strike", "dip", None), P(), P(), P()),
        out_specs=P("strike", "dip", None),
        check_vma=False,
    )
```

```python
import jax
import jax.numpy as jnp
import ml_dtypes
import numpy as np
from jax import lax
from jax.experimental import pallas as pl
from jax.experimental.pallas import tpu as pltpu
from jax.sharding import PartitionSpec as P

HIGHEST = lax.Precision.HIGHEST


def fill_band(weight_ref, band_ref):
    channels = weight_ref.shape[1]
    taps = weight_ref.shape[0] // (3 * channels)
    cells = band_ref.shape[1] // channels
    lane = lax.broadcasted_iota(jnp.int32, (channels, 128), 1)
    spread_out = (lane % channels == lax.broadcasted_iota(jnp.int32, (channels, 128), 0))
    tiled = jnp.dot(weight_ref[...], spread_out.astype(weight_ref.dtype), preferred_element_type=jnp.float32)
    quarter = lane // channels
    per_group = 128 // channels
    for tap in range(taps):
        for group in range(cells // per_group):
            for cell in range(max(0, per_group * group - 1), min(cells, per_group * group + per_group + 1)):
                block = jnp.zeros((channels, 128), jnp.float32)
                for out_cell in range(per_group):
                    depth = cell - per_group * group - out_cell + 1
                    if 0 <= depth <= 2:
                        row = (tap * 3 + depth) * channels
                        block = jnp.where(quarter == out_cell, tiled[row : row + channels], block)
                band_ref[tap, pl.ds(cell * channels, channels), pl.ds(128 * group, 128)] = block.astype(
                    band_ref.dtype
                )


def zero_band(band_ref, channels):
    cells = band_ref.shape[1] // channels
    per_group = 128 // channels
    for group in range(band_ref.shape[2] // 128):
        low, high = (0, cells - per_group) if group < 2 else (per_group, cells)
        written = range(max(0, per_group * group - 1), min(cells, per_group * group + per_group + 1))
        for cell in range(low, high):
            if cell not in written:
                band_ref[:, pl.ds(cell * channels, channels), pl.ds(128 * group, 128)] = jnp.zeros(
                    (band_ref.shape[0], channels, 128), band_ref.dtype
                )


def shifted(values):
    rows = values.shape[0]
    return (pltpu.roll(values, 1, 0), values, pltpu.roll(values, rows - 1, 0))


def conv_rows(parts, band_ref, width, count):
    lanes = band_ref.shape[1]
    totals = [None] * (lanes // 256)
    for one in range(3):
        for two in range(3):
            window = parts[two][one * width : one * width + count].astype(jnp.bfloat16)
            for half in range(lanes // 256):
                low = min(max(256 * half - 128, 0), lanes - 384)
                term = jnp.dot(
                    window[:, low : low + 384],
                    band_ref[one * 3 + two, low : low + 384, 256 * half : 256 * half + 256],
                    preferred_element_type=jnp.float32,
                )
                totals[half] = term if totals[half] is None else totals[half] + term
    return jnp.concatenate(totals, axis=1)


def keep_rows(place, grid_shape, own, first, count, width, low, high):
    index = lax.broadcasted_iota(jnp.int32, (count * width, 1), 0)
    whole = jnp.floor((index.astype(jnp.float32) + 0.5) / width).astype(jnp.int32)
    one = whole + first - 2
    two = index - whole * width - 2
    keep = ((one >= 0) | (place[0] > 0)) & ((one < own[0]) | (place[0] < grid_shape[0] - 1))
    keep = keep & ((two >= 0) | (place[1] > 0)) & ((two < own[1]) | (place[1] < grid_shape[1] - 1))
    return keep & (two + 2 >= low) & (two + 2 < high)


def silu(values):
    return 0.5 * values * (1.0 + jnp.tanh(0.5 * values))


def fill_up(weight_ref, table_ref, source_ref=None, copy_sems=None):
    channels = weight_ref.shape[1]
    lane = lax.broadcasted_iota(jnp.int32, (channels, 128), 1)
    spread_out = (lane % channels == lax.broadcasted_iota(jnp.int32, (channels, 128), 0))
    spread_out = spread_out.astype(weight_ref.dtype)
    quarter = lane // channels
    per_group = 128 // channels
    span = 8 * channels

    chunk = 16

    def one(step, carry):
        start = pl.multiple_of(step * chunk * span, chunk * span)
        if source_ref is not None:
            pltpu.make_async_copy(
                source_ref.at[pl.ds(start, chunk * span)], weight_ref.at[pl.ds(start, chunk * span)],
                copy_sems.at[step],
            ).wait()
        tiled = jnp.dot(
            weight_ref[pl.ds(start, chunk * span)], spread_out, preferred_element_type=jnp.float32
        )
        for part in range(chunk):
            table_ref[step * chunk + part, pl.ds(3 * channels, channels), :] = jnp.zeros(
                (channels, 128), table_ref.dtype
            )
            for cell in range(3):
                block = jnp.zeros((channels, 128), jnp.float32)
                for out_cell in range(per_group):
                    depth = 6 - 4 * cell + out_cell
                    if 0 <= depth < 8:
                        row = part * span + depth * channels
                        block = jnp.where(quarter == out_cell, tiled[row : row + channels], block)
                table_ref[step * chunk + part, pl.ds(cell * channels, channels), :] = block.astype(
                    table_ref.dtype
                )
        return carry

    lax.fori_loop(0, table_ref.shape[0] // chunk, one, 0)


DIRECTIONS = [(-1, -1), (-1, 0), (-1, 1), (0, -1), (0, 1), (1, -1), (1, 0), (1, 1)]


def halo_rows(own_ref, staging_ref, size_one, span):
    sub = lax.broadcasted_iota(jnp.int32, (span, own_ref.shape[2]), 0)

    def block_row(one, two, row):
        if (one, two) == (0, 0):
            values = own_ref[row]
        else:
            values = staging_ref[DIRECTIONS.index((one, two)), row]
        values = values.astype(jnp.float32)
        return jnp.concatenate([values, jnp.zeros((span - values.shape[0], values.shape[1]), jnp.float32)], axis=0)

    rows = []
    for ext in range(size_one + 2):
        one = -1 if ext == 0 else (1 if ext == size_one + 1 else 0)
        row = size_one - 1 if ext == 0 else (0 if ext == size_one + 1 else ext - 1)
        left = pltpu.roll(block_row(one, -1, row), 5, 0)
        middle = pltpu.roll(block_row(one, 0, row), 1, 0)
        right = pltpu.roll(block_row(one, 1, row), 5, 0)
        value = jnp.where(sub == 5, right, 0.0)
        value = jnp.where((sub >= 1) & (sub <= 4), middle, value)
        rows.append(jnp.where(sub == 0, left, value))
    return rows


def block_kernel(
    width, rows_out, cols_out, grid_shape,
    own_ref, up_ref, pick_ref, first_ref, second_ref,
    out_ref, band_ref, table_ref, staging_ref, send_sems, recv_sems, up_vmem, up_sems,
):
    pieces = up_sems.shape[0]
    piece = up_vmem.shape[0] // pieces
    for step in range(pieces):
        pltpu.make_async_copy(
            up_ref.at[pl.ds(step * piece, piece)], up_vmem.at[pl.ds(step * piece, piece)], up_sems.at[step]
        ).start()
    place = (lax.axis_index("strike"), lax.axis_index("dip"))
    present = [
        (place[0] + one >= 0) & (place[0] + one < grid_shape[0]) & (place[1] + two >= 0) & (place[1] + two < grid_shape[1])
        for one, two in DIRECTIONS
    ]
    for slot in range(len(DIRECTIONS)):
        @pl.when(jnp.logical_not(present[slot]))
        def _():
            staging_ref[slot] = jnp.zeros(staging_ref.shape[1:], staging_ref.dtype)

    barrier = pltpu.get_barrier_semaphore()
    for slot, (one, two) in enumerate(DIRECTIONS):
        @pl.when(present[slot])
        def _():
            pl.semaphore_signal(
                barrier, 1, device_id=(place[0] + one, place[1] + two),
                device_id_type=pl.DeviceIdType.MESH,
            )
    zero_band(band_ref, 32)
    fill_up(up_vmem, table_ref, up_ref, up_sems)
    count = sum(p.astype(jnp.int32) for p in present)
    pl.semaphore_wait(barrier, count)

    copies = []
    for slot, (one, two) in enumerate(DIRECTIONS):
        far = len(DIRECTIONS) - 1 - slot
        copy = pltpu.make_async_remote_copy(
            src_ref=own_ref, dst_ref=staging_ref.at[far], send_sem=send_sems.at[slot],
            recv_sem=recv_sems.at[far], device_id=(place[0] + one, place[1] + two),
            device_id_type=pl.DeviceIdType.MESH,
        )
        pl.when(present[slot])(copy.start)
        copies.append(copy)

    fill_band(first_ref, band_ref)

    for slot, (one, two) in enumerate(DIRECTIONS):
        incoming = pltpu.make_async_remote_copy(
            src_ref=own_ref, dst_ref=staging_ref.at[slot], send_sem=send_sems.at[slot],
            recv_sem=recv_sems.at[slot], device_id=(place[0] + one, place[1] + two),
            device_id_type=pl.DeviceIdType.MESH,
        )

        @pl.when(present[slot])
        def _():
            copies[slot].wait_send()
            incoming.wait_recv()

    size_one = own_ref.shape[0]
    span = 8
    ext = halo_rows(own_ref, staging_ref, size_one, span)
    groups = 4
    channels = table_ref.shape[1] // groups
    lane = lax.broadcasted_iota(jnp.int32, ((size_one + 1) * span, 128), 1)
    windows = []
    for high_one in (0, 1):
        for high_two in (0, 1):
            shifted_rows = [
                ext[m + 1 - high_one] if high_two else pltpu.roll(ext[m + 1 - high_one], span - 1, 0)
                for m in range(size_one + 1)
            ]
            rows = jnp.concatenate(shifted_rows, axis=0)
            parts = []
            for g in range(groups):
                rolled = pltpu.roll(rows, (channels - channels * g) % 128, 1)
                keep = lane < 3 * channels
                if g == 0:
                    keep = keep & (lane >= channels)
                if g == groups - 1:
                    keep = keep & (lane < 2 * channels)
                parts.append(jnp.where(keep, rolled, 0.0))
            windows.append(jnp.concatenate(parts, axis=0).astype(jnp.bfloat16))
    rows_in = (size_one + 1) * span
    phases = []
    for phase_one in range(4):
        for phase_two in range(4):
            total = None
            for high_one in (0, 1):
                for high_two in (0, 1):
                    taps = (4 * high_one + phase_one) * 8 + 4 * high_two + phase_two
                    term = jnp.dot(
                        windows[high_one * 2 + high_two], table_ref[taps],
                        preferred_element_type=jnp.float32,
                    )
                    total = term if total is None else total + term
            phases.append(
                jnp.concatenate([total[g * rows_in : (g + 1) * rows_in] for g in range(groups)], axis=1)
            )
    phase_rows = silu(jnp.concatenate(phases, axis=0)).astype(jnp.bfloat16)
    base = jnp.dot(pick_ref[...], phase_rows, preferred_element_type=jnp.float32)
    own = (rows_out, cols_out)
    base = jnp.where(keep_rows(place, grid_shape, own, 0, rows_out + 4, width, 0, cols_out + 4), base, 0.0)
    hidden_count = (rows_out + 2) * width
    first = conv_rows(shifted(base), band_ref, width, hidden_count)
    hidden_keep = keep_rows(place, grid_shape, own, 1, rows_out + 2, width, 1, cols_out + 3)
    hidden = jnp.where(hidden_keep, silu(first), 0.0)
    fill_band(second_ref, band_ref)
    out_count = rows_out * width
    second = conv_rows(shifted(hidden), band_ref, width, out_count)
    summed = base[2 * width : 2 * width + out_count] + second
    summed = pltpu.roll(summed, out_count - 2, 0).reshape(rows_out, width, summed.shape[1])
    out_ref[...] = summed[:, :cols_out].astype(out_ref.dtype)


def picker(rows, cols, width, span):
    place = np.arange(rows * width)
    one, two = place // width, place % width
    source = ((one % 4) * 4 + two % 4) * (rows // 4) * span + (one // 4) * span + two // 4
    chosen = (np.arange(16 * (rows // 4) * span)[None, :] == source[:, None]) & (two < cols)[:, None]
    return chosen.astype(ml_dtypes.bfloat16)


def body(coarse_field, up_weight, first_weight, second_weight):
    channels = up_weight.shape[3]
    coarse_depth = coarse_field.shape[2] // channels
    size_one, size_two = coarse_field.shape[:2]
    own_rows, own_cols = 4 * size_one, 4 * size_two
    lanes = 4 * coarse_depth * channels
    width, span = 24, 8
    vmem = pl.BlockSpec(memory_space=pltpu.VMEM)
    grid_shape = (lax.axis_size("strike"), lax.axis_size("dip"))
    return pl.pallas_call(
        lambda *refs: block_kernel(width, own_rows, own_cols, grid_shape, *refs),
        out_shape=jax.ShapeDtypeStruct((own_rows, own_cols, lanes), jnp.bfloat16),
        in_specs=[vmem, pl.BlockSpec(memory_space=pl.ANY)] + [vmem] * 3,
        out_specs=vmem,
        scratch_shapes=[
            pltpu.VMEM((9, lanes, lanes), jnp.bfloat16),
            pltpu.VMEM((64, 4 * channels, 128), jnp.bfloat16),
            pltpu.VMEM((len(DIRECTIONS),) + coarse_field.shape, coarse_field.dtype),
            pltpu.SemaphoreType.DMA((len(DIRECTIONS),)),
            pltpu.SemaphoreType.DMA((len(DIRECTIONS),)),
            pltpu.VMEM((up_weight.size // channels, channels), up_weight.dtype),
            pltpu.SemaphoreType.DMA((4,)),
        ],
        compiler_params=pltpu.CompilerParams(collective_id=0, has_side_effects=True),
    )(
        coarse_field,
        up_weight.reshape(-1, channels),
        jnp.asarray(picker(own_rows + 4, own_cols + 4, width, span)),
        first_weight.reshape(-1, channels),
        second_weight.reshape(-1, channels),
    )


def solution(mesh):
    return jax.shard_map(
        body,
        mesh=mesh,
        in_specs=(P("strike", "dip", None), P(), P(), P()),
        out_specs=P("strike", "dip", None),
        check_vma=False,
    )
```

```python
import jax
import jax.numpy as jnp
import ml_dtypes
import numpy as np
from jax import lax
from jax.experimental import pallas as pl
from jax.experimental.pallas import tpu as pltpu
from jax.sharding import PartitionSpec as P

HIGHEST = lax.Precision.HIGHEST


def fill_band(weight_ref, band_ref):
    channels = weight_ref.shape[1]
    taps = weight_ref.shape[0] // (3 * channels)
    cells = band_ref.shape[1] // channels
    lane = lax.broadcasted_iota(jnp.int32, (channels, 128), 1)
    spread_out = (lane % channels == lax.broadcasted_iota(jnp.int32, (channels, 128), 0))
    tiled = jnp.dot(weight_ref[...], spread_out.astype(weight_ref.dtype), preferred_element_type=jnp.float32)
    quarter = lane // channels
    per_group = 128 // channels
    for tap in range(taps):
        for group in range(cells // per_group):
            for cell in range(max(0, per_group * group - 1), min(cells, per_group * group + per_group + 1)):
                block = jnp.zeros((channels, 128), jnp.float32)
                for out_cell in range(per_group):
                    depth = cell - per_group * group - out_cell + 1
                    if 0 <= depth <= 2:
                        row = (tap * 3 + depth) * channels
                        block = jnp.where(quarter == out_cell, tiled[row : row + channels], block)
                band_ref[tap, pl.ds(cell * channels, channels), pl.ds(128 * group, 128)] = block.astype(
                    band_ref.dtype
                )


def shifted(values):
    rows = values.shape[0]
    return (pltpu.roll(values, 1, 0), values, pltpu.roll(values, rows - 1, 0))


def conv_rows(parts, band_ref, width, count):
    lanes = band_ref.shape[1]
    totals = [None] * (lanes // 256)
    for one in range(3):
        for two in range(3):
            window = parts[two][one * width : one * width + count].astype(jnp.bfloat16)
            for half in range(lanes // 256):
                low = min(max(256 * half - 128, 0), lanes - 384)
                term = jnp.dot(
                    window[:, low : low + 384],
                    band_ref[one * 3 + two, low : low + 384, 256 * half : 256 * half + 256],
                    preferred_element_type=jnp.float32,
                )
                totals[half] = term if totals[half] is None else totals[half] + term
    return jnp.concatenate(totals, axis=1)


def keep_rows(place, grid_shape, own, first, count, width, low, high):
    index = lax.broadcasted_iota(jnp.int32, (count * width, 1), 0)
    whole = jnp.floor((index.astype(jnp.float32) + 0.5) / width).astype(jnp.int32)
    one = whole + first - 2
    two = index - whole * width - 2
    keep = ((one >= 0) | (place[0] > 0)) & ((one < own[0]) | (place[0] < grid_shape[0] - 1))
    keep = keep & ((two >= 0) | (place[1] > 0)) & ((two < own[1]) | (place[1] < grid_shape[1] - 1))
    return keep & (two + 2 >= low) & (two + 2 < high)


def silu(values):
    return 0.5 * values * (1.0 + jnp.tanh(0.5 * values))


def fill_up(weight_ref, table_ref, source_ref=None, copy_sems=None):
    channels = weight_ref.shape[1]
    lane = lax.broadcasted_iota(jnp.int32, (channels, 128), 1)
    spread_out = (lane % channels == lax.broadcasted_iota(jnp.int32, (channels, 128), 0))
    spread_out = spread_out.astype(weight_ref.dtype)
    quarter = lane // channels
    per_group = 128 // channels
    span = 8 * channels

    chunk = 16

    def one(step, carry):
        start = pl.multiple_of(step * chunk * span, chunk * span)
        if source_ref is not None:
            pltpu.make_async_copy(
                source_ref.at[pl.ds(start, chunk * span)], weight_ref.at[pl.ds(start, chunk * span)],
                copy_sems.at[step],
            ).wait()
        tiled = jnp.dot(
            weight_ref[pl.ds(start, chunk * span)], spread_out, preferred_element_type=jnp.float32
        )
        for part in range(chunk):
            taps = step * chunk + part
            one, two = taps // 8, taps % 8
            phase = (one % 4) * 4 + two % 4
            first_row = ((one // 4) * 2 + two // 4) * 4 * channels
            table_ref[phase, pl.ds(pl.multiple_of(first_row + 3 * channels, channels), channels), :] = jnp.zeros(
                (channels, 128), table_ref.dtype
            )
            for cell in range(3):
                block = jnp.zeros((channels, 128), jnp.float32)
                for out_cell in range(per_group):
                    depth = 6 - 4 * cell + out_cell
                    if 0 <= depth < 8:
                        row = part * span + depth * channels
                        block = jnp.where(quarter == out_cell, tiled[row : row + channels], block)
                table_ref[phase, pl.ds(pl.multiple_of(first_row + cell * channels, channels), channels), :] = block.astype(
                    table_ref.dtype
                )
        return carry

    lax.fori_loop(0, weight_ref.shape[0] // span // chunk, one, 0)


DIRECTIONS = [(-1, -1), (-1, 0), (-1, 1), (0, -1), (0, 1), (1, -1), (1, 0), (1, 1)]


def halo_rows(own_ref, staging_ref, size_one, span):
    sub = lax.broadcasted_iota(jnp.int32, (span, own_ref.shape[2]), 0)

    def block_row(one, two, row):
        if (one, two) == (0, 0):
            values = own_ref[row]
        else:
            values = staging_ref[DIRECTIONS.index((one, two)), row]
        values = values.astype(jnp.float32)
        return jnp.concatenate([values, jnp.zeros((span - values.shape[0], values.shape[1]), jnp.float32)], axis=0)

    rows = []
    for ext in range(size_one + 2):
        one = -1 if ext == 0 else (1 if ext == size_one + 1 else 0)
        row = size_one - 1 if ext == 0 else (0 if ext == size_one + 1 else ext - 1)
        left = pltpu.roll(block_row(one, -1, row), 5, 0)
        middle = pltpu.roll(block_row(one, 0, row), 1, 0)
        right = pltpu.roll(block_row(one, 1, row), 5, 0)
        value = jnp.where(sub == 5, right, 0.0)
        value = jnp.where((sub >= 1) & (sub <= 4), middle, value)
        rows.append(jnp.where(sub == 0, left, value))
    return rows


def block_kernel(
    width, rows_out, cols_out, grid_shape,
    own_ref, up_ref, pick_ref, first_ref, second_ref,
    out_ref, band_ref, table_ref, staging_ref, send_sems, recv_sems, up_vmem, up_sems,
):
    pieces = up_sems.shape[0]
    piece = up_vmem.shape[0] // pieces
    for step in range(pieces):
        pltpu.make_async_copy(
            up_ref.at[pl.ds(step * piece, piece)], up_vmem.at[pl.ds(step * piece, piece)], up_sems.at[step]
        ).start()
    place = (lax.axis_index("strike"), lax.axis_index("dip"))
    present = [
        (place[0] + one >= 0) & (place[0] + one < grid_shape[0]) & (place[1] + two >= 0) & (place[1] + two < grid_shape[1])
        for one, two in DIRECTIONS
    ]
    for slot in range(len(DIRECTIONS)):
        @pl.when(jnp.logical_not(present[slot]))
        def _():
            staging_ref[slot] = jnp.zeros(staging_ref.shape[1:], staging_ref.dtype)

    barrier = pltpu.get_barrier_semaphore()
    for slot, (one, two) in enumerate(DIRECTIONS):
        @pl.when(present[slot])
        def _():
            pl.semaphore_signal(
                barrier, 1, device_id=(place[0] + one, place[1] + two),
                device_id_type=pl.DeviceIdType.MESH,
            )
    band_ref[...] = jnp.zeros(band_ref.shape, band_ref.dtype)
    fill_up(up_vmem, table_ref, up_ref, up_sems)
    count = sum(p.astype(jnp.int32) for p in present)
    pl.semaphore_wait(barrier, count)

    copies = []
    for slot, (one, two) in enumerate(DIRECTIONS):
        far = len(DIRECTIONS) - 1 - slot
        copy = pltpu.make_async_remote_copy(
            src_ref=own_ref, dst_ref=staging_ref.at[far], send_sem=send_sems.at[slot],
            recv_sem=recv_sems.at[far], device_id=(place[0] + one, place[1] + two),
            device_id_type=pl.DeviceIdType.MESH,
        )
        pl.when(present[slot])(copy.start)
        copies.append(copy)

    fill_band(first_ref, band_ref)

    for slot, (one, two) in enumerate(DIRECTIONS):
        incoming = pltpu.make_async_remote_copy(
            src_ref=own_ref, dst_ref=staging_ref.at[slot], send_sem=send_sems.at[slot],
            recv_sem=recv_sems.at[slot], device_id=(place[0] + one, place[1] + two),
            device_id_type=pl.DeviceIdType.MESH,
        )

        @pl.when(present[slot])
        def _():
            copies[slot].wait_send()
            incoming.wait_recv()

    size_one = own_ref.shape[0]
    span = 8
    ext = halo_rows(own_ref, staging_ref, size_one, span)
    groups = 4
    channels = table_ref.shape[1] // (4 * groups)
    lane = lax.broadcasted_iota(jnp.int32, ((size_one + 1) * span, 128), 1)
    windows = []
    for high_one in (0, 1):
        for high_two in (0, 1):
            shifted_rows = [
                ext[m + 1 - high_one] if high_two else pltpu.roll(ext[m + 1 - high_one], span - 1, 0)
                for m in range(size_one + 1)
            ]
            rows = jnp.concatenate(shifted_rows, axis=0)
            parts = []
            for g in range(groups):
                rolled = pltpu.roll(rows, (channels - channels * g) % 128, 1)
                keep = lane < 3 * channels
                if g == 0:
                    keep = keep & (lane >= channels)
                if g == groups - 1:
                    keep = keep & (lane < 2 * channels)
                parts.append(jnp.where(keep, rolled, 0.0))
            windows.append(jnp.concatenate(parts, axis=0).astype(jnp.bfloat16))
    rows_in = (size_one + 1) * span
    stacked = jnp.concatenate(windows, axis=1)
    phases = []
    for phase_one in range(4):
        for phase_two in range(4):
            total = jnp.dot(stacked, table_ref[phase_one * 4 + phase_two], preferred_element_type=jnp.float32)
            phases.append(
                jnp.concatenate([total[g * rows_in : (g + 1) * rows_in] for g in range(groups)], axis=1)
            )
    phase_rows = silu(jnp.concatenate(phases, axis=0)).astype(jnp.bfloat16)
    base = jnp.dot(pick_ref[...], phase_rows, preferred_element_type=jnp.float32)
    own = (rows_out, cols_out)
    base = jnp.where(keep_rows(place, grid_shape, own, 0, rows_out + 4, width, 0, cols_out + 4), base, 0.0)
    hidden_count = (rows_out + 2) * width
    first = conv_rows(shifted(base), band_ref, width, hidden_count)
    hidden_keep = keep_rows(place, grid_shape, own, 1, rows_out + 2, width, 1, cols_out + 3)
    hidden = jnp.where(hidden_keep, silu(first), 0.0)
    fill_band(second_ref, band_ref)
    out_count = rows_out * width
    second = conv_rows(shifted(hidden), band_ref, width, out_count)
    summed = base[2 * width : 2 * width + out_count] + second
    summed = pltpu.roll(summed, out_count - 2, 0).reshape(rows_out, width, summed.shape[1])
    out_ref[...] = summed[:, :cols_out].astype(out_ref.dtype)


def picker(rows, cols, width, span):
    place = np.arange(rows * width)
    one, two = place // width, place % width
    source = ((one % 4) * 4 + two % 4) * (rows // 4) * span + (one // 4) * span + two // 4
    chosen = (np.arange(16 * (rows // 4) * span)[None, :] == source[:, None]) & (two < cols)[:, None]
    return chosen.astype(ml_dtypes.bfloat16)


def body(coarse_field, up_weight, first_weight, second_weight):
    channels = up_weight.shape[3]
    coarse_depth = coarse_field.shape[2] // channels
    size_one, size_two = coarse_field.shape[:2]
    own_rows, own_cols = 4 * size_one, 4 * size_two
    lanes = 4 * coarse_depth * channels
    width, span = 24, 8
    vmem = pl.BlockSpec(memory_space=pltpu.VMEM)
    grid_shape = (lax.axis_size("strike"), lax.axis_size("dip"))
    return pl.pallas_call(
        lambda *refs: block_kernel(width, own_rows, own_cols, grid_shape, *refs),
        out_shape=jax.ShapeDtypeStruct((own_rows, own_cols, lanes), jnp.bfloat16),
        in_specs=[vmem, pl.BlockSpec(memory_space=pl.ANY)] + [vmem] * 3,
        out_specs=vmem,
        scratch_shapes=[
            pltpu.VMEM((9, lanes, lanes), jnp.bfloat16),
            pltpu.VMEM((16, 16 * channels, 128), jnp.bfloat16),
            pltpu.VMEM((len(DIRECTIONS),) + coarse_field.shape, coarse_field.dtype),
            pltpu.SemaphoreType.DMA((len(DIRECTIONS),)),
            pltpu.SemaphoreType.DMA((len(DIRECTIONS),)),
            pltpu.VMEM((up_weight.size // channels, channels), up_weight.dtype),
            pltpu.SemaphoreType.DMA((4,)),
        ],
        compiler_params=pltpu.CompilerParams(collective_id=0, has_side_effects=True),
    )(
        coarse_field,
        up_weight.reshape(-1, channels),
        jnp.asarray(picker(own_rows + 4, own_cols + 4, width, span)),
        first_weight.reshape(-1, channels),
        second_weight.reshape(-1, channels),
    )


def solution(mesh):
    return jax.shard_map(
        body,
        mesh=mesh,
        in_specs=(P("strike", "dip", None), P(), P(), P()),
        out_specs=P("strike", "dip", None),
        check_vma=False,
    )
```

```python
import jax
import jax.numpy as jnp
import ml_dtypes
import numpy as np
from jax import lax
from jax.experimental import pallas as pl
from jax.experimental.pallas import tpu as pltpu
from jax.sharding import PartitionSpec as P

HIGHEST = lax.Precision.HIGHEST


def fill_band(weight_ref, band_ref):
    channels = weight_ref.shape[1]
    taps = weight_ref.shape[0] // (3 * channels)
    cells = band_ref.shape[1] // channels
    lane = lax.broadcasted_iota(jnp.int32, (channels, 128), 1)
    spread_out = (lane % channels == lax.broadcasted_iota(jnp.int32, (channels, 128), 0))
    tiled = jnp.dot(weight_ref[...], spread_out.astype(weight_ref.dtype), preferred_element_type=jnp.float32)
    quarter = lane // channels
    per_group = 128 // channels
    for tap in range(taps):
        for group in range(cells // per_group):
            for cell in range(max(0, per_group * group - 1), min(cells, per_group * group + per_group + 1)):
                block = jnp.zeros((channels, 128), jnp.float32)
                for out_cell in range(per_group):
                    depth = cell - per_group * group - out_cell + 1
                    if 0 <= depth <= 2:
                        row = (tap * 3 + depth) * channels
                        block = jnp.where(quarter == out_cell, tiled[row : row + channels], block)
                band_ref[tap, pl.ds(cell * channels, channels), pl.ds(128 * group, 128)] = block.astype(
                    band_ref.dtype
                )


def shifted(values):
    rows = values.shape[0]
    return (pltpu.roll(values, 1, 0), values, pltpu.roll(values, rows - 1, 0))


def conv_rows(parts, band_ref, width, count):
    lanes = band_ref.shape[1]
    totals = [None] * (lanes // 256)
    for one in range(3):
        for two in range(3):
            window = parts[two][one * width : one * width + count].astype(jnp.bfloat16)
            for half in range(lanes // 256):
                low = min(max(256 * half - 128, 0), lanes - 384)
                term = jnp.dot(
                    window[:, low : low + 384],
                    band_ref[one * 3 + two, low : low + 384, 256 * half : 256 * half + 256],
                    preferred_element_type=jnp.float32,
                )
                totals[half] = term if totals[half] is None else totals[half] + term
    return jnp.concatenate(totals, axis=1)


def keep_rows(place, grid_shape, own, first, count, width, low, high):
    index = lax.broadcasted_iota(jnp.int32, (count * width, 1), 0)
    whole = jnp.floor((index.astype(jnp.float32) + 0.5) / width).astype(jnp.int32)
    one = whole + first - 2
    two = index - whole * width - 2
    keep = ((one >= 0) | (place[0] > 0)) & ((one < own[0]) | (place[0] < grid_shape[0] - 1))
    keep = keep & ((two >= 0) | (place[1] > 0)) & ((two < own[1]) | (place[1] < grid_shape[1] - 1))
    return keep & (two + 2 >= low) & (two + 2 < high)


def silu(values):
    return 0.5 * values * (1.0 + jnp.tanh(0.5 * values))


def fill_up(weight_ref, table_ref, source_ref=None, copy_sems=None):
    channels = weight_ref.shape[1]
    lane = lax.broadcasted_iota(jnp.int32, (channels, 128), 1)
    spread_out = (lane % channels == lax.broadcasted_iota(jnp.int32, (channels, 128), 0))
    spread_out = spread_out.astype(weight_ref.dtype)
    quarter = lane // channels
    per_group = 128 // channels
    span = 8 * channels

    chunk = 32

    def one(step, carry):
        start = pl.multiple_of(step * chunk * span, chunk * span)
        if source_ref is not None:
            pltpu.make_async_copy(
                source_ref.at[pl.ds(start, chunk * span)], weight_ref.at[pl.ds(start, chunk * span)],
                copy_sems.at[step],
            ).wait()
        tiled = jnp.dot(
            weight_ref[pl.ds(start, chunk * span)], spread_out, preferred_element_type=jnp.float32
        )
        for part in range(chunk):
            table_ref[step * chunk + part, pl.ds(3 * channels, channels), :] = jnp.zeros(
                (channels, 128), table_ref.dtype
            )
            for cell in range(3):
                block = jnp.zeros((channels, 128), jnp.float32)
                for out_cell in range(per_group):
                    depth = 6 - 4 * cell + out_cell
                    if 0 <= depth < 8:
                        row = part * span + depth * channels
                        block = jnp.where(quarter == out_cell, tiled[row : row + channels], block)
                table_ref[step * chunk + part, pl.ds(cell * channels, channels), :] = block.astype(
                    table_ref.dtype
                )
        return carry

    lax.fori_loop(0, table_ref.shape[0] // chunk, one, 0)


DIRECTIONS = [(-1, -1), (-1, 0), (-1, 1), (0, -1), (0, 1), (1, -1), (1, 0), (1, 1)]


def halo_rows(own_ref, staging_ref, size_one, span):
    sub = lax.broadcasted_iota(jnp.int32, (span, own_ref.shape[2]), 0)

    def block_row(one, two, row):
        if (one, two) == (0, 0):
            values = own_ref[row]
        else:
            values = staging_ref[DIRECTIONS.index((one, two)), row]
        values = values.astype(jnp.float32)
        return jnp.concatenate([values, jnp.zeros((span - values.shape[0], values.shape[1]), jnp.float32)], axis=0)

    rows = []
    for ext in range(size_one + 2):
        one = -1 if ext == 0 else (1 if ext == size_one + 1 else 0)
        row = size_one - 1 if ext == 0 else (0 if ext == size_one + 1 else ext - 1)
        left = pltpu.roll(block_row(one, -1, row), 5, 0)
        middle = pltpu.roll(block_row(one, 0, row), 1, 0)
        right = pltpu.roll(block_row(one, 1, row), 5, 0)
        value = jnp.where(sub == 5, right, 0.0)
        value = jnp.where((sub >= 1) & (sub <= 4), middle, value)
        rows.append(jnp.where(sub == 0, left, value))
    return rows


def block_kernel(
    width, rows_out, cols_out, grid_shape,
    own_ref, up_ref, pick_ref, first_ref, second_ref,
    out_ref, band_ref, table_ref, staging_ref, send_sems, recv_sems, up_vmem, up_sems,
):
    pieces = up_sems.shape[0]
    piece = up_vmem.shape[0] // pieces
    for step in range(pieces):
        pltpu.make_async_copy(
            up_ref.at[pl.ds(step * piece, piece)], up_vmem.at[pl.ds(step * piece, piece)], up_sems.at[step]
        ).start()
    place = (lax.axis_index("strike"), lax.axis_index("dip"))
    present = [
        (place[0] + one >= 0) & (place[0] + one < grid_shape[0]) & (place[1] + two >= 0) & (place[1] + two < grid_shape[1])
        for one, two in DIRECTIONS
    ]
    for slot in range(len(DIRECTIONS)):
        @pl.when(jnp.logical_not(present[slot]))
        def _():
            staging_ref[slot] = jnp.zeros(staging_ref.shape[1:], staging_ref.dtype)

    barrier = pltpu.get_barrier_semaphore()
    for slot, (one, two) in enumerate(DIRECTIONS):
        @pl.when(present[slot])
        def _():
            pl.semaphore_signal(
                barrier, 1, device_id=(place[0] + one, place[1] + two),
                device_id_type=pl.DeviceIdType.MESH,
            )
    band_ref[...] = jnp.zeros(band_ref.shape, band_ref.dtype)
    fill_up(up_vmem, table_ref, up_ref, up_sems)
    count = sum(p.astype(jnp.int32) for p in present)
    pl.semaphore_wait(barrier, count)

    copies = []
    for slot, (one, two) in enumerate(DIRECTIONS):
        far = len(DIRECTIONS) - 1 - slot
        copy = pltpu.make_async_remote_copy(
            src_ref=own_ref, dst_ref=staging_ref.at[far], send_sem=send_sems.at[slot],
            recv_sem=recv_sems.at[far], device_id=(place[0] + one, place[1] + two),
            device_id_type=pl.DeviceIdType.MESH,
        )
        pl.when(present[slot])(copy.start)
        copies.append(copy)

    fill_band(first_ref, band_ref)

    for slot, (one, two) in enumerate(DIRECTIONS):
        incoming = pltpu.make_async_remote_copy(
            src_ref=own_ref, dst_ref=staging_ref.at[slot], send_sem=send_sems.at[slot],
            recv_sem=recv_sems.at[slot], device_id=(place[0] + one, place[1] + two),
            device_id_type=pl.DeviceIdType.MESH,
        )

        @pl.when(present[slot])
        def _():
            copies[slot].wait_send()
            incoming.wait_recv()

    size_one = own_ref.shape[0]
    span = 8
    ext = halo_rows(own_ref, staging_ref, size_one, span)
    groups = 4
    channels = table_ref.shape[1] // groups
    lane = lax.broadcasted_iota(jnp.int32, ((size_one + 1) * span, 128), 1)
    windows = []
    for high_one in (0, 1):
        for high_two in (0, 1):
            shifted_rows = [
                ext[m + 1 - high_one] if high_two else pltpu.roll(ext[m + 1 - high_one], span - 1, 0)
                for m in range(size_one + 1)
            ]
            rows = jnp.concatenate(shifted_rows, axis=0)
            parts = []
            for g in range(groups):
                rolled = pltpu.roll(rows, (channels - channels * g) % 128, 1)
                keep = lane < 3 * channels
                if g == 0:
                    keep = keep & (lane >= channels)
                if g == groups - 1:
                    keep = keep & (lane < 2 * channels)
                parts.append(jnp.where(keep, rolled, 0.0))
            windows.append(jnp.concatenate(parts, axis=0).astype(jnp.bfloat16))
    rows_in = (size_one + 1) * span
    phases = []
    for phase_one in range(4):
        for phase_two in range(4):
            total = None
            for high_one in (0, 1):
                for high_two in (0, 1):
                    taps = (4 * high_one + phase_one) * 8 + 4 * high_two + phase_two
                    term = jnp.dot(
                        windows[high_one * 2 + high_two], table_ref[taps],
                        preferred_element_type=jnp.float32,
                    )
                    total = term if total is None else total + term
            phases.append(
                jnp.concatenate([total[g * rows_in : (g + 1) * rows_in] for g in range(groups)], axis=1)
            )
    phase_rows = silu(jnp.concatenate(phases, axis=0)).astype(jnp.bfloat16)
    base = jnp.dot(pick_ref[...], phase_rows, preferred_element_type=jnp.float32)
    own = (rows_out, cols_out)
    base = jnp.where(keep_rows(place, grid_shape, own, 0, rows_out + 4, width, 0, cols_out + 4), base, 0.0)
    hidden_count = (rows_out + 2) * width
    first = conv_rows(shifted(base), band_ref, width, hidden_count)
    hidden_keep = keep_rows(place, grid_shape, own, 1, rows_out + 2, width, 1, cols_out + 3)
    hidden = jnp.where(hidden_keep, silu(first), 0.0)
    fill_band(second_ref, band_ref)
    out_count = rows_out * width
    second = conv_rows(shifted(hidden), band_ref, width, out_count)
    summed = base[2 * width : 2 * width + out_count] + second
    summed = pltpu.roll(summed, out_count - 2, 0).reshape(rows_out, width, summed.shape[1])
    out_ref[...] = summed[:, :cols_out].astype(out_ref.dtype)


def picker(rows, cols, width, span):
    place = np.arange(rows * width)
    one, two = place // width, place % width
    source = ((one % 4) * 4 + two % 4) * (rows // 4) * span + (one // 4) * span + two // 4
    chosen = (np.arange(16 * (rows // 4) * span)[None, :] == source[:, None]) & (two < cols)[:, None]
    return chosen.astype(ml_dtypes.bfloat16)


def body(coarse_field, up_weight, first_weight, second_weight):
    channels = up_weight.shape[3]
    coarse_depth = coarse_field.shape[2] // channels
    size_one, size_two = coarse_field.shape[:2]
    own_rows, own_cols = 4 * size_one, 4 * size_two
    lanes = 4 * coarse_depth * channels
    width, span = 24, 8
    vmem = pl.BlockSpec(memory_space=pltpu.VMEM)
    grid_shape = (lax.axis_size("strike"), lax.axis_size("dip"))
    return pl.pallas_call(
        lambda *refs: block_kernel(width, own_rows, own_cols, grid_shape, *refs),
        out_shape=jax.ShapeDtypeStruct((own_rows, own_cols, lanes), jnp.bfloat16),
        in_specs=[vmem, pl.BlockSpec(memory_space=pl.ANY)] + [vmem] * 3,
        out_specs=vmem,
        scratch_shapes=[
            pltpu.VMEM((9, lanes, lanes), jnp.bfloat16),
            pltpu.VMEM((64, 4 * channels, 128), jnp.bfloat16),
            pltpu.VMEM((len(DIRECTIONS),) + coarse_field.shape, coarse_field.dtype),
            pltpu.SemaphoreType.DMA((len(DIRECTIONS),)),
            pltpu.SemaphoreType.DMA((len(DIRECTIONS),)),
            pltpu.VMEM((up_weight.size // channels, channels), up_weight.dtype),
            pltpu.SemaphoreType.DMA((2,)),
        ],
        compiler_params=pltpu.CompilerParams(collective_id=0, has_side_effects=True),
    )(
        coarse_field,
        up_weight.reshape(-1, channels),
        jnp.asarray(picker(own_rows + 4, own_cols + 4, width, span)),
        first_weight.reshape(-1, channels),
        second_weight.reshape(-1, channels),
    )


def solution(mesh):
    return jax.shard_map(
        body,
        mesh=mesh,
        in_specs=(P("strike", "dip", None), P(), P(), P()),
        out_specs=P("strike", "dip", None),
        check_vma=False,
    )
```
